256 devices in a mesh: coil: 8 (over z_hi, y), space: 32 (over x, z_lo, core).
Axes of the slice: x: 4, y: 4, z: 8 (z_hi: 2, z_lo: 4; z = z_hi * 4 + z_lo), core: 2. Of those that a mesh axis runs over, the one named last changes fastest.
Arguments:
- measured: bfloat16 [16, 2, 8, 512, 512], P('coil', None, None, 'space'), may hold values from -6 to 6
- sensitivity: bfloat16 [16, 2, 8, 512, 512], P('coil', None, None, 'space'), may hold values from -1.5 to 1.5
- sample_lines: int32 [8, 128], replicated, may hold values from 0 to 511, as said below
- kspace_first: bfloat16 [64, 2, 3, 3], replicated, may hold values from -1.5 to 1.5
- kspace_second: bfloat16 [2, 64, 3, 3], replicated, may hold values from -0.25 to 0.25
- image_first: bfloat16 [64, 2, 3, 3, 3], replicated, may hold values from -0.875 to 0.875
- image_second: bfloat16 [2, 64, 3, 3, 3], replicated, may hold values from -0.15625 to 0.15625
Outputs:
- kspace_out: bfloat16 [16, 2, 8, 512, 512], P('coil', None, None, 'space')
- image_out: bfloat16 [2, 8, 512, 512], P(None, None, 'space')
The draws below stay inside these ranges and needn't reach their ends.
Inputs may be any that keep to these rules, and one draw needn't show every extreme that they name: `sample_lines`: each slice lists 128 distinct k-space rows, always including row 0 and row 511.
All inputs are finite; a program needn't handle non-finite values.
Results may differ from the reference program's by a relative error of at most 0.01.
Values may be sent and summed in bfloat16 or wider, within the bound.
No kernel may reach another device: no remote copies, remote signals or barrier semaphores. Data moves between devices by JAX's collectives and lax.ppermute only.
A program may use at most 64 MiB of HBM per device.

```python
import math
import jax
import jax.numpy as jnp
from jax import lax

NROW = 512
NCOL = 512
COILS = 16
SLICES = 8
KCH = 64
ICH = 64
CASCADES = 1
LINES = 128


def draw_sample_lines(key, part):
    slice_keys = jax.random.split(key, SLICES)

    def one_slice(slice_key):
        inner = jax.random.permutation(slice_key, NROW - 2).astype(jnp.int32) + 1
        edges = jnp.array([0, NROW - 1], dtype=jnp.int32)
        picked = jnp.concatenate([edges, inner[:LINES - 2]])
        shuffle = jax.random.permutation(jax.random.fold_in(slice_key, 7), LINES)
        return picked[shuffle]
    return jax.vmap(one_slice)(slice_keys).astype(jnp.int32)


def spiked(values, key, source, target, blocks, factor):
    owner, partner = [(jnp.arange(values.shape[dim]) // (values.shape[dim] // blocks)).reshape([-1 if axis == dim else 1 for axis in range(values.ndim)]) for dim in (source, target)]
    chosen = jax.random.permutation(key, blocks)[partner]
    strong = (owner == chosen) | (owner == (partner + blocks // 2) % blocks)
    return jnp.where(strong, factor * values, values)


def shard_levels(key, dims, cuts, least, top_value):
    def one(dim, blocks):
        draws = jax.random.uniform(jax.random.fold_in(jax.random.fold_in(key, 6), dim), (blocks,), jnp.float32, least / len(cuts), top_value / len(cuts))
        return jnp.repeat(jnp.exp(draws), dims[dim] // blocks).reshape((-1,) + (1,) * (len(dims) - dim - 1))

    loudness = one(*cuts[0])
    for cut in cuts[1:]:
        loudness = loudness * one(*cut)
    return loudness


def bell_draw(rng, dims, deviation, bound, pieces=(), kind=jnp.bfloat16):
    factor_of = shard_levels(rng, dims, pieces, -0.22, 0.18) if pieces else 1.0
    entries = jax.random.normal(rng, dims, jnp.float32) * deviation * factor_of
    return jnp.minimum(jnp.maximum(entries, -bound), bound).astype(kind)


def noise_with(own_key, dims, scale, reach, pieces, heavy, kind=jnp.bfloat16):
    values = scale * jax.random.normal(own_key, dims, jnp.float32)
    if pieces:
        values = values * shard_levels(own_key, dims, pieces, -0.22, 0.18)
    return jnp.clip(spiked(values, jax.random.fold_in(own_key, 3), *heavy), -reach, reach).astype(kind)


def setup_inputs(seed: int = 0) -> dict:
    streams_of = jax.random.split(jax.random.key(seed), 8)
    measured = bell_draw(streams_of[0], (COILS, 2, SLICES, NROW, NCOL), 1.0, 6.0, ((0, 8), (3, 32)))
    sensitivity = noise_with(streams_of[1], (COILS, 2, SLICES, NCOL, NROW), (COILS ** -0.5), 1.5, ((0, 8), (3, 32)), (0, 2, 8, 2.0))
    sample_lines = draw_sample_lines(jax.random.fold_in(streams_of[7], 71), 0)
    kspace_first = bell_draw(streams_of[3], (KCH, 2, 3, 3), 18 ** -0.5, 1.5)
    kspace_second = bell_draw(streams_of[4], (2, KCH, 3, 3), (9 * KCH) ** -0.5, 0.25)
    image_first = bell_draw(streams_of[5], (ICH, 2, 3, 3, 3), 54 ** -0.5, 0.875)
    image_second = bell_draw(streams_of[6], (2, ICH, 3, 3, 3), (27 * ICH) ** -0.5, 0.15625)
    return dict(measured=measured, sensitivity=sensitivity, sample_lines=sample_lines, kspace_first=kspace_first, kspace_second=kspace_second, image_first=image_first, image_second=image_second)


def dft_table(length, direction_sign):
    positions = jnp.arange(length, dtype=jnp.int32)
    wrapped = positions[:, None] * positions[None, :] % length
    angles = wrapped.astype(jnp.float32) * (2.0 * math.pi / length)
    factor = 1.0 / math.sqrt(length)
    return jnp.stack([jnp.cos(angles) * factor, direction_sign * jnp.sin(angles) * factor]).astype(jnp.bfloat16)

def transform(operand, dft_matrix, contract_axis, part_axis):
    product = lax.dot_general(operand.astype(jnp.float32), dft_matrix.astype(jnp.float32), (((contract_axis,), (2,)), ((), ())), preferred_element_type=jnp.float32)
    first_part = lax.index_in_dim(product, 0, part_axis, keepdims=False)
    second_part = lax.index_in_dim(product, 1, part_axis, keepdims=False)
    real_part = first_part[..., 0, :] - second_part[..., 1, :]
    imag_part = first_part[..., 1, :] + second_part[..., 0, :]
    return jnp.stack([real_part, imag_part], axis=part_axis)

def offset_list(spatial):
    collected = [()]
    for level_index in range(spatial):
        collected = [earlier + (shift_by,) for earlier in collected for shift_by in range(3)]
    return collected

def window(array_in, offset):
    leading = array_in.ndim - len(offset)
    selector = [slice(None)] * leading
    for position, shift_by in enumerate(offset):
        extent = array_in.shape[leading + position] - 2
        selector.append(slice(shift_by, shift_by + extent))
    return array_in[tuple(selector)]

def patch_product(padded, weight, spatial):
    offsets = offset_list(spatial)
    patches = jnp.stack([window(padded, offset) for offset in offsets], axis=1)
    patches = patches.reshape((patches.shape[0] * patches.shape[1],) + patches.shape[2:])
    flat_weight = weight.reshape(weight.shape[0], -1)
    return lax.dot_general(flat_weight.astype(jnp.float32), patches.astype(jnp.float32), (((1,), (0,)), ((), ())), preferred_element_type=jnp.float32)

def shift_product(padded, weight, spatial):
    offsets = offset_list(spatial)
    outputs = weight.shape[0]
    inputs = weight.shape[1]
    moved = jnp.moveaxis(weight, 1, -1).reshape(outputs * len(offsets), inputs)
    spread = lax.dot_general(moved.astype(jnp.float32), padded.astype(jnp.float32), (((1,), (0,)), ((), ())), preferred_element_type=jnp.float32)
    spread = spread.reshape((outputs, len(offsets)) + padded.shape[1:])
    running = window(spread[:, 0], offsets[0])
    for number in range(1, len(offsets)):
        running = running + window(spread[:, number], offsets[number])
    return running

def conj_product(maps, field, part_axis):
    maps = maps.astype(jnp.float32)
    map_real = lax.index_in_dim(maps, 0, part_axis, keepdims=False)
    map_imag = lax.index_in_dim(maps, 1, part_axis, keepdims=False)
    field_real = lax.index_in_dim(field, 0, part_axis, keepdims=False)
    field_imag = lax.index_in_dim(field, 1, part_axis, keepdims=False)
    real_part = map_real * field_real + map_imag * field_imag
    imag_part = map_real * field_imag - map_imag * field_real
    return jnp.stack([real_part, imag_part], axis=part_axis)

def expand_product(maps, image, part_axis):
    maps = maps.astype(jnp.float32)
    image = image.astype(jnp.float32)
    map_real = lax.index_in_dim(maps, 0, part_axis, keepdims=False)
    map_imag = lax.index_in_dim(maps, 1, part_axis, keepdims=False)
    real_part = map_real * image[0] - map_imag * image[1]
    imag_part = map_real * image[1] + map_imag * image[0]
    return jnp.stack([real_part, imag_part], axis=part_axis)

def kspace_net(coil_kspace, first_weight, second_weight):
    widths = ((0, 0), (0, 0), (1, 1), (1, 1))
    hidden = jax.nn.relu(patch_product(jnp.pad(coil_kspace, widths), first_weight, 2)).astype(jnp.bfloat16)
    update = shift_product(jnp.pad(hidden, widths), second_weight, 2)
    return (coil_kspace.astype(jnp.float32) + update).astype(jnp.bfloat16)

def image_net(image_in, first_weight, second_weight):
    widths = ((0, 0), (1, 1), (1, 1), (1, 1))
    hidden = jax.nn.relu(patch_product(jnp.pad(image_in, widths), first_weight, 3)).astype(jnp.bfloat16)
    update = shift_product(jnp.pad(hidden, widths), second_weight, 3)
    return (image_in.astype(jnp.float32) + update).astype(jnp.bfloat16)

def reference(measured, sensitivity, sample_lines, kspace_first, kspace_second, image_first, image_second):
    all_rows = jnp.arange(NROW, dtype=jnp.int32)
    sampled = jnp.any(sample_lines[:, :, None] == all_rows[None, None, :], axis=1)
    keep_mask = sampled[None, None, :, :, None]
    kspace = jnp.where(keep_mask, measured, jnp.zeros_like(measured))
    inverse_col = dft_table(NCOL, 1.0)
    inverse_row = dft_table(NROW, 1.0)
    forward_row = dft_table(NROW, -1.0)
    forward_col = dft_table(NCOL, -1.0)
    image_out = jnp.zeros((2, SLICES, NCOL, NROW), jnp.bfloat16)
    for cascade in range(CASCADES):

        def add_coil(running, pair):
            coil_kspace, coil_maps = pair
            refined = kspace_net(coil_kspace, kspace_first, kspace_second)
            half_done = transform(refined, inverse_col, 3, 0).astype(jnp.bfloat16)
            coil_image = transform(half_done, inverse_row, 2, 0)
            return (running + conj_product(coil_maps, coil_image, 0), None)
        running, unused = lax.scan(add_coil, jnp.zeros((2, SLICES, NCOL, NROW), jnp.float32), (kspace, sensitivity))
        image_in = running.astype(jnp.bfloat16)
        image_out = image_net(image_in, image_first, image_second)

        def coil_kspace_of(pair):
            coil_measured, coil_maps = pair
            coil_data = expand_product(coil_maps, image_out, 0).astype(jnp.bfloat16)
            midway = transform(coil_data, forward_row, 3, 0).astype(jnp.bfloat16)
            predicted = transform(midway, forward_col, 2, 0)
            return jnp.where(sampled[None, :, :, None], coil_measured, predicted.astype(jnp.bfloat16))
        kspace = lax.map(coil_kspace_of, (measured, sensitivity))
    return (kspace, image_out)
```

```python
import math

import jax
import jax.numpy as jnp
import numpy as np
from jax import lax
from jax.experimental import pallas as pl
from jax.experimental.pallas import tpu as pltpu
from jax.sharding import PartitionSpec as P

N = 512
COILS = 2
SLICES = 8
ROWS = 16
CH = 64
SPACE = 32
COIL = 8
PAIRS = COILS * SLICES
LANES = PAIRS * ROWS
HROWS = ROWS + 2
BF = jnp.bfloat16
F32 = jnp.float32
VMEM = pl.BlockSpec(memory_space=pltpu.VMEM)
SMEM = pl.BlockSpec(memory_space=pltpu.SMEM)
NT = (((1,), (1,)), ((), ()))


def dft_tables():
    position = np.arange(N)
    angles = (position[:, None] * position[None, :] % N).astype(np.float32) * np.float32(
        2.0 * math.pi / N
    )
    factor = np.float32(1.0 / math.sqrt(N))
    return (np.cos(angles) * factor).astype(BF), (np.sin(angles) * factor).astype(BF)


def kspace_bands():
    first = np.zeros((HROWS, 18, 128), np.float32)
    for r in range(HROWS):
        for h in range(2):
            for p in range(3):
                for q in range(3):
                    row = r + p
                    if 2 <= row < 18:
                        column = q * 32 + h * 16 + row - 2
                    else:
                        e = row if row < 2 else row - 16
                        column = 96 + q * 8 + h * 4 + e
                    first[r, h * 9 + p * 3 + q, column] = 1
    second = np.zeros((HROWS // 2, 96, 36), np.float32)
    for pair in range(HROWS // 2):
        for parity in range(2):
            for q in range(3):
                for o in range(2):
                    for r in range(ROWS):
                        p = 2 * pair + parity - r
                        if 0 <= p < 3:
                            second[pair, q * 32 + o * 16 + r, parity * 18 + q * 6 + o * 3 + p] = 1
    return first.astype(BF), second.astype(BF)


def image_bands():
    first = np.zeros((4, 54, 144), np.float32)
    for x in range(4):
        for h in range(2):
            for a in range(3):
                for p in range(3):
                    for q in range(3):
                        first[x, h * 27 + a * 9 + p * 3 + q, a * 48 + q * 16 + (x + p) * 2 + h] = 1
    second = np.zeros((2, 72, 108), np.float32)
    for pair in range(2):
        for parity in range(2):
            for o in range(2):
                for a in range(3):
                    for q in range(3):
                        for e in range(2):
                            p = 2 * pair + parity - e
                            if 0 <= p < 3:
                                second[
                                    pair,
                                    a * 24 + q * 8 + o * 2 + e,
                                    parity * 54 + o * 27 + a * 9 + p * 3 + q,
                                ] = 1
    return first.astype(BF), second.astype(BF)


def dot(a, b):
    return jnp.dot(a, b, preferred_element_type=F32)


def dot_nt(a, b):
    return lax.dot_general(a, b, NT, preferred_element_type=F32)


def before(v):
    lane = lax.broadcasted_iota(jnp.int32, v.shape, 1)
    return jnp.where(lane == 0, 0.0, pltpu.roll(v, 1, 1))


def after(v):
    lane = lax.broadcasted_iota(jnp.int32, v.shape, 1)
    return jnp.where(lane == N - 1, 0.0, pltpu.roll(v, N - 1, 1))


def blocks_swapped(tiles):
    tiles = list(tiles)
    group = lax.broadcasted_iota(jnp.int32, tiles[0].shape, 1) // 16
    for bit in (4, 2, 1):
        upper = (group & bit) != 0
        for i in range(8):
            if i & bit:
                continue
            a, b = tiles[i], tiles[i + bit]
            tiles[i] = jnp.where(upper, pltpu.roll(b, 16 * bit, 1), a)
            tiles[i + bit] = jnp.where(upper, b, pltpu.roll(a, 128 - 16 * bit, 1))
    return tiles


def wide(ref, *where):
    *lead, rows = where
    return jnp.concatenate([ref[(*lead, b, rows, slice(None))] for b in range(4)], axis=1)


def put(ref, value, *where):
    *lead, rows = where
    for b in range(4):
        ref[(*lead, b, rows, slice(None))] = value[:, b * 128 : (b + 1) * 128]


def regroup(received, left):
    for octet in range(SPACE // 8):
        for coil in range(COILS):
            tiles = [
                received[octet * 8 + i, :, :, coil * 128 : (coil + 1) * 128]
                .astype(F32)
                .reshape(32, 128)
                for i in range(8)
            ]
            for s, tile in enumerate(blocks_swapped(tiles)):
                row = coil * 128 + s * 16
                tile = tile.astype(BF)
                for h in range(2):
                    left[h, row : row + 16, octet * 128 : (octet + 1) * 128] = tile[
                        h * 16 : (h + 1) * 16
                    ]


def kspace_kernel(
    edge, measured, halo, keep, first, second, band1, band2, cos, sin, out, w1, w2, x3, hidden, refined
):
    for r in range(HROWS):
        block = dot(first[...], band1[r])
        if r == 0:
            block = block * edge[0]
        if r == HROWS - 1:
            block = block * edge[1]
        w1[r * CH : (r + 1) * CH, :] = block.astype(BF)
    for pair in range(HROWS // 2):
        w2[:, pair * 128 : (pair + 1) * 128] = dot(band2[pair], second[...]).astype(BF)

    def one(i, carry):
        c, s = i // SLICES, i % SLICES
        mask = keep[s] > 0
        own = jnp.concatenate(
            [jnp.where(mask, measured[c, h, s].astype(F32), 0.0) for h in range(2)], axis=0
        )
        rim = halo[i].astype(F32)
        x3[0:32] = before(own).astype(BF)
        x3[32:64] = own.astype(BF)
        x3[64:96] = after(own).astype(BF)
        x3[96:128] = jnp.concatenate(
            [before(rim), rim, after(rim), jnp.zeros_like(rim)], axis=0
        ).astype(BF)
        hidden[...] = jnp.maximum(dot(w1[...], x3[...]).astype(BF), 0)
        spread = dot(w2[...], hidden[...])
        total = own + before(spread[0:32]) + spread[32:64] + after(spread[64:96])
        total = total.astype(BF)
        row = pl.multiple_of(i * 16, 16)
        for h in range(2):
            refined[h, pl.ds(row, 16), :] = total[h * 16 : (h + 1) * 16]
        return carry

    lax.fori_loop(0, PAIRS, one, 0)
    for part in range(2):
        rows = pl.ds(part * 256, 256)
        co, si = cos[rows, :], sin[rows, :]
        real = dot_nt(co, refined[0]) - dot_nt(si, refined[1])
        imag = dot_nt(si, refined[0]) + dot_nt(co, refined[1])
        out[part * 16 : (part + 1) * 16, 0] = real.astype(BF).reshape(16, 16, LANES)
        out[part * 16 : (part + 1) * 16, 1] = imag.astype(BF).reshape(16, 16, LANES)


def combine_kernel(received, sens, cos, sin, out, left, image, partial):
    regroup(received, left)
    for c in range(COILS):
        rows = slice(c * 128, (c + 1) * 128)
        image[0] = dot(left[0, rows], cos[...]) - dot(left[1, rows], sin[...])
        image[1] = dot(left[0, rows], sin[...]) + dot(left[1, rows], cos[...])
        for s in range(SLICES):
            rows = slice(s * 16, (s + 1) * 16)
            real, imag = image[0, rows], image[1, rows]
            sr, si = sens[c, 0, s].astype(F32), sens[c, 1, s].astype(F32)
            pr = sr * real + si * imag
            pi = sr * imag - si * real
            if c:
                pr = pr + wide(partial, 0, rows)
                pi = pi + wide(partial, 1, rows)
            put(partial, pr, 0, rows)
            put(partial, pi, 1, rows)
    for g in range(COIL):
        for e in range(2):
            both = jnp.concatenate(
                [wide(partial, h, pl.ds(2 * g + e, 8, stride=16)) for h in range(2)], axis=0
            )
            out[g, e * 16 : (e + 1) * 16] = both.astype(BF)


def image_kernel(
    edge, previous, own, following, first, second, band1, band2, out, w1, w2, rows6, x3, acc, fin
):
    for x in range(4):
        block = dot(first[...], band1[x])
        if x == 0:
            block = block * edge[0]
        if x == 3:
            block = block * edge[1]
        w1[x * CH : (x + 1) * CH, :] = block.astype(BF)
    for pair in range(2):
        w2[:, pair * 128 : (pair + 1) * 128] = dot(band2[pair], second[...]).astype(BF)
    for n, source in enumerate((previous, own, following)):
        put(rows6, source[...].astype(F32), slice(n * 32, (n + 1) * 32))
    put(rows6, jnp.zeros((32, N), F32), slice(96, 128))
    x3[0:48] = jnp.zeros((48, N), BF)
    x3[432:480] = jnp.zeros((48, N), BF)
    for s in range(SLICES):
        v = wide(rows6, pl.ds(s, 16, stride=8))
        base = (s + 1) * 48
        x3[base : base + 16] = before(v).astype(BF)
        x3[base + 16 : base + 32] = v.astype(BF)
        x3[base + 32 : base + 48] = after(v).astype(BF)
    acc[...] = jnp.zeros_like(acc)
    for t in range(SLICES):
        hidden = jnp.maximum(dot(w1[...], x3[t * 48 : t * 48 + 144]).astype(BF), 0)
        spread = dot(w2[...], hidden)
        for a in range(3):
            s = t + 1 - a
            if 0 <= s < SLICES:
                acc[s * 24 : (s + 1) * 24] = acc[s * 24 : (s + 1) * 24] + spread[a * 24 : (a + 1) * 24]
    for s in range(SLICES):
        v = acc[s * 24 : (s + 1) * 24]
        put(fin, before(v[0:8]) + v[8:16] + after(v[16:24]), slice(s * 8, (s + 1) * 8))
    for e in range(2):
        update = jnp.concatenate([wide(fin, pl.ds(o * 2 + e, 8, stride=8)) for o in range(2)], axis=0)
        rows = slice(32 + e * 16, 48 + e * 16)
        value = (wide(rows6, rows) + update).astype(BF)
        for g in range(COIL):
            out[g, e * 16 : (e + 1) * 16] = value


def expand_kernel(gathered, sens, cos, sin, out, image_out, image, data):
    for g in range(COIL):
        for e in range(2):
            both = gathered[g, e * 16 : (e + 1) * 16].astype(F32)
            for h in range(2):
                put(image, both[h * 8 : (h + 1) * 8], h, pl.ds(2 * g + e, 8, stride=16))
    for s in range(SLICES):
        rows = slice(s * 16, (s + 1) * 16)
        real, imag = wide(image, 0, rows), wide(image, 1, rows)
        image_out[0, s] = real.astype(BF)
        image_out[1, s] = imag.astype(BF)
        for c in range(COILS):
            sr, si = sens[c, 0, s].astype(F32), sens[c, 1, s].astype(F32)
            rows = slice(c * 128 + s * 16, c * 128 + (s + 1) * 16)
            data[0, rows] = (sr * real - si * imag).astype(BF)
            data[1, rows] = (sr * imag + si * real).astype(BF)
    for part in range(2):
        rows = pl.ds(part * 256, 256)
        co, si = cos[rows, :], sin[rows, :]
        real = dot_nt(co, data[0]) + dot_nt(si, data[1])
        imag = dot_nt(co, data[1]) - dot_nt(si, data[0])
        out[part * 16 : (part + 1) * 16, 0] = real.astype(BF).reshape(16, 16, LANES)
        out[part * 16 : (part + 1) * 16, 1] = imag.astype(BF).reshape(16, 16, LANES)


def finish_kernel(received, measured, keep, cos, sin, out, left):
    regroup(received, left)
    for c in range(COILS):
        rows = slice(c * 128, (c + 1) * 128)
        real = dot(left[0, rows], cos[...]) + dot(left[1, rows], sin[...])
        imag = dot(left[1, rows], cos[...]) - dot(left[0, rows], sin[...])
        for s in range(SLICES):
            mask = keep[s] > 0
            rows = slice(s * 16, (s + 1) * 16)
            for h, value in enumerate((real, imag)):
                out[c, h, s] = jnp.where(
                    mask, measured[c, h, s].astype(F32), value[rows]
                ).astype(BF)


def call(kernel, shapes, scratch, scalars, *operands):
    single = not isinstance(shapes, list)
    return pl.pallas_call(
        kernel,
        out_shape=shapes,
        in_specs=[SMEM] * scalars + [VMEM] * (len(operands) - scalars),
        out_specs=VMEM if single else [VMEM] * len(shapes),
        scratch_shapes=scratch,
        compiler_params=pltpu.CompilerParams(vmem_limit_bytes=40 * 1024 * 1024),
    )(*operands)


def spread(array, axis):
    return lax.all_to_all(array, axis, split_axis=0, concat_axis=0, tiled=True)


def arr(*shape, dtype=BF):
    return jax.ShapeDtypeStruct(shape, dtype)


def local(
    measured, sensitivity, sample_lines, kspace_first, kspace_second, image_first, image_second
):
    space, coil = lax.axis_index("space"), lax.axis_index("coil")
    cos, sin = (jnp.asarray(t) for t in dft_tables())
    kband1, kband2 = (jnp.asarray(t) for t in kspace_bands())
    iband1, iband2 = (jnp.asarray(t) for t in image_bands())

    rows = space * ROWS + jnp.arange(ROWS, dtype=jnp.int32)
    sampled = jnp.any(sample_lines[:, :, None] == rows[None, None, :], axis=1)
    keep = sampled.astype(F32)[:, :, None]

    def rim(start):
        part = jnp.where(
            sampled[None, None, :, start : start + 2, None],
            measured[:, :, :, start : start + 2, :],
            jnp.zeros((), BF),
        )
        return part.transpose(0, 2, 1, 3, 4)

    up = [(i, i + 1) for i in range(SPACE - 1)]
    down = [(i + 1, i) for i in range(SPACE - 1)]
    low = lax.ppermute(rim(ROWS - 2), "space", up)
    high = lax.ppermute(rim(0), "space", down)
    halo = jnp.concatenate([low, high], axis=3).reshape(PAIRS, 8, N)

    def ends(first, last):
        return jnp.stack([1 - first.astype(F32), 1 - last.astype(F32)])

    kedge = ends(space == 0, space == SPACE - 1)
    kfirst = kspace_first.reshape(CH, 18)
    ksecond = kspace_second.transpose(3, 0, 2, 1).reshape(18, CH)
    zero = jnp.zeros_like(ksecond)
    ksecond = jnp.block([[ksecond, zero], [zero, ksecond]])
    ifirst = image_first.reshape(CH, 54)
    isecond = image_second.transpose(0, 2, 3, 4, 1).reshape(54, CH)
    zero = jnp.zeros_like(isecond)
    isecond = jnp.block([[isecond, zero], [zero, isecond]])

    half_done = call(
        kspace_kernel,
        arr(SPACE, 2, ROWS, LANES),
        [
            pltpu.VMEM((HROWS * CH, 128), BF),
            pltpu.VMEM((96, HROWS * CH), BF),
            pltpu.VMEM((128, N), BF),
            pltpu.VMEM((HROWS * CH, N), BF),
            pltpu.VMEM((2, LANES, N), BF),
        ],
        1,
        kedge, measured, halo, keep, kfirst, ksecond, kband1, kband2, cos, sin,
    )
    half_done = spread(half_done, "space")
    partial = call(
        combine_kernel,
        arr(COIL, 32, N),
        [
            pltpu.VMEM((2, LANES, N), BF),
            pltpu.VMEM((2, 128, N), F32),
            pltpu.VMEM((2, 4, 128, 128), F32),
        ],
        0,
        half_done, sensitivity, cos, sin,
    )
    image_in = spread(partial, "coil").astype(F32).sum(axis=0).astype(BF)

    def place(i):
        return (i % COIL) * SPACE + i // COIL

    count = COIL * SPACE
    forward = [(place(i), place(i + 1)) for i in range(count - 1)]
    previous = lax.ppermute(image_in, ("coil", "space"), forward)
    following = lax.ppermute(image_in, ("coil", "space"), [(b, a) for a, b in forward])
    iedge = ends(
        (space == 0) & (coil == 0), (space == SPACE - 1) & (coil == COIL - 1)
    )
    copies = call(
        image_kernel,
        arr(COIL, 32, N),
        [
            pltpu.VMEM((4 * CH, 144), BF),
            pltpu.VMEM((72, 4 * CH), BF),
            pltpu.VMEM((4, 128, 128), F32),
            pltpu.VMEM((480, N), BF),
            pltpu.VMEM((SLICES * 24, N), F32),
            pltpu.VMEM((4, SLICES * 8, 128), F32),
        ],
        1,
        iedge, previous, image_in, following, ifirst, isecond, iband1, iband2,
    )
    gathered = spread(copies, "coil")
    midway, image_out = call(
        expand_kernel,
        [arr(SPACE, 2, ROWS, LANES), arr(2, SLICES, ROWS, N)],
        [pltpu.VMEM((2, 4, 128, 128), F32), pltpu.VMEM((2, LANES, N), BF)],
        0,
        gathered, sensitivity, cos, sin,
    )
    midway = spread(midway, "space")
    kspace_out = call(
        finish_kernel,
        arr(COILS, 2, SLICES, ROWS, N),
        [pltpu.VMEM((2, LANES, N), BF)],
        0,
        midway, measured, keep, cos, sin,
    )
    return kspace_out, image_out


def solution(mesh):
    placed = P("coil", None, None, "space", None)
    return jax.shard_map(
        local,
        mesh=mesh,
        in_specs=(placed, placed, P(), P(), P(), P(), P()),
        out_specs=(placed, P(None, None, "space", None)),
        check_vma=False,
    )
```

```python
import math

import jax
import jax.numpy as jnp
import numpy as np
from jax import lax
from jax.experimental import pallas as pl
from jax.experimental.pallas import tpu as pltpu
from jax.sharding import Mesh
from jax.sharding import PartitionSpec as P

N = 512
COILS = 2
SLICES = 8
ROWS = 16
CH = 64
SPACE = 32
RING = 4
HALVES = 2
PAIRS = COILS * SLICES
LANES = PAIRS * ROWS
HROWS = ROWS + 2
BF = jnp.bfloat16
F32 = jnp.float32
VMEM = pl.BlockSpec(memory_space=pltpu.VMEM)
SMEM = pl.BlockSpec(memory_space=pltpu.SMEM)
NT = (((1,), (1,)), ((), ()))


def dft_tables():
    position = np.arange(N)
    angles = (position[:, None] * position[None, :] % N).astype(np.float32) * np.float32(
        2.0 * math.pi / N
    )
    factor = np.float32(1.0 / math.sqrt(N))
    return (np.cos(angles) * factor).astype(BF), (np.sin(angles) * factor).astype(BF)


def kspace_bands():
    first = np.zeros((HROWS, 18, 128), np.float32)
    for r in range(HROWS):
        for h in range(2):
            for p in range(3):
                for q in range(3):
                    row = r + p
                    if 2 <= row < 18:
                        column = q * 32 + h * 16 + row - 2
                    else:
                        e = row if row < 2 else row - 16
                        column = 96 + q * 8 + h * 4 + e
                    first[r, h * 9 + p * 3 + q, column] = 1
    second = np.zeros((HROWS // 2, 96, 36), np.float32)
    for pair in range(HROWS // 2):
        for parity in range(2):
            for q in range(3):
                for o in range(2):
                    for r in range(ROWS):
                        p = 2 * pair + parity - r
                        if 0 <= p < 3:
                            second[pair, q * 32 + o * 16 + r, parity * 18 + q * 6 + o * 3 + p] = 1
    return first.astype(BF), second.astype(BF)


def image_bands():
    first = np.zeros((6, 54, 144), np.float32)
    for x in range(6):
        for h in range(2):
            for a in range(3):
                for p in range(3):
                    for q in range(3):
                        first[x, h * 27 + a * 9 + p * 3 + q, a * 48 + q * 16 + (x + p) * 2 + h] = 1
    second = np.zeros((3, 72, 108), np.float32)
    for pair in range(3):
        for parity in range(2):
            for o in range(2):
                for a in range(3):
                    for q in range(3):
                        for e in range(4):
                            p = 2 * pair + parity - e
                            if 0 <= p < 3:
                                second[
                                    pair,
                                    a * 24 + q * 8 + o * 4 + e,
                                    parity * 54 + o * 27 + a * 9 + p * 3 + q,
                                ] = 1
    return first.astype(BF), second.astype(BF)


def dot(a, b):
    return jnp.dot(a, b, preferred_element_type=F32)


def dot_nt(a, b):
    return lax.dot_general(a, b, NT, preferred_element_type=F32)


def before(v):
    lane = lax.broadcasted_iota(jnp.int32, v.shape, 1)
    return jnp.where(lane == 0, 0.0, pltpu.roll(v, 1, 1))


def after(v):
    lane = lax.broadcasted_iota(jnp.int32, v.shape, 1)
    return jnp.where(lane == N - 1, 0.0, pltpu.roll(v, N - 1, 1))


def blocks_swapped(tiles):
    tiles = list(tiles)
    group = lax.broadcasted_iota(jnp.int32, tiles[0].shape, 1) // 16
    for bit in (4, 2, 1):
        upper = (group & bit) != 0
        for i in range(8):
            if i & bit:
                continue
            a, b = tiles[i], tiles[i + bit]
            tiles[i] = jnp.where(upper, pltpu.roll(b, 16 * bit, 1), a)
            tiles[i + bit] = jnp.where(upper, b, pltpu.roll(a, 128 - 16 * bit, 1))
    return tiles


def wide(ref, *where):
    *lead, rows = where
    return jnp.concatenate([ref[(*lead, b, rows, slice(None))] for b in range(4)], axis=1)


def put(ref, value, *where):
    *lead, rows = where
    for b in range(4):
        ref[(*lead, b, rows, slice(None))] = value[:, b * 128 : (b + 1) * 128]


def regroup(received, left):
    for octet in range(SPACE // 8):
        for coil in range(COILS):
            tiles = [
                received[octet * 8 + i, :, :, coil * 128 : (coil + 1) * 128]
                .astype(F32)
                .reshape(32, 128)
                for i in range(8)
            ]
            for s, tile in enumerate(blocks_swapped(tiles)):
                row = coil * 128 + s * 16
                tile = tile.astype(BF)
                for h in range(2):
                    left[h, row : row + 16, octet * 128 : (octet + 1) * 128] = tile[
                        h * 16 : (h + 1) * 16
                    ]


def kspace_kernel(
    edge, measured, halo, keep, first, second, band1, band2, cos, sin, out, w1, w2, x3, hidden, refined
):
    for r in range(HROWS):
        block = dot(first[...], band1[r])
        if r == 0:
            block = block * edge[0]
        if r == HROWS - 1:
            block = block * edge[1]
        w1[r * CH : (r + 1) * CH, :] = block.astype(BF)
    for pair in range(HROWS // 2):
        w2[:, pair * 128 : (pair + 1) * 128] = dot(band2[pair], second[...]).astype(BF)

    def one(i, carry):
        c, s = i // SLICES, i % SLICES
        mask = keep[s] > 0
        own = jnp.concatenate(
            [jnp.where(mask, measured[c, h, s].astype(F32), 0.0) for h in range(2)], axis=0
        )
        rim = halo[i].astype(F32)
        x3[0:32] = before(own).astype(BF)
        x3[32:64] = own.astype(BF)
        x3[64:96] = after(own).astype(BF)
        x3[96:128] = jnp.concatenate(
            [before(rim), rim, after(rim), jnp.zeros_like(rim)], axis=0
        ).astype(BF)
        hidden[...] = jnp.maximum(dot(w1[...], x3[...]).astype(BF), 0)
        spread = dot(w2[...], hidden[...])
        total = own + before(spread[0:32]) + spread[32:64] + after(spread[64:96])
        total = total.astype(BF)
        row = pl.multiple_of(i * 16, 16)
        for h in range(2):
            refined[h, pl.ds(row, 16), :] = total[h * 16 : (h + 1) * 16]
        return carry

    lax.fori_loop(0, PAIRS, one, 0)
    for part in range(2):
        rows = pl.ds(part * 256, 256)
        co, si = cos[rows, :], sin[rows, :]
        real = dot_nt(co, refined[0]) - dot_nt(si, refined[1])
        imag = dot_nt(si, refined[0]) + dot_nt(co, refined[1])
        out[part * 16 : (part + 1) * 16, 0] = real.astype(BF).reshape(16, 16, LANES)
        out[part * 16 : (part + 1) * 16, 1] = imag.astype(BF).reshape(16, 16, LANES)


def combine_kernel(received, sens, cos, sin, out, left, image, partial):
    regroup(received, left)
    for c in range(COILS):
        rows = slice(c * 128, (c + 1) * 128)
        image[0] = dot(left[0, rows], cos[...]) - dot(left[1, rows], sin[...])
        image[1] = dot(left[0, rows], sin[...]) + dot(left[1, rows], cos[...])
        for s in range(SLICES):
            rows = slice(s * 16, (s + 1) * 16)
            real, imag = image[0, rows], image[1, rows]
            sr, si = sens[c, 0, s].astype(F32), sens[c, 1, s].astype(F32)
            pr = sr * real + si * imag
            pi = sr * imag - si * real
            if c:
                pr = pr + wide(partial, 0, rows)
                pi = pi + wide(partial, 1, rows)
            put(partial, pr, 0, rows)
            put(partial, pi, 1, rows)
    for x in range(ROWS):
        both = jnp.concatenate(
            [wide(partial, h, pl.ds(x, 8, stride=16)) for h in range(2)], axis=0
        )
        out[x // 4, x % 4 * 16 : (x % 4 + 1) * 16] = both.astype(BF)


def image_kernel(
    edge, own, other, before1, before2, after1, after2, first, second, band1, band2, out,
    w1, w2, rows8, x3, acc, fin
):
    for x in range(6):
        block = dot(first[...], band1[x])
        if x == 0:
            block = block * edge[0]
        if x == 5:
            block = block * edge[1]
        w1[x * CH : (x + 1) * CH, :] = block.astype(BF)
    for pair in range(3):
        w2[:, pair * 128 : (pair + 1) * 128] = dot(band2[pair], second[...]).astype(BF)
    for start, stop, a, b in ((0, 32, before1, before2), (32, 96, own, other), (96, 128, after1, after2)):
        total = (a[...].astype(F32) + b[...].astype(F32)).astype(BF)
        put(rows8, total.astype(F32), slice(start, stop))
    x3[0:48] = jnp.zeros((48, N), BF)
    x3[432:480] = jnp.zeros((48, N), BF)
    for s in range(SLICES):
        v = wide(rows8, pl.ds(s, 16, stride=8))
        base = (s + 1) * 48
        x3[base : base + 16] = before(v).astype(BF)
        x3[base + 16 : base + 32] = v.astype(BF)
        x3[base + 32 : base + 48] = after(v).astype(BF)
    acc[...] = jnp.zeros_like(acc)
    for t in range(SLICES):
        hidden = jnp.maximum(dot(w1[...], x3[t * 48 : t * 48 + 144]).astype(BF), 0)
        spread = dot(w2[...], hidden)
        for a in range(3):
            s = t + 1 - a
            if 0 <= s < SLICES:
                acc[s * 24 : (s + 1) * 24] = acc[s * 24 : (s + 1) * 24] + spread[a * 24 : (a + 1) * 24]
    for s in range(SLICES):
        v = acc[s * 24 : (s + 1) * 24]
        put(fin, before(v[0:8]) + v[8:16] + after(v[16:24]), slice(s * 8, (s + 1) * 8))
    for e in range(4):
        update = jnp.concatenate([wide(fin, pl.ds(o * 4 + e, 8, stride=8)) for o in range(2)], axis=0)
        value = (wide(rows8, slice(32 + e * 16, 48 + e * 16)) + update).astype(BF)
        for y in range(RING):
            out[y, e * 16 : (e + 1) * 16] = value


def expand_kernel(gathered, sens, cos, sin, out, image_out, image, data):
    for x in range(ROWS):
        both = gathered[x // 4, x % 4 * 16 : (x % 4 + 1) * 16].astype(F32)
        for h in range(2):
            put(image, both[h * 8 : (h + 1) * 8], h, pl.ds(x, 8, stride=16))
    for s in range(SLICES):
        rows = slice(s * 16, (s + 1) * 16)
        real, imag = wide(image, 0, rows), wide(image, 1, rows)
        image_out[0, s] = real.astype(BF)
        image_out[1, s] = imag.astype(BF)
        for c in range(COILS):
            sr, si = sens[c, 0, s].astype(F32), sens[c, 1, s].astype(F32)
            rows = slice(c * 128 + s * 16, c * 128 + (s + 1) * 16)
            data[0, rows] = (sr * real - si * imag).astype(BF)
            data[1, rows] = (sr * imag + si * real).astype(BF)
    for part in range(2):
        rows = pl.ds(part * 256, 256)
        co, si = cos[rows, :], sin[rows, :]
        real = dot_nt(co, data[0]) + dot_nt(si, data[1])
        imag = dot_nt(co, data[1]) - dot_nt(si, data[0])
        out[part * 16 : (part + 1) * 16, 0] = real.astype(BF).reshape(16, 16, LANES)
        out[part * 16 : (part + 1) * 16, 1] = imag.astype(BF).reshape(16, 16, LANES)


def finish_kernel(received, measured, keep, cos, sin, out, left):
    regroup(received, left)
    for c in range(COILS):
        rows = slice(c * 128, (c + 1) * 128)
        real = dot(left[0, rows], cos[...]) + dot(left[1, rows], sin[...])
        imag = dot(left[1, rows], cos[...]) - dot(left[0, rows], sin[...])
        for s in range(SLICES):
            mask = keep[s] > 0
            rows = slice(s * 16, (s + 1) * 16)
            for h, value in enumerate((real, imag)):
                out[c, h, s] = jnp.where(
                    mask, measured[c, h, s].astype(F32), value[rows]
                ).astype(BF)


def call(kernel, shapes, scratch, scalars, *operands):
    single = not isinstance(shapes, list)
    return pl.pallas_call(
        kernel,
        out_shape=shapes,
        in_specs=[SMEM] * scalars + [VMEM] * (len(operands) - scalars),
        out_specs=VMEM if single else [VMEM] * len(shapes),
        scratch_shapes=scratch,
        compiler_params=pltpu.CompilerParams(vmem_limit_bytes=40 * 1024 * 1024),
    )(*operands)


def spread(array, axis):
    return lax.all_to_all(array, axis, split_axis=0, concat_axis=0, tiled=True)


def arr(*shape, dtype=BF):
    return jax.ShapeDtypeStruct(shape, dtype)


def local(
    measured, sensitivity, sample_lines, kspace_first, kspace_second, image_first, image_second
):
    space, ring = lax.axis_index("space"), lax.axis_index("ring")
    cos, sin = (jnp.asarray(t) for t in dft_tables())
    kband1, kband2 = (jnp.asarray(t) for t in kspace_bands())
    iband1, iband2 = (jnp.asarray(t) for t in image_bands())

    rows = space * ROWS + jnp.arange(ROWS, dtype=jnp.int32)
    sampled = jnp.any(sample_lines[:, :, None] == rows[None, None, :], axis=1)
    keep = sampled.astype(F32)[:, :, None]

    def rim(start):
        part = jnp.where(
            sampled[None, None, :, start : start + 2, None],
            measured[:, :, :, start : start + 2, :],
            jnp.zeros((), BF),
        )
        return part.transpose(0, 2, 1, 3, 4)

    up = [(i, i + 1) for i in range(SPACE - 1)]
    down = [(i + 1, i) for i in range(SPACE - 1)]
    low = lax.ppermute(rim(ROWS - 2), "space", up)
    high = lax.ppermute(rim(0), "space", down)
    halo = jnp.concatenate([low, high], axis=3).reshape(PAIRS, 8, N)

    def ends(first, last):
        return jnp.stack([1 - first.astype(F32), 1 - last.astype(F32)])

    kedge = ends(space == 0, space == SPACE - 1)
    kfirst = kspace_first.reshape(CH, 18)
    ksecond = kspace_second.transpose(3, 0, 2, 1).reshape(18, CH)
    zero = jnp.zeros_like(ksecond)
    ksecond = jnp.block([[ksecond, zero], [zero, ksecond]])
    ifirst = image_first.reshape(CH, 54)
    isecond = image_second.transpose(0, 2, 3, 4, 1).reshape(54, CH)
    zero = jnp.zeros_like(isecond)
    isecond = jnp.block([[isecond, zero], [zero, isecond]])

    half_done = call(
        kspace_kernel,
        arr(SPACE, 2, ROWS, LANES),
        [
            pltpu.VMEM((HROWS * CH, 128), BF),
            pltpu.VMEM((96, HROWS * CH), BF),
            pltpu.VMEM((128, N), BF),
            pltpu.VMEM((HROWS * CH, N), BF),
            pltpu.VMEM((2, LANES, N), BF),
        ],
        1,
        kedge, measured, halo, keep, kfirst, ksecond, kband1, kband2, cos, sin,
    )
    half_done = spread(half_done, "space")
    partial = call(
        combine_kernel,
        arr(RING, 64, N),
        [
            pltpu.VMEM((2, LANES, N), BF),
            pltpu.VMEM((2, 128, N), F32),
            pltpu.VMEM((2, 4, 128, 128), F32),
        ],
        0,
        half_done, sensitivity, cos, sin,
    )
    part = spread(partial, "ring").astype(F32).sum(axis=0).astype(BF)

    def place(half, i):
        return (half * RING + i % RING) * SPACE + i // RING

    count = RING * SPACE
    axes = ("half", "ring", "space")

    def moved(array, step, flip):
        pairs = [
            (place(half, i), place(half ^ flip, i + step))
            for half in range(HALVES)
            for i in range(count)
            if 0 <= i + step < count
        ]
        return lax.ppermute(array, axes, pairs)

    low, high = part[:32], part[32:]
    before2 = moved(high, 1, 1)
    after2 = moved(low, -1, 1)
    other = moved(part, 0, 1)
    before1 = moved(high, 1, 0)
    after1 = moved(low, -1, 0)
    iedge = ends((space == 0) & (ring == 0), (space == SPACE - 1) & (ring == RING - 1))
    copies = call(
        image_kernel,
        arr(RING, 64, N),
        [
            pltpu.VMEM((6 * CH, 144), BF),
            pltpu.VMEM((72, 6 * CH), BF),
            pltpu.VMEM((4, 128, 128), F32),
            pltpu.VMEM((480, N), BF),
            pltpu.VMEM((SLICES * 24, N), F32),
            pltpu.VMEM((4, SLICES * 8, 128), F32),
        ],
        1,
        iedge, part, other, before1, before2, after1, after2, ifirst, isecond, iband1, iband2,
    )
    gathered = spread(copies, "ring")
    midway, image_out = call(
        expand_kernel,
        [arr(SPACE, 2, ROWS, LANES), arr(2, SLICES, ROWS, N)],
        [pltpu.VMEM((2, 4, 128, 128), F32), pltpu.VMEM((2, LANES, N), BF)],
        0,
        gathered, sensitivity, cos, sin,
    )
    midway = spread(midway, "space")
    kspace_out = call(
        finish_kernel,
        arr(COILS, 2, SLICES, ROWS, N),
        [pltpu.VMEM((2, LANES, N), BF)],
        0,
        midway, measured, keep, cos, sin,
    )
    return kspace_out, image_out


def solution(mesh):
    mesh = Mesh(mesh.devices.reshape(HALVES, RING, SPACE), ("half", "ring", "space"))
    placed = P(("half", "ring"), None, None, "space", None)
    return jax.shard_map(
        local,
        mesh=mesh,
        in_specs=(placed, placed, P(), P(), P(), P(), P()),
        out_specs=(placed, P(None, None, "space", None)),
        check_vma=False,
    )
```

```python
import math

import jax
import jax.numpy as jnp
import numpy as np
from jax import lax
from jax.experimental import pallas as pl
from jax.experimental.pallas import tpu as pltpu
from jax.sharding import Mesh
from jax.sharding import PartitionSpec as P

N = 512
COILS = 2
SLICES = 8
ROWS = 16
CH = 64
SPACE = 32
RING = 4
HALVES = 2
PAIRS = COILS * SLICES
LANES = PAIRS * ROWS
HROWS = ROWS + 2
UNROLL = 2
BF = jnp.bfloat16
F32 = jnp.float32
VMEM = pl.BlockSpec(memory_space=pltpu.VMEM)
SMEM = pl.BlockSpec(memory_space=pltpu.SMEM)
NT = (((1,), (1,)), ((), ()))


def dft_tables():
    position = np.arange(N)
    angles = (position[:, None] * position[None, :] % N).astype(np.float32) * np.float32(
        2.0 * math.pi / N
    )
    factor = np.float32(1.0 / math.sqrt(N))
    return (np.cos(angles) * factor).astype(BF), (np.sin(angles) * factor).astype(BF)


def kspace_bands():
    first = np.zeros((HROWS, 18, 128), np.float32)
    for r in range(HROWS):
        for h in range(2):
            for p in range(3):
                for q in range(3):
                    row = r + p
                    if 2 <= row < 18:
                        column = q * 32 + h * 16 + row - 2
                    else:
                        e = row if row < 2 else row - 16
                        column = 96 + q * 8 + h * 4 + e
                    first[r, h * 9 + p * 3 + q, column] = 1
    second = np.zeros((HROWS // 2, 96, 36), np.float32)
    for pair in range(HROWS // 2):
        for parity in range(2):
            for q in range(3):
                for o in range(2):
                    for r in range(ROWS):
                        p = 2 * pair + parity - r
                        if 0 <= p < 3:
                            second[pair, q * 32 + o * 16 + r, parity * 18 + q * 6 + o * 3 + p] = 1
    return first.astype(BF), second.astype(BF)


def image_bands():
    first = np.zeros((6, 54, 144), np.float32)
    for x in range(6):
        for h in range(2):
            for a in range(3):
                for p in range(3):
                    for q in range(3):
                        first[x, h * 27 + a * 9 + p * 3 + q, a * 48 + q * 16 + (x + p) * 2 + h] = 1
    second = np.zeros((3, 72, 108), np.float32)
    for pair in range(3):
        for parity in range(2):
            for o in range(2):
                for a in range(3):
                    for q in range(3):
                        for e in range(4):
                            p = 2 * pair + parity - e
                            if 0 <= p < 3:
                                second[
                                    pair,
                                    a * 24 + q * 8 + o * 4 + e,
                                    parity * 54 + o * 27 + a * 9 + p * 3 + q,
                                ] = 1
    return first.astype(BF), second.astype(BF)


def dot(a, b):
    return jnp.dot(a, b, preferred_element_type=F32)


def dot_nt(a, b):
    return lax.dot_general(a, b, NT, preferred_element_type=F32)


def before(v):
    lane = lax.broadcasted_iota(jnp.int32, v.shape, 1)
    return jnp.where(lane == 0, 0.0, pltpu.roll(v, 1, 1))


def after(v):
    lane = lax.broadcasted_iota(jnp.int32, v.shape, 1)
    return jnp.where(lane == N - 1, 0.0, pltpu.roll(v, N - 1, 1))


def blocks_swapped(tiles):
    tiles = list(tiles)
    group = lax.broadcasted_iota(jnp.int32, tiles[0].shape, 1) // 16
    for bit in (4, 2, 1):
        upper = (group & bit) != 0
        for i in range(8):
            if i & bit:
                continue
            a, b = tiles[i], tiles[i + bit]
            tiles[i] = jnp.where(upper, pltpu.roll(b, 16 * bit, 1), a)
            tiles[i + bit] = jnp.where(upper, b, pltpu.roll(a, 128 - 16 * bit, 1))
    return tiles


def wide(ref, *where):
    *lead, rows = where
    return jnp.concatenate([ref[(*lead, b, rows, slice(None))] for b in range(4)], axis=1)


def put(ref, value, *where):
    *lead, rows = where
    for b in range(4):
        ref[(*lead, b, rows, slice(None))] = value[:, b * 128 : (b + 1) * 128]


def regroup(received, left):
    for octet in range(SPACE // 8):
        for coil in range(COILS):
            tiles = [
                received[octet * 8 + i, :, :, coil * 128 : (coil + 1) * 128]
                .astype(F32)
                .reshape(32, 128)
                for i in range(8)
            ]
            for s, tile in enumerate(blocks_swapped(tiles)):
                row = coil * 128 + s * 16
                tile = tile.astype(BF)
                for h in range(2):
                    left[h, row : row + 16, octet * 128 : (octet + 1) * 128] = tile[
                        h * 16 : (h + 1) * 16
                    ]


def kspace_weights_kernel(edge, first, second, band1, band2, w1, w2):
    for r in range(HROWS):
        block = dot(first[...], band1[r])
        if r == 0:
            block = block * edge[0]
        if r == HROWS - 1:
            block = block * edge[1]
        w1[r * CH : (r + 1) * CH, :] = block.astype(BF)
    for pair in range(HROWS // 2):
        w2[:, pair * 128 : (pair + 1) * 128] = dot(band2[pair], second[...]).astype(BF)


def kspace_kernel(measured, halo, keep, w1, w2, cos, sin, out, refined, *scratch):
    def one(i, x3, hidden):
        c, s = i // SLICES, i % SLICES
        mask = keep[s] > 0
        own = jnp.concatenate(
            [jnp.where(mask, measured[c, h, s].astype(F32), 0.0) for h in range(2)], axis=0
        )
        rim = halo[i].astype(F32)
        x3[0:32] = before(own).astype(BF)
        x3[32:64] = own.astype(BF)
        x3[64:96] = after(own).astype(BF)
        x3[96:128] = jnp.concatenate(
            [before(rim), rim, after(rim), jnp.zeros_like(rim)], axis=0
        ).astype(BF)
        hidden[...] = jnp.maximum(dot(w1[...], x3[...]).astype(BF), 0)
        spread = dot(w2[...], hidden[...])
        total = own + before(spread[0:32]) + spread[32:64] + after(spread[64:96])
        total = total.astype(BF)
        row = pl.multiple_of(i * 16, 16)
        for h in range(2):
            refined[h, pl.ds(row, 16), :] = total[h * 16 : (h + 1) * 16]

    def step(i, carry):
        for k in range(UNROLL):
            one(i * UNROLL + k, scratch[2 * k], scratch[2 * k + 1])
        return carry

    lax.fori_loop(0, PAIRS // UNROLL, step, 0)
    for part in range(2):
        rows = pl.ds(part * 256, 256)
        co, si = cos[rows, :], sin[rows, :]
        real = dot_nt(co, refined[0]) - dot_nt(si, refined[1])
        imag = dot_nt(si, refined[0]) + dot_nt(co, refined[1])
        out[part * 16 : (part + 1) * 16, 0] = real.astype(BF).reshape(16, 16, LANES)
        out[part * 16 : (part + 1) * 16, 1] = imag.astype(BF).reshape(16, 16, LANES)


def combine_kernel(received, sens, cos, sin, out, left, image, partial):
    regroup(received, left)
    for c in range(COILS):
        rows = slice(c * 128, (c + 1) * 128)
        image[0] = dot(left[0, rows], cos[...]) - dot(left[1, rows], sin[...])
        image[1] = dot(left[0, rows], sin[...]) + dot(left[1, rows], cos[...])
        for s in range(SLICES):
            rows = slice(s * 16, (s + 1) * 16)
            real, imag = image[0, rows], image[1, rows]
            sr, si = sens[c, 0, s].astype(F32), sens[c, 1, s].astype(F32)
            pr = sr * real + si * imag
            pi = sr * imag - si * real
            if c:
                pr = pr + wide(partial, 0, rows)
                pi = pi + wide(partial, 1, rows)
            put(partial, pr, 0, rows)
            put(partial, pi, 1, rows)
    for x in range(ROWS):
        both = jnp.concatenate(
            [wide(partial, h, pl.ds(x, 8, stride=16)) for h in range(2)], axis=0
        )
        out[x // 4, x % 4 * 16 : (x % 4 + 1) * 16] = both.astype(BF)


def image_kernel(
    edge, previous, own, following, first, second, band1, band2, out,
    w1, w2, rows8, x3, acc, fin
):
    for x in range(6):
        block = dot(first[...], band1[x])
        if x == 0:
            block = block * edge[0]
        if x == 5:
            block = block * edge[1]
        w1[x * CH : (x + 1) * CH, :] = block.astype(BF)
    for pair in range(3):
        w2[:, pair * 128 : (pair + 1) * 128] = dot(band2[pair], second[...]).astype(BF)
    for start, stop, source in ((0, 32, previous), (32, 96, own), (96, 128, following)):
        put(rows8, source[...].astype(F32), slice(start, stop))
    x3[0:48] = jnp.zeros((48, N), BF)
    x3[432:480] = jnp.zeros((48, N), BF)
    for s in range(SLICES):
        v = wide(rows8, pl.ds(s, 16, stride=8))
        base = (s + 1) * 48
        x3[base : base + 16] = before(v).astype(BF)
        x3[base + 16 : base + 32] = v.astype(BF)
        x3[base + 32 : base + 48] = after(v).astype(BF)
    acc[...] = jnp.zeros_like(acc)
    for t in range(SLICES):
        hidden = jnp.maximum(dot(w1[...], x3[t * 48 : t * 48 + 144]).astype(BF), 0)
        spread = dot(w2[...], hidden)
        for a in range(3):
            s = t + 1 - a
            if 0 <= s < SLICES:
                acc[s * 24 : (s + 1) * 24] = acc[s * 24 : (s + 1) * 24] + spread[a * 24 : (a + 1) * 24]
    for s in range(SLICES):
        v = acc[s * 24 : (s + 1) * 24]
        put(fin, before(v[0:8]) + v[8:16] + after(v[16:24]), slice(s * 8, (s + 1) * 8))
    for e in range(4):
        update = jnp.concatenate([wide(fin, pl.ds(o * 4 + e, 8, stride=8)) for o in range(2)], axis=0)
        value = (wide(rows8, slice(32 + e * 16, 48 + e * 16)) + update).astype(BF)
        for y in range(RING):
            out[y, e * 16 : (e + 1) * 16] = value


def expand_kernel(gathered, sens, cos, sin, out, image_out, image, data):
    for x in range(ROWS):
        both = gathered[x // 4, x % 4 * 16 : (x % 4 + 1) * 16].astype(F32)
        for h in range(2):
            put(image, both[h * 8 : (h + 1) * 8], h, pl.ds(x, 8, stride=16))
    for s in range(SLICES):
        rows = slice(s * 16, (s + 1) * 16)
        real, imag = wide(image, 0, rows), wide(image, 1, rows)
        image_out[0, s] = real.astype(BF)
        image_out[1, s] = imag.astype(BF)
        for c in range(COILS):
            sr, si = sens[c, 0, s].astype(F32), sens[c, 1, s].astype(F32)
            rows = slice(c * 128 + s * 16, c * 128 + (s + 1) * 16)
            data[0, rows] = (sr * real - si * imag).astype(BF)
            data[1, rows] = (sr * imag + si * real).astype(BF)
    for part in range(2):
        rows = pl.ds(part * 256, 256)
        co, si = cos[rows, :], sin[rows, :]
        real = dot_nt(co, data[0]) + dot_nt(si, data[1])
        imag = dot_nt(co, data[1]) - dot_nt(si, data[0])
        out[part * 16 : (part + 1) * 16, 0] = real.astype(BF).reshape(16, 16, LANES)
        out[part * 16 : (part + 1) * 16, 1] = imag.astype(BF).reshape(16, 16, LANES)


def finish_kernel(received, measured, keep, cos, sin, out, left):
    regroup(received, left)
    for c in range(COILS):
        rows = slice(c * 128, (c + 1) * 128)
        real = dot(left[0, rows], cos[...]) + dot(left[1, rows], sin[...])
        imag = dot(left[1, rows], cos[...]) - dot(left[0, rows], sin[...])
        for s in range(SLICES):
            mask = keep[s] > 0
            rows = slice(s * 16, (s + 1) * 16)
            for h, value in enumerate((real, imag)):
                out[c, h, s] = jnp.where(
                    mask, measured[c, h, s].astype(F32), value[rows]
                ).astype(BF)


def call(kernel, shapes, scratch, scalars, *operands):
    single = not isinstance(shapes, list)
    return pl.pallas_call(
        kernel,
        out_shape=shapes,
        in_specs=[SMEM] * scalars + [VMEM] * (len(operands) - scalars),
        out_specs=VMEM if single else [VMEM] * len(shapes),
        scratch_shapes=scratch,
        compiler_params=pltpu.CompilerParams(vmem_limit_bytes=40 * 1024 * 1024),
    )(*operands)


def spread(array, axis):
    return lax.all_to_all(array, axis, split_axis=0, concat_axis=0, tiled=True)


def arr(*shape, dtype=BF):
    return jax.ShapeDtypeStruct(shape, dtype)


def local(
    measured, sensitivity, sample_lines, kspace_first, kspace_second, image_first, image_second
):
    space, ring = lax.axis_index("space"), lax.axis_index("ring")
    cos, sin = (jnp.asarray(t) for t in dft_tables())
    kband1, kband2 = (jnp.asarray(t) for t in kspace_bands())
    iband1, iband2 = (jnp.asarray(t) for t in image_bands())

    rows = space * ROWS + jnp.arange(ROWS, dtype=jnp.int32)
    sampled = jnp.any(sample_lines[:, :, None] == rows[None, None, :], axis=1)
    keep = sampled.astype(F32)[:, :, None]

    def rim(start):
        part = jnp.where(
            sampled[None, None, :, start : start + 2, None],
            measured[:, :, :, start : start + 2, :],
            jnp.zeros((), BF),
        )
        return part.transpose(0, 2, 1, 3, 4)

    up = [(i, i + 1) for i in range(SPACE - 1)]
    down = [(i + 1, i) for i in range(SPACE - 1)]
    low = lax.ppermute(rim(ROWS - 2), "space", up)
    high = lax.ppermute(rim(0), "space", down)
    halo = jnp.concatenate([low, high], axis=3).reshape(PAIRS, 8, N)

    def ends(first, last):
        return jnp.stack([1 - first.astype(F32), 1 - last.astype(F32)])

    kedge = ends(space == 0, space == SPACE - 1)
    kfirst = kspace_first.reshape(CH, 18)
    ksecond = kspace_second.transpose(3, 0, 2, 1).reshape(18, CH)
    zero = jnp.zeros_like(ksecond)
    ksecond = jnp.block([[ksecond, zero], [zero, ksecond]])
    ifirst = image_first.reshape(CH, 54)
    isecond = image_second.transpose(0, 2, 3, 4, 1).reshape(54, CH)
    zero = jnp.zeros_like(isecond)
    isecond = jnp.block([[isecond, zero], [zero, isecond]])

    kw1, kw2 = call(
        kspace_weights_kernel,
        [arr(HROWS * CH, 128), arr(96, HROWS * CH)],
        [],
        1,
        kedge, kfirst, ksecond, kband1, kband2,
    )
    half_done = call(
        kspace_kernel,
        arr(SPACE, 2, ROWS, LANES),
        [pltpu.VMEM((2, LANES, N), BF)]
        + [pltpu.VMEM((128, N), BF), pltpu.VMEM((HROWS * CH, N), BF)] * UNROLL,
        0,
        measured, halo, keep, kw1, kw2, cos, sin,
    )
    half_done = spread(half_done, "space")
    partial = call(
        combine_kernel,
        arr(RING, 64, N),
        [
            pltpu.VMEM((2, LANES, N), BF),
            pltpu.VMEM((2, 128, N), F32),
            pltpu.VMEM((2, 4, 128, 128), F32),
        ],
        0,
        half_done, sensitivity, cos, sin,
    )
    part = spread(partial, "ring").astype(F32).sum(axis=0).astype(BF)

    def place(half, i):
        return (half * RING + i % RING) * SPACE + i // RING

    count = RING * SPACE
    axes = ("half", "ring", "space")

    def moved(array, step, flip):
        pairs = [
            (place(half, i), place(half ^ flip, i + step))
            for half in range(HALVES)
            for i in range(count)
            if 0 <= i + step < count
        ]
        return lax.ppermute(array, axes, pairs)

    other = moved(part, 0, 1)
    image_in = (part.astype(F32) + other.astype(F32)).astype(BF)
    previous = moved(image_in[32:], 1, 0)
    following = moved(image_in[:32], -1, 0)
    iedge = ends((space == 0) & (ring == 0), (space == SPACE - 1) & (ring == RING - 1))
    copies = call(
        image_kernel,
        arr(RING, 64, N),
        [
            pltpu.VMEM((6 * CH, 144), BF),
            pltpu.VMEM((72, 6 * CH), BF),
            pltpu.VMEM((4, 128, 128), F32),
            pltpu.VMEM((480, N), BF),
            pltpu.VMEM((SLICES * 24, N), F32),
            pltpu.VMEM((4, SLICES * 8, 128), F32),
        ],
        1,
        iedge, previous, image_in, following, ifirst, isecond, iband1, iband2,
    )
    gathered = spread(copies, "ring")
    midway, image_out = call(
        expand_kernel,
        [arr(SPACE, 2, ROWS, LANES), arr(2, SLICES, ROWS, N)],
        [pltpu.VMEM((2, 4, 128, 128), F32), pltpu.VMEM((2, LANES, N), BF)],
        0,
        gathered, sensitivity, cos, sin,
    )
    midway = spread(midway, "space")
    kspace_out = call(
        finish_kernel,
        arr(COILS, 2, SLICES, ROWS, N),
        [pltpu.VMEM((2, LANES, N), BF)],
        0,
        midway, measured, keep, cos, sin,
    )
    return kspace_out, image_out


def solution(mesh):
    mesh = Mesh(mesh.devices.reshape(HALVES, RING, SPACE), ("half", "ring", "space"))
    placed = P(("half", "ring"), None, None, "space", None)
    return jax.shard_map(
        local,
        mesh=mesh,
        in_specs=(placed, placed, P(), P(), P(), P(), P()),
        out_specs=(placed, P(None, None, "space", None)),
        check_vma=False,
    )
```

```python
import math

import jax
import jax.numpy as jnp
import numpy as np
from jax import lax
from jax.experimental import pallas as pl
from jax.experimental.pallas import tpu as pltpu
from jax.sharding import Mesh
from jax.sharding import PartitionSpec as P

N = 512
COILS = 2
SLICES = 8
ROWS = 16
CH = 64
SPACE = 32
RING = 4
HALVES = 2
PAIRS = COILS * SLICES
LANES = PAIRS * ROWS
HROWS = ROWS + 2
UNROLL = 4
BF = jnp.bfloat16
F32 = jnp.float32
VMEM = pl.BlockSpec(memory_space=pltpu.VMEM)
SMEM = pl.BlockSpec(memory_space=pltpu.SMEM)
NT = (((1,), (1,)), ((), ()))


def dft_tables():
    position = np.arange(N)
    angles = (position[:, None] * position[None, :] % N).astype(np.float32) * np.float32(
        2.0 * math.pi / N
    )
    factor = np.float32(1.0 / math.sqrt(N))
    cos, sin = (np.cos(angles) * factor).astype(BF), (np.sin(angles) * factor).astype(BF)
    late = (position + np.where(position % ROWS < 2, ROWS, 0)) % N
    return cos, sin, cos[late], sin[late]


def iota(shape, dim):
    return lax.broadcasted_iota(jnp.int32, shape, dim)


def split(v, size, count):
    quotient = sum((v >= size * n).astype(jnp.int32) for n in range(1, count))
    return quotient, v - quotient * size


def kspace_weights(edge, first, second, w1, w2):
    h_row, rest = split(iota((18, 128), 0), 9, 2)
    p_row, q_row = split(rest, 3, 3)
    lane = iota((18, 128), 1)
    late = lane >= 96
    rest = jnp.where(late, lane - 96, lane)
    q_lane = jnp.where(late, rest >> 3, rest >> 5)
    h_lane = jnp.where(late, (rest >> 2) & 1, (rest >> 4) & 1)
    row = jnp.where(late, ROWS + (rest & 3), rest & 15)
    hidden_row = jnp.where((h_row == h_lane) & (q_row == q_lane), row - p_row, -1)
    late = iota((CH, 128), 1) >= 96
    for r in range(HROWS):
        band = jnp.where(hidden_row == r, 1.0, 0.0).astype(BF)
        block = dot(first[...], band)
        across = ~late if r + 1 >= ROWS else late
        block = jnp.where(across, block * edge[1], block)
        w1[r * CH : (r + 1) * CH, :] = block.astype(BF)
    line, lane = iota((96, 36), 0), iota((96, 36), 1)
    parity, rest = split(lane, 18, 2)
    q_lane, rest = split(rest, 6, 3)
    o_lane, p_lane = split(rest, 3, 2)
    place = line & 15
    place = jnp.where(place < 2, place + ROWS, place)
    match = (line >> 5 == q_lane) & ((line >> 4) & 1 == o_lane)
    pair_row = jnp.where(match, place + p_lane - 2 - parity, -1)
    late = (iota((96, 128), 0) & 15) < 2
    upper = iota((96, 128), 1) >= CH
    for pair in range(HROWS // 2):
        band = jnp.where(pair_row == 2 * pair, 1.0, 0.0).astype(BF)
        block = dot(band, second[...])
        beyond = 2 * pair + 1 + upper.astype(jnp.int32) >= ROWS
        block = jnp.where(late != beyond, block * edge[1], block)
        w2[:, pair * 128 : (pair + 1) * 128] = block.astype(BF)


def image_bands():
    first = np.zeros((6, 54, 144), np.float32)
    for x in range(6):
        for h in range(2):
            for a in range(3):
                for p in range(3):
                    for q in range(3):
                        first[x, h * 27 + a * 9 + p * 3 + q, a * 48 + q * 16 + (x + p) * 2 + h] = 1
    second = np.zeros((3, 72, 108), np.float32)
    for pair in range(3):
        for parity in range(2):
            for o in range(2):
                for a in range(3):
                    for q in range(3):
                        for e in range(4):
                            p = 2 * pair + parity - e
                            if 0 <= p < 3:
                                second[
                                    pair,
                                    a * 24 + q * 8 + o * 4 + e,
                                    parity * 54 + o * 27 + a * 9 + p * 3 + q,
                                ] = 1
    return first.astype(BF), second.astype(BF)


def dot(a, b):
    return jnp.dot(a, b, preferred_element_type=F32)


def dot_nt(a, b):
    return lax.dot_general(a, b, NT, preferred_element_type=F32)


def before(v):
    lane = lax.broadcasted_iota(jnp.int32, v.shape, 1)
    return jnp.where(lane == 0, 0.0, pltpu.roll(v, 1, 1))


def after(v):
    lane = lax.broadcasted_iota(jnp.int32, v.shape, 1)
    return jnp.where(lane == N - 1, 0.0, pltpu.roll(v, N - 1, 1))


def blocks_swapped(tiles):
    tiles = list(tiles)
    group = lax.broadcasted_iota(jnp.int32, tiles[0].shape, 1) // 16
    for bit in (4, 2, 1):
        upper = (group & bit) != 0
        for i in range(8):
            if i & bit:
                continue
            a, b = tiles[i], tiles[i + bit]
            tiles[i] = jnp.where(upper, pltpu.roll(b, 16 * bit, 1), a)
            tiles[i + bit] = jnp.where(upper, b, pltpu.roll(a, 128 - 16 * bit, 1))
    return tiles


def wide(ref, *where):
    *lead, rows = where
    return jnp.concatenate([ref[(*lead, b, rows, slice(None))] for b in range(4)], axis=1)


def put(ref, value, *where):
    *lead, rows = where
    for b in range(4):
        ref[(*lead, b, rows, slice(None))] = value[:, b * 128 : (b + 1) * 128]


def regroup(received, left):
    for octet in range(SPACE // 8):
        for coil in range(COILS):
            tiles = [
                received[octet * 8 + i, :, :, coil * 128 : (coil + 1) * 128]
                .astype(F32)
                .reshape(32, 128)
                for i in range(8)
            ]
            for s, tile in enumerate(blocks_swapped(tiles)):
                row = coil * 128 + s * 16
                tile = tile.astype(BF)
                for h in range(2):
                    left[h, row : row + 16, octet * 128 : (octet + 1) * 128] = tile[
                        h * 16 : (h + 1) * 16
                    ]


def kspace_kernel(measured, halo, keep, follow, w1, w2, cos, sin, out, refined, *scratch):
    def one(i, x3, hidden):
        c, s = i // SLICES, i % SLICES
        mask = keep[s] > 0
        own = jnp.concatenate(
            [jnp.where(mask, measured[c, h, s].astype(F32), 0.0) for h in range(2)], axis=0
        )
        rim = jnp.where(follow[s] > 0, halo[i].astype(F32)[0:8], 0.0)
        two = iota((8, N), 0) < 2
        held = jnp.concatenate(
            [
                jnp.where(two, rim, own[0:8]),
                own[8:16],
                jnp.where(two, pltpu.roll(rim, 4, 0), own[16:24]),
                own[24:32],
            ],
            axis=0,
        )
        x3[0:32] = before(own).astype(BF)
        x3[32:64] = own.astype(BF)
        x3[64:96] = after(own).astype(BF)
        x3[96:128] = jnp.concatenate(
            [before(rim), rim, after(rim), jnp.zeros_like(rim)], axis=0
        ).astype(BF)
        hidden[...] = jnp.maximum(dot(w1[...], x3[...]).astype(BF), 0)
        spread = dot(w2[...], hidden[...])
        total = held + before(spread[0:32]) + spread[32:64] + after(spread[64:96])
        total = total.astype(BF)
        row = pl.multiple_of(i * 16, 16)
        for h in range(2):
            refined[h, pl.ds(row, 16), :] = total[h * 16 : (h + 1) * 16]

    def step(i, carry):
        for k in range(UNROLL):
            one(i * UNROLL + k, scratch[2 * k], scratch[2 * k + 1])
        return carry

    lax.fori_loop(0, PAIRS // UNROLL, step, 0)
    for part in range(2):
        rows = pl.ds(part * 256, 256)
        co, si = cos[rows, :], sin[rows, :]
        real = dot_nt(co, refined[0]) - dot_nt(si, refined[1])
        imag = dot_nt(si, refined[0]) + dot_nt(co, refined[1])
        out[part * 16 : (part + 1) * 16, 0] = real.astype(BF).reshape(16, 16, LANES)
        out[part * 16 : (part + 1) * 16, 1] = imag.astype(BF).reshape(16, 16, LANES)


def combine_kernel(received, sens, halo, cos, sin, out, left, image, partial):
    regroup(received, left)
    for c in range(COILS):
        rows = slice(c * 128, (c + 1) * 128)
        image[0] = dot(left[0, rows], cos[...]) - dot(left[1, rows], sin[...])
        image[1] = dot(left[0, rows], sin[...]) + dot(left[1, rows], cos[...])
        for s in range(SLICES):
            rows = slice(s * 16, (s + 1) * 16)
            real, imag = image[0, rows], image[1, rows]
            extra = halo[c * SLICES + s].astype(F32)
            sr, si = (
                jnp.concatenate(
                    [extra[8 + 2 * h : 10 + 2 * h], sens[c, h, s].astype(F32)[2:]], axis=0
                )
                for h in range(2)
            )
            pr = sr * real + si * imag
            pi = sr * imag - si * real
            if c:
                pr = pr + wide(partial, 0, rows)
                pi = pi + wide(partial, 1, rows)
            put(partial, pr, 0, rows)
            put(partial, pi, 1, rows)
    for x in range(ROWS):
        place = (x + 2) % ROWS
        both = jnp.concatenate(
            [wide(partial, h, pl.ds(place, 8, stride=16)) for h in range(2)], axis=0
        )
        out[x // 4, x % 4 * 16 : (x % 4 + 1) * 16] = both.astype(BF)


def image_kernel(
    edge, previous, own, first, second, band1, band2, out,
    w1, w2, rows8, x3, acc, fin
):
    for x in range(6):
        block = dot(first[...], band1[x])
        if x == 0:
            block = block * edge[0]
        if x == 5:
            block = block * edge[1]
        w1[x * CH : (x + 1) * CH, :] = block.astype(BF)
    for pair in range(3):
        w2[:, pair * 128 : (pair + 1) * 128] = dot(band2[pair], second[...]).astype(BF)
    put(rows8, previous[0:32].astype(F32) * edge[0], slice(0, 32))
    put(rows8, previous[32:64].astype(F32), slice(32, 64))
    put(rows8, own[0:32].astype(F32), slice(64, 96))
    put(rows8, own[32:64].astype(F32) * edge[1], slice(96, 128))
    x3[0:48] = jnp.zeros((48, N), BF)
    x3[432:480] = jnp.zeros((48, N), BF)
    for s in range(SLICES):
        v = wide(rows8, pl.ds(s, 16, stride=8))
        base = (s + 1) * 48
        x3[base : base + 16] = before(v).astype(BF)
        x3[base + 16 : base + 32] = v.astype(BF)
        x3[base + 32 : base + 48] = after(v).astype(BF)
    acc[...] = jnp.zeros_like(acc)
    for t in range(SLICES):
        hidden = jnp.maximum(dot(w1[...], x3[t * 48 : t * 48 + 144]).astype(BF), 0)
        spread = dot(w2[...], hidden)
        for a in range(3):
            s = t + 1 - a
            if 0 <= s < SLICES:
                acc[s * 24 : (s + 1) * 24] = acc[s * 24 : (s + 1) * 24] + spread[a * 24 : (a + 1) * 24]
    for s in range(SLICES):
        v = acc[s * 24 : (s + 1) * 24]
        put(fin, before(v[0:8]) + v[8:16] + after(v[16:24]), slice(s * 8, (s + 1) * 8))
    for e in range(4):
        update = jnp.concatenate([wide(fin, pl.ds(o * 4 + e, 8, stride=8)) for o in range(2)], axis=0)
        value = (wide(rows8, slice(32 + e * 16, 48 + e * 16)) + update).astype(BF)
        for y in range(RING):
            out[y, e * 16 : (e + 1) * 16] = value


def expand_kernel(gathered, sens, cos, sin, out, image_out, image, data):
    for x in range(ROWS):
        both = gathered[x // 4, x % 4 * 16 : (x % 4 + 1) * 16].astype(F32)
        for h in range(2):
            put(image, both[h * 8 : (h + 1) * 8], h, pl.ds(x, 8, stride=16))
    for s in range(SLICES):
        rows = slice(s * 16, (s + 1) * 16)
        real, imag = wide(image, 0, rows), wide(image, 1, rows)
        image_out[0, s] = real.astype(BF)
        image_out[1, s] = imag.astype(BF)
        for c in range(COILS):
            sr, si = sens[c, 0, s].astype(F32), sens[c, 1, s].astype(F32)
            rows = slice(c * 128 + s * 16, c * 128 + (s + 1) * 16)
            data[0, rows] = (sr * real - si * imag).astype(BF)
            data[1, rows] = (sr * imag + si * real).astype(BF)
    for part in range(2):
        rows = pl.ds(part * 256, 256)
        co, si = cos[rows, :], sin[rows, :]
        real = dot_nt(co, data[0]) + dot_nt(si, data[1])
        imag = dot_nt(co, data[1]) - dot_nt(si, data[0])
        out[part * 16 : (part + 1) * 16, 0] = real.astype(BF).reshape(16, 16, LANES)
        out[part * 16 : (part + 1) * 16, 1] = imag.astype(BF).reshape(16, 16, LANES)


def finish_kernel(received, measured, keep, cos, sin, out, left):
    regroup(received, left)
    for c in range(COILS):
        rows = slice(c * 128, (c + 1) * 128)
        real = dot(left[0, rows], cos[...]) + dot(left[1, rows], sin[...])
        imag = dot(left[1, rows], cos[...]) - dot(left[0, rows], sin[...])
        for s in range(SLICES):
            mask = keep[s] > 0
            rows = slice(s * 16, (s + 1) * 16)
            for h, value in enumerate((real, imag)):
                out[c, h, s] = jnp.where(
                    mask, measured[c, h, s].astype(F32), value[rows]
                ).astype(BF)


def call(kernel, shapes, scratch, scalars, *operands):
    single = not isinstance(shapes, list)
    return pl.pallas_call(
        kernel,
        out_shape=shapes,
        in_specs=[SMEM] * scalars + [VMEM] * (len(operands) - scalars),
        out_specs=VMEM if single else [VMEM] * len(shapes),
        scratch_shapes=scratch,
        compiler_params=pltpu.CompilerParams(vmem_limit_bytes=40 * 1024 * 1024),
    )(*operands)


def spread(array, axis):
    return lax.all_to_all(array, axis, split_axis=0, concat_axis=0, tiled=True)


def arr(*shape, dtype=BF):
    return jax.ShapeDtypeStruct(shape, dtype)


def local(
    measured, sensitivity, sample_lines, kspace_first, kspace_second, image_first, image_second
):
    space, ring = lax.axis_index("space"), lax.axis_index("ring")
    cos, sin, lcos, lsin = (jnp.asarray(t) for t in dft_tables())
    iband1, iband2 = (jnp.asarray(t) for t in image_bands())

    rim = jnp.concatenate(
        [
            measured[:, :, :, :4].transpose(0, 2, 1, 3, 4).reshape(PAIRS, 8, N),
            sensitivity[:, :, :, :2].transpose(0, 2, 1, 3, 4).reshape(PAIRS, 4, N),
        ],
        axis=1,
    )
    halo = lax.ppermute(rim, "space", [((i + 1) % SPACE, i) for i in range(SPACE)])

    rows = (space * ROWS + jnp.arange(ROWS + 4, dtype=jnp.int32)) % N
    sampled = jnp.any(sample_lines[:, :, None] == rows[None, None, :], axis=1).astype(F32)
    keep = sampled[:, :ROWS, None]
    follow = jnp.tile(sampled[:, ROWS:], (1, 2))[:, :, None]

    def ends(first, last):
        return jnp.stack([1 - first.astype(F32), 1 - last.astype(F32)])

    kedge = ends(space == 0, space == SPACE - 1)
    kfirst = kspace_first.reshape(CH, 18)
    ksecond = kspace_second.transpose(3, 0, 2, 1).reshape(18, CH)
    zero = jnp.zeros_like(ksecond)
    ksecond = jnp.block([[ksecond, zero], [zero, ksecond]])
    ifirst = image_first.reshape(CH, 54)
    isecond = image_second.transpose(0, 2, 3, 4, 1).reshape(54, CH)
    zero = jnp.zeros_like(isecond)
    isecond = jnp.block([[isecond, zero], [zero, isecond]])

    kw1, kw2 = call(
        kspace_weights,
        [arr(HROWS * CH, 128), arr(96, HROWS * CH)],
        [],
        1,
        kedge, kfirst, ksecond,
    )
    half_done = call(
        kspace_kernel,
        arr(SPACE, 2, ROWS, LANES),
        [pltpu.VMEM((2, LANES, N), BF)]
        + [pltpu.VMEM((128, N), BF), pltpu.VMEM((HROWS * CH, N), BF)] * UNROLL,
        0,
        measured, halo, keep, follow, kw1, kw2, lcos, lsin,
    )
    half_done = spread(half_done, "space")
    partial = call(
        combine_kernel,
        arr(RING, 64, N),
        [
            pltpu.VMEM((2, LANES, N), BF),
            pltpu.VMEM((2, 128, N), F32),
            pltpu.VMEM((2, 4, 128, 128), F32),
        ],
        0,
        half_done, sensitivity, halo, lcos, lsin,
    )
    part = spread(partial, "ring").astype(F32).sum(axis=0).astype(BF)

    def place(half, i):
        return (half * RING + i % RING) * SPACE + i // RING

    count = RING * SPACE
    axes = ("half", "ring", "space")

    def moved(array, step, flip):
        pairs = [
            (place(half, i), place(half ^ flip, (i + step) % count))
            for half in range(HALVES)
            for i in range(count)
        ]
        return lax.ppermute(array, axes, pairs)

    other = moved(part, 0, 1)
    image_in = (part.astype(F32) + other.astype(F32)).astype(BF)
    previous = moved(image_in, 1, 0)
    iedge = ends((space == 0) & (ring == 0), (space == SPACE - 1) & (ring == RING - 1))
    copies = call(
        image_kernel,
        arr(RING, 64, N),
        [
            pltpu.VMEM((6 * CH, 144), BF),
            pltpu.VMEM((72, 6 * CH), BF),
            pltpu.VMEM((4, 128, 128), F32),
            pltpu.VMEM((480, N), BF),
            pltpu.VMEM((SLICES * 24, N), F32),
            pltpu.VMEM((4, SLICES * 8, 128), F32),
        ],
        1,
        iedge, previous, image_in, ifirst, isecond, iband1, iband2,
    )
    gathered = spread(copies, "ring")
    midway, image_out = call(
        expand_kernel,
        [arr(SPACE, 2, ROWS, LANES), arr(2, SLICES, ROWS, N)],
        [pltpu.VMEM((2, 4, 128, 128), F32), pltpu.VMEM((2, LANES, N), BF)],
        0,
        gathered, sensitivity, cos, sin,
    )
    midway = spread(midway, "space")
    kspace_out = call(
        finish_kernel,
        arr(COILS, 2, SLICES, ROWS, N),
        [pltpu.VMEM((2, LANES, N), BF)],
        0,
        midway, measured, keep, cos, sin,
    )
    return kspace_out, image_out


def solution(mesh):
    mesh = Mesh(mesh.devices.reshape(HALVES, RING, SPACE), ("half", "ring", "space"))
    placed = P(("half", "ring"), None, None, "space", None)
    return jax.shard_map(
        local,
        mesh=mesh,
        in_specs=(placed, placed, P(), P(), P(), P(), P()),
        out_specs=(placed, P(None, None, "space", None)),
        check_vma=False,
    )
```

```python
import math

import jax
import jax.numpy as jnp
import numpy as np
from jax import lax
from jax.experimental import pallas as pl
from jax.experimental.pallas import tpu as pltpu
from jax.sharding import Mesh
from jax.sharding import PartitionSpec as P

N = 512
COILS = 2
SLICES = 8
ROWS = 16
CH = 64
SPACE = 32
RING = 4
HALVES = 2
PAIRS = COILS * SLICES
LANES = PAIRS * ROWS
HROWS = ROWS + 2
UNROLL = 8
BF = jnp.bfloat16
F32 = jnp.float32
VMEM = pl.BlockSpec(memory_space=pltpu.VMEM)
SMEM = pl.BlockSpec(memory_space=pltpu.SMEM)
NT = (((1,), (1,)), ((), ()))


def dft_tables():
    position = np.arange(N)
    angles = (position[:, None] * position[None, :] % N).astype(np.float32) * np.float32(
        2.0 * math.pi / N
    )
    factor = np.float32(1.0 / math.sqrt(N))
    cos, sin = (np.cos(angles) * factor).astype(BF), (np.sin(angles) * factor).astype(BF)
    late = (position + np.where(position % ROWS < 2, ROWS, 0)) % N
    return cos, sin, cos[late], sin[late]


def iota(shape, dim):
    return lax.broadcasted_iota(jnp.int32, shape, dim)


def split(v, size, count):
    quotient = sum((v >= size * n).astype(jnp.int32) for n in range(1, count))
    return quotient, v - quotient * size


def kspace_weights(edge, first, second, w1, w2):
    h_row, rest = split(iota((18, 128), 0), 9, 2)
    p_row, q_row = split(rest, 3, 3)
    lane = iota((18, 128), 1)
    late = lane >= 96
    rest = jnp.where(late, lane - 96, lane)
    q_lane = jnp.where(late, rest >> 3, rest >> 5)
    h_lane = jnp.where(late, (rest >> 2) & 1, (rest >> 4) & 1)
    row = jnp.where(late, ROWS + (rest & 3), rest & 15)
    hidden_row = jnp.where((h_row == h_lane) & (q_row == q_lane), row - p_row, -1)
    late = iota((CH, 128), 1) >= 96
    for r in range(HROWS):
        band = jnp.where(hidden_row == r, 1.0, 0.0).astype(BF)
        block = dot(first[...], band)
        across = ~late if r + 1 >= ROWS else late
        block = jnp.where(across, block * edge[1], block)
        w1[r * CH : (r + 1) * CH, :] = block.astype(BF)
    line, lane = iota((96, 36), 0), iota((96, 36), 1)
    parity, rest = split(lane, 18, 2)
    q_lane, rest = split(rest, 6, 3)
    o_lane, p_lane = split(rest, 3, 2)
    place = line & 15
    place = jnp.where(place < 2, place + ROWS, place)
    match = (line >> 5 == q_lane) & ((line >> 4) & 1 == o_lane)
    pair_row = jnp.where(match, place + p_lane - 2 - parity, -1)
    late = (iota((96, 128), 0) & 15) < 2
    upper = iota((96, 128), 1) >= CH
    for pair in range(HROWS // 2):
        band = jnp.where(pair_row == 2 * pair, 1.0, 0.0).astype(BF)
        block = dot(band, second[...])
        beyond = 2 * pair + 1 + upper.astype(jnp.int32) >= ROWS
        block = jnp.where(late != beyond, block * edge[1], block)
        w2[:, pair * 128 : (pair + 1) * 128] = block.astype(BF)


def image_bands():
    first = np.zeros((6, 54, 144), np.float32)
    for x in range(6):
        for h in range(2):
            for a in range(3):
                for p in range(3):
                    for q in range(3):
                        first[x, h * 27 + a * 9 + p * 3 + q, a * 48 + q * 16 + (x + p) * 2 + h] = 1
    second = np.zeros((3, 72, 108), np.float32)
    for pair in range(3):
        for parity in range(2):
            for o in range(2):
                for a in range(3):
                    for q in range(3):
                        for e in range(4):
                            p = 2 * pair + parity - e
                            if 0 <= p < 3:
                                second[
                                    pair,
                                    a * 24 + q * 8 + o * 4 + e,
                                    parity * 54 + o * 27 + a * 9 + p * 3 + q,
                                ] = 1
    return first.astype(BF), second.astype(BF)


def dot(a, b):
    return jnp.dot(a, b, preferred_element_type=F32)


def dot_nt(a, b):
    return lax.dot_general(a, b, NT, preferred_element_type=F32)


def before(v):
    lane = lax.broadcasted_iota(jnp.int32, v.shape, 1)
    return jnp.where(lane == 0, 0.0, pltpu.roll(v, 1, 1))


def after(v):
    lane = lax.broadcasted_iota(jnp.int32, v.shape, 1)
    return jnp.where(lane == N - 1, 0.0, pltpu.roll(v, N - 1, 1))


def blocks_swapped(tiles):
    tiles = list(tiles)
    group = lax.broadcasted_iota(jnp.int32, tiles[0].shape, 1) // 16
    for bit in (4, 2, 1):
        upper = (group & bit) != 0
        for i in range(8):
            if i & bit:
                continue
            a, b = tiles[i], tiles[i + bit]
            tiles[i] = jnp.where(upper, pltpu.roll(b, 16 * bit, 1), a)
            tiles[i + bit] = jnp.where(upper, b, pltpu.roll(a, 128 - 16 * bit, 1))
    return tiles


def wide(ref, *where):
    *lead, rows = where
    return jnp.concatenate([ref[(*lead, b, rows, slice(None))] for b in range(4)], axis=1)


def put(ref, value, *where):
    *lead, rows = where
    for b in range(4):
        ref[(*lead, b, rows, slice(None))] = value[:, b * 128 : (b + 1) * 128]


def regroup(received, left, coil):
    for octet in range(SPACE // 8):
        tiles = [
            received[octet * 8 + i, :, :, coil * 128 : (coil + 1) * 128]
            .astype(F32)
            .reshape(32, 128)
            for i in range(8)
        ]
        for s, tile in enumerate(blocks_swapped(tiles)):
            row = coil * 128 + s * 16
            tile = tile.astype(BF)
            for h in range(2):
                left[h, row : row + 16, octet * 128 : (octet + 1) * 128] = tile[
                    h * 16 : (h + 1) * 16
                ]


def pack_kernel(measured, sens, out):
    for i in range(PAIRS):
        c, s = i // SLICES, i % SLICES
        out[i] = jnp.concatenate(
            [measured[c, h, s].astype(F32)[:4] for h in range(2)]
            + [sens[c, h, s].astype(F32)[:2] for h in range(2)],
            axis=0,
        ).astype(BF)


def kspace_kernel(measured, halo, keep, follow, w1, w2, cos, sin, out, refined, *scratch):
    def one(i, x3, hidden):
        c, s = i // SLICES, i % SLICES
        mask = keep[s] > 0
        own = jnp.concatenate(
            [jnp.where(mask, measured[c, h, s].astype(F32), 0.0) for h in range(2)], axis=0
        )
        rim = jnp.where(follow[s] > 0, halo[i].astype(F32)[0:8], 0.0)
        two = iota((8, N), 0) < 2
        held = jnp.concatenate(
            [
                jnp.where(two, rim, own[0:8]),
                own[8:16],
                jnp.where(two, pltpu.roll(rim, 4, 0), own[16:24]),
                own[24:32],
            ],
            axis=0,
        )
        x3[0:32] = before(own).astype(BF)
        x3[32:64] = own.astype(BF)
        x3[64:96] = after(own).astype(BF)
        x3[96:128] = jnp.concatenate(
            [before(rim), rim, after(rim), jnp.zeros_like(rim)], axis=0
        ).astype(BF)
        hidden[...] = jnp.maximum(dot(w1[...], x3[...]).astype(BF), 0)
        spread = dot(w2[...], hidden[...])
        total = held + before(spread[0:32]) + spread[32:64] + after(spread[64:96])
        total = total.astype(BF)
        row = pl.multiple_of(i * 16, 16)
        for h in range(2):
            refined[h, pl.ds(row, 16), :] = total[h * 16 : (h + 1) * 16]

    def step(i, carry):
        for k in range(UNROLL):
            one(i * UNROLL + k, scratch[2 * k], scratch[2 * k + 1])
        return carry

    lax.fori_loop(0, PAIRS // UNROLL, step, 0)
    for part in range(2):
        rows = pl.ds(part * 256, 256)
        co, si = cos[rows, :], sin[rows, :]
        real = dot_nt(co, refined[0]) - dot_nt(si, refined[1])
        imag = dot_nt(si, refined[0]) + dot_nt(co, refined[1])
        out[part * 16 : (part + 1) * 16, 0] = real.astype(BF).reshape(16, 16, LANES)
        out[part * 16 : (part + 1) * 16, 1] = imag.astype(BF).reshape(16, 16, LANES)


def combine_kernel(received, sens, halo, cos, sin, out, left, image, partial):
    for c in range(COILS):
        regroup(received, left, c)
        rows = slice(c * 128, (c + 1) * 128)
        image[c, 0] = dot(left[0, rows], cos[...]) - dot(left[1, rows], sin[...])
        image[c, 1] = dot(left[0, rows], sin[...]) + dot(left[1, rows], cos[...])
        for s in range(SLICES):
            rows = slice(s * 16, (s + 1) * 16)
            real, imag = image[c, 0, rows], image[c, 1, rows]
            extra = halo[c * SLICES + s].astype(F32)
            sr, si = (
                jnp.concatenate(
                    [extra[8 + 2 * h : 10 + 2 * h], sens[c, h, s].astype(F32)[2:]], axis=0
                )
                for h in range(2)
            )
            pr = sr * real + si * imag
            pi = sr * imag - si * real
            if c:
                pr = pr + wide(partial, 0, rows)
                pi = pi + wide(partial, 1, rows)
            put(partial, pr, 0, rows)
            put(partial, pi, 1, rows)
    for x in range(ROWS):
        place = (x + 2) % ROWS
        both = jnp.concatenate(
            [wide(partial, h, pl.ds(place, 8, stride=16)) for h in range(2)], axis=0
        )
        out[x // 4, x % 4 * 16 : (x % 4 + 1) * 16] = both.astype(BF)


def image_weights(edge, first, second, band1, band2, w1, w2):
    for x in range(6):
        block = dot(first[...], band1[x])
        if x == 0:
            block = block * edge[0]
        if x == 5:
            block = block * edge[1]
        w1[x * CH : (x + 1) * CH, :] = block.astype(BF)
    for pair in range(3):
        w2[:, pair * 128 : (pair + 1) * 128] = dot(band2[pair], second[...]).astype(BF)


def image_kernel(edge, previous, own, w1, w2, out, rows8, x3, acc, fin):
    put(rows8, previous[0:32].astype(F32) * edge[0], slice(0, 32))
    put(rows8, previous[32:64].astype(F32), slice(32, 64))
    put(rows8, own[0:32].astype(F32), slice(64, 96))
    put(rows8, own[32:64].astype(F32) * edge[1], slice(96, 128))
    x3[0:48] = jnp.zeros((48, N), BF)
    x3[432:480] = jnp.zeros((48, N), BF)
    for s in range(SLICES):
        v = wide(rows8, pl.ds(s, 16, stride=8))
        base = (s + 1) * 48
        x3[base : base + 16] = before(v).astype(BF)
        x3[base + 16 : base + 32] = v.astype(BF)
        x3[base + 32 : base + 48] = after(v).astype(BF)
    acc[...] = jnp.zeros_like(acc)
    for t in range(SLICES):
        hidden = jnp.maximum(dot(w1[...], x3[t * 48 : t * 48 + 144]).astype(BF), 0)
        spread = dot(w2[...], hidden)
        for a in range(3):
            s = t + 1 - a
            if 0 <= s < SLICES:
                acc[s * 24 : (s + 1) * 24] = acc[s * 24 : (s + 1) * 24] + spread[a * 24 : (a + 1) * 24]
    for s in range(SLICES):
        v = acc[s * 24 : (s + 1) * 24]
        put(fin, before(v[0:8]) + v[8:16] + after(v[16:24]), slice(s * 8, (s + 1) * 8))
    for e in range(4):
        update = jnp.concatenate([wide(fin, pl.ds(o * 4 + e, 8, stride=8)) for o in range(2)], axis=0)
        value = (wide(rows8, slice(32 + e * 16, 48 + e * 16)) + update).astype(BF)
        for y in range(RING):
            out[y, e * 16 : (e + 1) * 16] = value


def expand_kernel(gathered, sens, cos, sin, out, image_out, image, data):
    for x in range(ROWS):
        both = gathered[x // 4, x % 4 * 16 : (x % 4 + 1) * 16].astype(F32)
        for h in range(2):
            put(image, both[h * 8 : (h + 1) * 8], h, pl.ds(x, 8, stride=16))
    for s in range(SLICES):
        rows = slice(s * 16, (s + 1) * 16)
        real, imag = wide(image, 0, rows), wide(image, 1, rows)
        image_out[0, s] = real.astype(BF)
        image_out[1, s] = imag.astype(BF)
        for c in range(COILS):
            sr, si = sens[c, 0, s].astype(F32), sens[c, 1, s].astype(F32)
            rows = slice(c * 128 + s * 16, c * 128 + (s + 1) * 16)
            data[0, rows] = (sr * real - si * imag).astype(BF)
            data[1, rows] = (sr * imag + si * real).astype(BF)
    for part in range(2):
        rows = pl.ds(part * 256, 256)
        co, si = cos[rows, :], sin[rows, :]
        real = dot_nt(co, data[0]) + dot_nt(si, data[1])
        imag = dot_nt(co, data[1]) - dot_nt(si, data[0])
        out[part * 16 : (part + 1) * 16, 0] = real.astype(BF).reshape(16, 16, LANES)
        out[part * 16 : (part + 1) * 16, 1] = imag.astype(BF).reshape(16, 16, LANES)


def finish_kernel(received, measured, keep, cos, sin, out, left):
    for c in range(COILS):
        regroup(received, left, c)
        rows = slice(c * 128, (c + 1) * 128)
        real = dot(left[0, rows], cos[...]) + dot(left[1, rows], sin[...])
        imag = dot(left[1, rows], cos[...]) - dot(left[0, rows], sin[...])
        for s in range(SLICES):
            mask = keep[s] > 0
            rows = slice(s * 16, (s + 1) * 16)
            for h, value in enumerate((real, imag)):
                out[c, h, s] = jnp.where(
                    mask, measured[c, h, s].astype(F32), value[rows]
                ).astype(BF)


def call(kernel, shapes, scratch, scalars, *operands):
    single = not isinstance(shapes, list)
    return pl.pallas_call(
        kernel,
        out_shape=shapes,
        in_specs=[SMEM] * scalars + [VMEM] * (len(operands) - scalars),
        out_specs=VMEM if single else [VMEM] * len(shapes),
        scratch_shapes=scratch,
        compiler_params=pltpu.CompilerParams(vmem_limit_bytes=40 * 1024 * 1024),
    )(*operands)


def spread(array, axis):
    return lax.all_to_all(array, axis, split_axis=0, concat_axis=0, tiled=True)


def arr(*shape, dtype=BF):
    return jax.ShapeDtypeStruct(shape, dtype)


def local(
    measured, sensitivity, sample_lines, kspace_first, kspace_second, image_first, image_second
):
    space, ring = lax.axis_index("space"), lax.axis_index("ring")
    cos, sin, lcos, lsin = (jnp.asarray(t) for t in dft_tables())
    iband1, iband2 = (jnp.asarray(t) for t in image_bands())

    eight = pl.BlockSpec((COILS, 2, SLICES, 8, N), lambda i: (0, 0, 0, 0, 0))
    rim = pl.pallas_call(
        pack_kernel, grid=(1,), out_shape=arr(PAIRS, 12, N), in_specs=[eight, eight]
    )(measured, sensitivity)
    halo = lax.ppermute(rim, "space", [((i + 1) % SPACE, i) for i in range(SPACE)])

    rows = (space * ROWS + jnp.arange(ROWS + 4, dtype=jnp.int32)) % N
    sampled = jnp.any(sample_lines[:, :, None] == rows[None, None, :], axis=1).astype(F32)
    keep = sampled[:, :ROWS, None]
    follow = jnp.tile(sampled[:, ROWS:], (1, 2))[:, :, None]

    def ends(first, last):
        return jnp.stack([1 - first.astype(F32), 1 - last.astype(F32)])

    kedge = ends(space == 0, space == SPACE - 1)
    kfirst = kspace_first.reshape(CH, 18)
    ksecond = kspace_second.transpose(3, 0, 2, 1).reshape(18, CH)
    zero = jnp.zeros_like(ksecond)
    ksecond = jnp.block([[ksecond, zero], [zero, ksecond]])
    ifirst = image_first.reshape(CH, 54)
    isecond = image_second.transpose(0, 2, 3, 4, 1).reshape(54, CH)
    zero = jnp.zeros_like(isecond)
    isecond = jnp.block([[isecond, zero], [zero, isecond]])

    kw1, kw2 = call(
        kspace_weights,
        [arr(HROWS * CH, 128), arr(96, HROWS * CH)],
        [],
        1,
        kedge, kfirst, ksecond,
    )
    half_done = call(
        kspace_kernel,
        arr(SPACE, 2, ROWS, LANES),
        [pltpu.VMEM((2, LANES, N), BF)]
        + [pltpu.VMEM((128, N), BF), pltpu.VMEM((HROWS * CH, N), BF)] * UNROLL,
        0,
        measured, halo, keep, follow, kw1, kw2, lcos, lsin,
    )
    half_done = spread(half_done, "space")
    partial = call(
        combine_kernel,
        arr(RING, 64, N),
        [
            pltpu.VMEM((2, LANES, N), BF),
            pltpu.VMEM((COILS, 2, 128, N), F32),
            pltpu.VMEM((2, 4, 128, 128), F32),
        ],
        0,
        half_done, sensitivity, halo, lcos, lsin,
    )
    part = spread(partial, "ring").astype(F32).sum(axis=0).astype(BF)

    def place(half, i):
        return (half * RING + i % RING) * SPACE + i // RING

    count = RING * SPACE
    axes = ("half", "ring", "space")

    def moved(array, step, flip):
        pairs = [
            (place(half, i), place(half ^ flip, (i + step) % count))
            for half in range(HALVES)
            for i in range(count)
        ]
        return lax.ppermute(array, axes, pairs)

    other = moved(part, 0, 1)
    image_in = (part.astype(F32) + other.astype(F32)).astype(BF)
    previous = moved(image_in, 1, 0)
    iedge = ends((space == 0) & (ring == 0), (space == SPACE - 1) & (ring == RING - 1))
    iw1, iw2 = call(
        image_weights,
        [arr(6 * CH, 144), arr(72, 6 * CH)],
        [],
        1,
        iedge, ifirst, isecond, iband1, iband2,
    )
    copies = call(
        image_kernel,
        arr(RING, 64, N),
        [
            pltpu.VMEM((4, 128, 128), F32),
            pltpu.VMEM((480, N), BF),
            pltpu.VMEM((SLICES * 24, N), F32),
            pltpu.VMEM((4, SLICES * 8, 128), F32),
        ],
        1,
        iedge, previous, image_in, iw1, iw2,
    )
    gathered = spread(copies, "ring")
    midway, image_out = call(
        expand_kernel,
        [arr(SPACE, 2, ROWS, LANES), arr(2, SLICES, ROWS, N)],
        [pltpu.VMEM((2, 4, 128, 128), F32), pltpu.VMEM((2, LANES, N), BF)],
        0,
        gathered, sensitivity, cos, sin,
    )
    midway = spread(midway, "space")
    kspace_out = call(
        finish_kernel,
        arr(COILS, 2, SLICES, ROWS, N),
        [pltpu.VMEM((2, LANES, N), BF)],
        0,
        midway, measured, keep, cos, sin,
    )
    return kspace_out, image_out


def solution(mesh):
    mesh = Mesh(mesh.devices.reshape(HALVES, RING, SPACE), ("half", "ring", "space"))
    placed = P(("half", "ring"), None, None, "space", None)
    return jax.shard_map(
        local,
        mesh=mesh,
        in_specs=(placed, placed, P(), P(), P(), P(), P()),
        out_specs=(placed, P(None, None, "space", None)),
        check_vma=False,
    )
```

```python
import math

import jax
import jax.numpy as jnp
import numpy as np
from jax import lax
from jax.experimental import pallas as pl
from jax.experimental.pallas import tpu as pltpu
from jax.sharding import Mesh
from jax.sharding import PartitionSpec as P

N = 512
COILS = 2
SLICES = 8
ROWS = 16
CH = 64
SPACE = 32
RING = 4
HALVES = 2
PAIRS = COILS * SLICES
LANES = PAIRS * ROWS
HROWS = ROWS + 2
UNROLL = 8
BF = jnp.bfloat16
F32 = jnp.float32
VMEM = pl.BlockSpec(memory_space=pltpu.VMEM)
SMEM = pl.BlockSpec(memory_space=pltpu.SMEM)
NT = (((1,), (1,)), ((), ()))
TN = (((0,), (0,)), ((), ()))


def dft_tables():
    position = np.arange(N)
    angles = (position[:, None] * position[None, :] % N).astype(np.float32) * np.float32(
        2.0 * math.pi / N
    )
    factor = np.float32(1.0 / math.sqrt(N))
    cos, sin = (np.cos(angles) * factor).astype(BF), (np.sin(angles) * factor).astype(BF)
    late = (position + np.where(position % ROWS < 2, ROWS, 0)) % N
    return cos, sin, cos[late], sin[late]


def iota(shape, dim):
    return lax.broadcasted_iota(jnp.int32, shape, dim)


def split(v, size, count):
    quotient = sum((v >= size * n).astype(jnp.int32) for n in range(1, count))
    return quotient, v - quotient * size


def rows_of(ref, *dims):
    return jnp.concatenate([ref[where].astype(F32) for where in np.ndindex(*dims)], axis=0).astype(BF)


def doubled(block):
    zero = jnp.zeros_like(block)
    return jnp.concatenate(
        [jnp.concatenate([block, zero], axis=1), jnp.concatenate([zero, block], axis=1)], axis=0
    )


def kspace_weights(spot, lines, first, second, w1, w2, keep, follow):
    row = spot[0] * ROWS + iota((24, 128), 0)
    row = jnp.where(iota((24, 128), 0) >= ROWS + 4, row - 4, row)
    row = jnp.where(row >= N, row - N, row)
    for s in range(SLICES):
        hit = jnp.where(lines[s : s + 1, :] == row, 1.0, 0.0)
        hit = jnp.max(hit, axis=1, keepdims=True)
        keep[s] = hit[:ROWS]
        follow[s] = hit[ROWS:]
    whole = jnp.where(spot[0] == SPACE - 1, 0.0, 1.0)
    rest = iota((18, 128), 0)
    h_row = rest & 1
    p_row, q_row = split(rest >> 1, 3, 3)
    matrix = rows_of(first, 3, 3)
    lane = iota((18, 128), 1)
    late = lane >= 96
    rest = jnp.where(late, lane - 96, lane)
    q_lane = jnp.where(late, rest >> 3, rest >> 5)
    h_lane = jnp.where(late, (rest >> 2) & 1, (rest >> 4) & 1)
    row = jnp.where(late, ROWS + (rest & 3), rest & 15)
    hidden_row = jnp.where((h_row == h_lane) & (q_row == q_lane), row - p_row, -1)
    late = iota((CH, 128), 1) >= 96
    for r in range(HROWS):
        band = jnp.where(hidden_row == r, 1.0, 0.0).astype(BF)
        block = dot_tn(matrix, band)
        across = ~late if r + 1 >= ROWS else late
        block = jnp.where(across, block * whole, block)
        w1[r * CH : (r + 1) * CH, :] = block.astype(BF)
    line, lane = iota((96, 36), 0), iota((96, 36), 1)
    parity, rest = split(lane, 18, 2)
    o_lane = rest & 1
    p_lane, q_lane = split(rest >> 1, 3, 3)
    matrix = doubled(rows_of(second, 3, 3))
    place = line & 15
    place = jnp.where(place < 2, place + ROWS, place)
    match = (line >> 5 == q_lane) & ((line >> 4) & 1 == o_lane)
    pair_row = jnp.where(match, place + p_lane - 2 - parity, -1)
    late = (iota((96, 128), 0) & 15) < 2
    upper = iota((96, 128), 1) >= CH
    for pair in range(HROWS // 2):
        band = jnp.where(pair_row == 2 * pair, 1.0, 0.0).astype(BF)
        block = dot(band, matrix)
        beyond = 2 * pair + 1 + upper.astype(jnp.int32) >= ROWS
        block = jnp.where(late != beyond, block * whole, block)
        w2[:, pair * 128 : (pair + 1) * 128] = block.astype(BF)


def image_bands():
    first = np.zeros((6, 54, 144), np.float32)
    for x in range(6):
        for h in range(2):
            for a in range(3):
                for p in range(3):
                    for q in range(3):
                        first[x, a * 18 + p * 6 + q * 2 + h, a * 48 + q * 16 + (x + p) * 2 + h] = 1
    second = np.zeros((3, 72, 108), np.float32)
    for pair in range(3):
        for parity in range(2):
            for o in range(2):
                for a in range(3):
                    for q in range(3):
                        for e in range(4):
                            p = 2 * pair + parity - e
                            if 0 <= p < 3:
                                second[
                                    pair,
                                    a * 24 + q * 8 + o * 4 + e,
                                    parity * 54 + a * 18 + p * 6 + q * 2 + o,
                                ] = 1
    return first.astype(BF), second.astype(BF)


def dot(a, b):
    return jnp.dot(a, b, preferred_element_type=F32)


def dot_tn(a, b):
    return lax.dot_general(a, b, TN, preferred_element_type=F32)


def dot_nt(a, b):
    return lax.dot_general(a, b, NT, preferred_element_type=F32)


def before(v):
    lane = lax.broadcasted_iota(jnp.int32, v.shape, 1)
    return jnp.where(lane == 0, 0.0, pltpu.roll(v, 1, 1))


def after(v):
    lane = lax.broadcasted_iota(jnp.int32, v.shape, 1)
    return jnp.where(lane == N - 1, 0.0, pltpu.roll(v, N - 1, 1))


def blocks_swapped(tiles):
    tiles = list(tiles)
    group = lax.broadcasted_iota(jnp.int32, tiles[0].shape, 1) // 16
    for bit in (4, 2, 1):
        upper = (group & bit) != 0
        for i in range(8):
            if i & bit:
                continue
            a, b = tiles[i], tiles[i + bit]
            tiles[i] = jnp.where(upper, pltpu.roll(b, 16 * bit, 1), a)
            tiles[i + bit] = jnp.where(upper, b, pltpu.roll(a, 128 - 16 * bit, 1))
    return tiles


def wide(ref, *where):
    *lead, rows = where
    return jnp.concatenate([ref[(*lead, b, rows, slice(None))] for b in range(4)], axis=1)


def put(ref, value, *where):
    *lead, rows = where
    for b in range(4):
        ref[(*lead, b, rows, slice(None))] = value[:, b * 128 : (b + 1) * 128]


def regroup(received, left, coil):
    for octet in range(SPACE // 8):
        tiles = [
            received[octet * 8 + i, :, :, coil * 128 : (coil + 1) * 128]
            .astype(F32)
            .reshape(32, 128)
            for i in range(8)
        ]
        for s, tile in enumerate(blocks_swapped(tiles)):
            row = coil * 128 + s * 16
            tile = tile.astype(BF)
            for h in range(2):
                left[h, row : row + 16, octet * 128 : (octet + 1) * 128] = tile[
                    h * 16 : (h + 1) * 16
                ]


def pack_kernel(measured, sens, out, mine, maps, sems):
    copies = [
        pltpu.make_async_copy(source.at[:, :, :, pl.ds(0, 8), :], target, sems.at[n])
        for n, (source, target) in enumerate(((measured, mine), (sens, maps)))
    ]
    for copy in copies:
        copy.start()
    for copy in copies:
        copy.wait()
    for i in range(PAIRS):
        c, s = i // SLICES, i % SLICES
        out[i] = jnp.concatenate(
            [mine[c, h, s].astype(F32)[:4] for h in range(2)]
            + [maps[c, h, s].astype(F32)[:2] for h in range(2)],
            axis=0,
        ).astype(BF)


def kspace_kernel(
    measured, halo, keep, follow, w1, w2, far_cos, far_sin, out, refined, cos, sin, sems, *scratch
):
    tables = [
        pltpu.make_async_copy(source, target, sems.at[n])
        for n, (source, target) in enumerate(((far_cos, cos), (far_sin, sin)))
    ]
    for table in tables:
        table.start()

    def one(i, x3, hidden):
        c, s = i // SLICES, i % SLICES
        mask = keep[s] > 0
        own = jnp.concatenate(
            [jnp.where(mask, measured[c, h, s].astype(F32), 0.0) for h in range(2)], axis=0
        )
        rim = jnp.where(follow[s] > 0, halo[i].astype(F32)[0:8], 0.0)
        two = iota((8, N), 0) < 2
        held = jnp.concatenate(
            [
                jnp.where(two, rim, own[0:8]),
                own[8:16],
                jnp.where(two, pltpu.roll(rim, 4, 0), own[16:24]),
                own[24:32],
            ],
            axis=0,
        )
        x3[0:32] = before(own).astype(BF)
        x3[32:64] = own.astype(BF)
        x3[64:96] = after(own).astype(BF)
        x3[96:128] = jnp.concatenate(
            [before(rim), rim, after(rim), jnp.zeros_like(rim)], axis=0
        ).astype(BF)
        hidden[...] = jnp.maximum(dot(w1[...], x3[...]).astype(BF), 0)
        spread = dot(w2[...], hidden[...])
        total = held + before(spread[0:32]) + spread[32:64] + after(spread[64:96])
        total = total.astype(BF)
        row = pl.multiple_of(i * 16, 16)
        for h in range(2):
            refined[h, pl.ds(row, 16), :] = total[h * 16 : (h + 1) * 16]

    def step(i, carry):
        for k in range(UNROLL):
            one(i * UNROLL + k, scratch[2 * k], scratch[2 * k + 1])
        return carry

    lax.fori_loop(0, PAIRS // UNROLL, step, 0)
    for table in tables:
        table.wait()
    for part in range(2):
        rows = pl.ds(part * 256, 256)
        co, si = cos[rows, :], sin[rows, :]
        real = dot_nt(co, refined[0]) - dot_nt(si, refined[1])
        imag = dot_nt(si, refined[0]) + dot_nt(co, refined[1])
        out[part * 16 : (part + 1) * 16, 0] = real.astype(BF).reshape(16, 16, LANES)
        out[part * 16 : (part + 1) * 16, 1] = imag.astype(BF).reshape(16, 16, LANES)


def combine_kernel(spot, received, sens, halo, cos, sin, out, left, image, partial):
    for c in range(COILS):
        regroup(received, left, c)
        rows = slice(c * 128, (c + 1) * 128)
        image[c, 0] = dot(left[0, rows], cos[...]) - dot(left[1, rows], sin[...])
        image[c, 1] = dot(left[0, rows], sin[...]) + dot(left[1, rows], cos[...])
        for s in range(SLICES):
            rows = slice(s * 16, (s + 1) * 16)
            real, imag = image[c, 0, rows], image[c, 1, rows]
            extra = halo[c * SLICES + s].astype(F32)
            sr, si = (
                jnp.concatenate(
                    [extra[8 + 2 * h : 10 + 2 * h], sens[c, h, s].astype(F32)[2:]], axis=0
                )
                for h in range(2)
            )
            pr = sr * real + si * imag
            pi = sr * imag - si * real
            if c:
                pr = pr + wide(partial, 0, rows)
                pi = pi + wide(partial, 1, rows)
            put(partial, pr, 0, rows)
            put(partial, pi, 1, rows)
    turn = RING - spot[0] % RING
    for x in range(ROWS):
        place = (x + 2) % ROWS
        both = jnp.concatenate(
            [wide(partial, h, pl.ds(place, 8, stride=16)) for h in range(2)], axis=0
        )
        out[(x // 4 + turn) % RING, x % 4 * 16 : (x % 4 + 1) * 16] = both.astype(BF)


def outer(spot):
    quarter = (spot[0] + spot[1]) % RING
    first = jnp.where((spot[0] == 0) & (quarter == 0), 0.0, 1.0)
    last = jnp.where((spot[0] == SPACE - 1) & (quarter == RING - 1), 0.0, 1.0)
    return first, last


def image_weights(spot, first, second, band1, band2, w1, w2):
    edge = outer(spot)
    matrix = rows_of(first, 3, 3, 3)
    for x in range(6):
        block = dot_tn(matrix, band1[x])
        if x == 0:
            block = block * edge[0]
        if x == 5:
            block = block * edge[1]
        w1[x * CH : (x + 1) * CH, :] = block.astype(BF)
    matrix = doubled(rows_of(second, 3, 3, 3))
    for pair in range(3):
        w2[:, pair * 128 : (pair + 1) * 128] = dot(band2[pair], matrix).astype(BF)


def image_kernel(spot, previous, own, w1, w2, out, rows8, x3, acc, fin):
    edge = outer(spot)
    put(rows8, previous[0:32].astype(F32) * edge[0], slice(0, 32))
    put(rows8, previous[32:64].astype(F32), slice(32, 64))
    put(rows8, own[0:32].astype(F32), slice(64, 96))
    put(rows8, own[32:64].astype(F32) * edge[1], slice(96, 128))
    x3[0:48] = jnp.zeros((48, N), BF)
    x3[432:480] = jnp.zeros((48, N), BF)
    for s in range(SLICES):
        v = wide(rows8, pl.ds(s, 16, stride=8))
        base = (s + 1) * 48
        x3[base : base + 16] = before(v).astype(BF)
        x3[base + 16 : base + 32] = v.astype(BF)
        x3[base + 32 : base + 48] = after(v).astype(BF)
    acc[...] = jnp.zeros_like(acc)
    for t in range(SLICES):
        hidden = jnp.maximum(dot(w1[...], x3[t * 48 : t * 48 + 144]).astype(BF), 0)
        spread = dot(w2[...], hidden)
        for a in range(3):
            s = t + 1 - a
            if 0 <= s < SLICES:
                acc[s * 24 : (s + 1) * 24] = acc[s * 24 : (s + 1) * 24] + spread[a * 24 : (a + 1) * 24]
    for s in range(SLICES):
        v = acc[s * 24 : (s + 1) * 24]
        put(fin, before(v[0:8]) + v[8:16] + after(v[16:24]), slice(s * 8, (s + 1) * 8))
    for e in range(4):
        update = jnp.concatenate([wide(fin, pl.ds(o * 4 + e, 8, stride=8)) for o in range(2)], axis=0)
        value = (wide(rows8, slice(32 + e * 16, 48 + e * 16)) + update).astype(BF)
        for y in range(RING):
            out[y, e * 16 : (e + 1) * 16] = value


def expand_kernel(spot, gathered, sens, cos, sin, out, image_out, image, data):
    turn = RING - spot[0] % RING
    for x in range(ROWS):
        both = gathered[(x // 4 + turn) % RING, x % 4 * 16 : (x % 4 + 1) * 16].astype(F32)
        for h in range(2):
            put(image, both[h * 8 : (h + 1) * 8], h, pl.ds(x, 8, stride=16))
    for s in range(SLICES):
        rows = slice(s * 16, (s + 1) * 16)
        real, imag = wide(image, 0, rows), wide(image, 1, rows)
        image_out[0, s] = real.astype(BF)
        image_out[1, s] = imag.astype(BF)
        for c in range(COILS):
            sr, si = sens[c, 0, s].astype(F32), sens[c, 1, s].astype(F32)
            rows = slice(c * 128 + s * 16, c * 128 + (s + 1) * 16)
            data[0, rows] = (sr * real - si * imag).astype(BF)
            data[1, rows] = (sr * imag + si * real).astype(BF)
    for part in range(2):
        rows = pl.ds(part * 256, 256)
        co, si = cos[rows, :], sin[rows, :]
        real = dot_nt(co, data[0]) + dot_nt(si, data[1])
        imag = dot_nt(co, data[1]) - dot_nt(si, data[0])
        out[part * 16 : (part + 1) * 16, 0] = real.astype(BF).reshape(16, 16, LANES)
        out[part * 16 : (part + 1) * 16, 1] = imag.astype(BF).reshape(16, 16, LANES)


def finish_kernel(received, measured, keep, cos, sin, out, left):
    for c in range(COILS):
        regroup(received, left, c)
        rows = slice(c * 128, (c + 1) * 128)
        real = dot(left[0, rows], cos[...]) + dot(left[1, rows], sin[...])
        imag = dot(left[1, rows], cos[...]) - dot(left[0, rows], sin[...])
        for s in range(SLICES):
            mask = keep[s] > 0
            rows = slice(s * 16, (s + 1) * 16)
            for h, value in enumerate((real, imag)):
                out[c, h, s] = jnp.where(
                    mask, measured[c, h, s].astype(F32), value[rows]
                ).astype(BF)


def call(kernel, shapes, scratch, scalars, *operands, far=0):
    single = not isinstance(shapes, list)
    return pl.pallas_call(
        kernel,
        out_shape=shapes,
        in_specs=[SMEM] * scalars
        + [VMEM] * (len(operands) - scalars - far)
        + [pl.BlockSpec(memory_space=pl.ANY)] * far,
        out_specs=VMEM if single else [VMEM] * len(shapes),
        scratch_shapes=scratch,
        compiler_params=pltpu.CompilerParams(vmem_limit_bytes=40 * 1024 * 1024),
    )(*operands)


def spread(array, axis):
    return lax.all_to_all(array, axis, split_axis=0, concat_axis=0, tiled=True)


def arr(*shape, dtype=BF):
    return jax.ShapeDtypeStruct(shape, dtype)


def local(
    measured, sensitivity, sample_lines, kspace_first, kspace_second, image_first, image_second
):
    space, ring = lax.axis_index("space"), lax.axis_index("ring")
    cos, sin, lcos, lsin = (jnp.asarray(t) for t in dft_tables())
    iband1, iband2 = (jnp.asarray(t) for t in image_bands())

    spot = jnp.stack([space, ring])
    rim = pl.pallas_call(
        pack_kernel,
        out_shape=arr(PAIRS, 12, N),
        in_specs=[pl.BlockSpec(memory_space=pl.ANY)] * 2,
        out_specs=VMEM,
        scratch_shapes=[pltpu.VMEM((COILS, 2, SLICES, 8, N), BF)] * 2
        + [pltpu.SemaphoreType.DMA((2,))],
    )(measured, sensitivity)
    halo = lax.ppermute(rim, "space", [((i + 1) % SPACE, i) for i in range(SPACE)])

    kw1, kw2, keep, follow = call(
        kspace_weights,
        [
            arr(HROWS * CH, 128),
            arr(96, HROWS * CH),
            arr(SLICES, ROWS, 1, dtype=F32),
            arr(SLICES, 8, 1, dtype=F32),
        ],
        [],
        1,
        spot, sample_lines, kspace_first.transpose(2, 3, 1, 0), kspace_second.transpose(2, 3, 0, 1),
    )
    half_done = call(
        kspace_kernel,
        arr(SPACE, 2, ROWS, LANES),
        [
            pltpu.VMEM((2, LANES, N), BF),
            pltpu.VMEM((N, N), BF),
            pltpu.VMEM((N, N), BF),
            pltpu.SemaphoreType.DMA((2,)),
        ]
        + [pltpu.VMEM((128, N), BF), pltpu.VMEM((HROWS * CH, N), BF)] * UNROLL,
        0,
        measured, halo, keep, follow, kw1, kw2, lcos, lsin,
        far=2,
    )
    half_done = spread(half_done, "space")
    partial = call(
        combine_kernel,
        arr(RING, 64, N),
        [
            pltpu.VMEM((2, LANES, N), BF),
            pltpu.VMEM((COILS, 2, 128, N), F32),
            pltpu.VMEM((2, 4, 128, 128), F32),
        ],
        1,
        spot, half_done, sensitivity, halo, lcos, lsin,
    )
    part = spread(partial, "ring").astype(F32).sum(axis=0).astype(BF)

    def place(half, i):
        block, quarter = i // RING % SPACE, i % RING
        return (half * RING + (quarter - block) % RING) * SPACE + block

    axes = ("half", "ring", "space")
    count = RING * SPACE
    exchange = [(place(half, i), place(1 - half, i)) for half in range(HALVES) for i in range(count)]
    forward = [
        (place(half ^ (i % (8 * RING) == 8 * RING - 1), i), place(half, i + 1))
        for half in range(HALVES)
        for i in range(count)
    ]
    other = lax.ppermute(part, axes, exchange)
    image_in = (part.astype(F32) + other.astype(F32)).astype(BF)
    previous = lax.ppermute(image_in, axes, forward)
    iw1, iw2 = call(
        image_weights,
        [arr(6 * CH, 144), arr(72, 6 * CH)],
        [],
        1,
        spot, image_first.transpose(2, 3, 4, 1, 0), image_second.transpose(2, 3, 4, 0, 1), iband1, iband2,
    )
    copies = call(
        image_kernel,
        arr(RING, 64, N),
        [
            pltpu.VMEM((4, 128, 128), F32),
            pltpu.VMEM((480, N), BF),
            pltpu.VMEM((SLICES * 24, N), F32),
            pltpu.VMEM((4, SLICES * 8, 128), F32),
        ],
        1,
        spot, previous, image_in, iw1, iw2,
    )
    gathered = spread(copies, "ring")
    midway, image_out = call(
        expand_kernel,
        [arr(SPACE, 2, ROWS, LANES), arr(2, SLICES, ROWS, N)],
        [pltpu.VMEM((2, 4, 128, 128), F32), pltpu.VMEM((2, LANES, N), BF)],
        1,
        spot, gathered, sensitivity, cos, sin,
    )
    midway = spread(midway, "space")
    kspace_out = call(
        finish_kernel,
        arr(COILS, 2, SLICES, ROWS, N),
        [pltpu.VMEM((2, LANES, N), BF)],
        0,
        midway, measured, keep, cos, sin,
    )
    return kspace_out, image_out


def solution(mesh):
    mesh = Mesh(mesh.devices.reshape(HALVES, RING, SPACE), ("half", "ring", "space"))
    placed = P(("half", "ring"), None, None, "space", None)
    return jax.shard_map(
        local,
        mesh=mesh,
        in_specs=(placed, placed, P(), P(), P(), P(), P()),
        out_specs=(placed, P(None, None, "space", None)),
        check_vma=False,
    )
```

```python
import math

import jax
import jax.numpy as jnp
import numpy as np
from jax import lax
from jax.experimental import pallas as pl
from jax.experimental.pallas import tpu as pltpu
from jax.sharding import Mesh
from jax.sharding import PartitionSpec as P

N = 512
COILS = 2
SLICES = 8
ROWS = 16
CH = 64
SPACE = 32
RING = 4
HALVES = 2
PAIRS = COILS * SLICES
LANES = PAIRS * ROWS
MIB = 1024 * 1024
HROWS = ROWS + 2
UNROLL = 8
BF = jnp.bfloat16
F32 = jnp.float32
VMEM = pl.BlockSpec(memory_space=pltpu.VMEM)
HBM = pl.BlockSpec(memory_space=pltpu.HBM)
NT = (((1,), (1,)), ((), ()))
TN = (((0,), (0,)), ((), ()))


def dft_tables():
    position = np.arange(N)
    angles = (position[:, None] * position[None, :] % N).astype(np.float32) * np.float32(
        2.0 * math.pi / N
    )
    factor = np.float32(1.0 / math.sqrt(N))
    cos, sin = (np.cos(angles) * factor).astype(BF), (np.sin(angles) * factor).astype(BF)
    late = (position + np.where(position % ROWS < 2, ROWS, 0)) % N
    plain = np.stack([cos, sin])
    return plain, plain[:, late]


def iota(shape, dim):
    return lax.broadcasted_iota(jnp.int32, shape, dim)


def split(v, size, count):
    quotient = sum((v >= size * n).astype(jnp.int32) for n in range(1, count))
    return quotient, v - quotient * size


def rows_of(ref, *dims):
    return jnp.concatenate([ref[where].astype(F32) for where in np.ndindex(*dims)], axis=0).astype(BF)


def doubled(block):
    zero = jnp.zeros_like(block)
    return jnp.concatenate(
        [jnp.concatenate([block, zero], axis=1), jnp.concatenate([zero, block], axis=1)], axis=0
    )


def kspace_weights(lines, first, second, table, w1, w2, keep, follow):
    space = lax.axis_index("space")
    row = space * ROWS + iota((24, 128), 0)
    row = jnp.where(iota((24, 128), 0) >= ROWS + 4, row - 4, row)
    row = jnp.where(row >= N, row - N, row)
    for s in range(SLICES):
        hit = jnp.where(lines[s : s + 1, :] == row, 1.0, 0.0)
        hit = jnp.max(hit, axis=1, keepdims=True)
        keep[s] = hit[:ROWS]
        follow[s] = hit[ROWS:]
    whole = jnp.where(space == SPACE - 1, 0.0, 1.0)
    rest = iota((18, 128), 0)
    h_row = rest & 1
    p_row, q_row = split(rest >> 1, 3, 3)
    matrix = rows_of(first, 3, 3)
    lane = iota((18, 128), 1)
    late = lane >= 96
    rest = jnp.where(late, lane - 96, lane)
    q_lane = jnp.where(late, rest >> 3, rest >> 5)
    h_lane = jnp.where(late, (rest >> 2) & 1, (rest >> 4) & 1)
    row = jnp.where(late, ROWS + (rest & 3), rest & 15)
    hidden_row = jnp.where((h_row == h_lane) & (q_row == q_lane), row - p_row, -1)
    late = iota((CH, 128), 1) >= 96
    for r in range(HROWS):
        band = jnp.where(hidden_row == r, 1.0, 0.0).astype(BF)
        block = dot_tn(matrix, band)
        across = ~late if r + 1 >= ROWS else late
        block = jnp.where(across, block * whole, block)
        w1[r * CH : (r + 1) * CH, :] = block.astype(BF)
    line, lane = iota((96, 36), 0), iota((96, 36), 1)
    parity, rest = split(lane, 18, 2)
    o_lane = rest & 1
    p_lane, q_lane = split(rest >> 1, 3, 3)
    matrix = doubled(rows_of(second, 3, 3))
    place = line & 15
    place = jnp.where(place < 2, place + ROWS, place)
    match = (line >> 5 == q_lane) & ((line >> 4) & 1 == o_lane)
    pair_row = jnp.where(match, place + p_lane - 2 - parity, -1)
    late = (iota((96, 128), 0) & 15) < 2
    upper = iota((96, 128), 1) >= CH
    for pair in range(HROWS // 2):
        band = jnp.where(pair_row == 2 * pair, 1.0, 0.0).astype(BF)
        block = dot(band, matrix)
        beyond = 2 * pair + 1 + upper.astype(jnp.int32) >= ROWS
        block = jnp.where(late != beyond, block * whole, block)
        w2[:, pair * 128 : (pair + 1) * 128] = block.astype(BF)


def image_bands():
    first = np.zeros((6, 54, 144), np.float32)
    for x in range(6):
        for h in range(2):
            for a in range(3):
                for p in range(3):
                    for q in range(3):
                        first[x, a * 18 + p * 6 + q * 2 + h, a * 48 + q * 16 + (x + p) * 2 + h] = 1
    second = np.zeros((3, 72, 108), np.float32)
    for pair in range(3):
        for parity in range(2):
            for o in range(2):
                for a in range(3):
                    for q in range(3):
                        for e in range(4):
                            p = 2 * pair + parity - e
                            if 0 <= p < 3:
                                second[
                                    pair,
                                    a * 24 + q * 8 + o * 4 + e,
                                    parity * 54 + a * 18 + p * 6 + q * 2 + o,
                                ] = 1
    return first.astype(BF), second.astype(BF)


def dot(a, b):
    return jnp.dot(a, b, preferred_element_type=F32)


def dot_tn(a, b):
    return lax.dot_general(a, b, TN, preferred_element_type=F32)


def dot_nt(a, b):
    return lax.dot_general(a, b, NT, preferred_element_type=F32)


def before(v):
    lane = lax.broadcasted_iota(jnp.int32, v.shape, 1)
    return jnp.where(lane == 0, 0.0, pltpu.roll(v, 1, 1))


def after(v):
    lane = lax.broadcasted_iota(jnp.int32, v.shape, 1)
    return jnp.where(lane == N - 1, 0.0, pltpu.roll(v, N - 1, 1))


def blocks_swapped(tiles):
    tiles = list(tiles)
    group = lax.broadcasted_iota(jnp.int32, tiles[0].shape, 1) // 16
    for bit in (4, 2, 1):
        upper = (group & bit) != 0
        for i in range(8):
            if i & bit:
                continue
            a, b = tiles[i], tiles[i + bit]
            tiles[i] = jnp.where(upper, pltpu.roll(b, 16 * bit, 1), a)
            tiles[i + bit] = jnp.where(upper, b, pltpu.roll(a, 128 - 16 * bit, 1))
    return tiles


def wide(ref, *where):
    *lead, rows = where
    return jnp.concatenate([ref[(*lead, b, rows, slice(None))] for b in range(4)], axis=1)


def put(ref, value, *where):
    *lead, rows = where
    for b in range(4):
        ref[(*lead, b, rows, slice(None))] = value[:, b * 128 : (b + 1) * 128]


def regroup(received, left, coil):
    for octet in range(SPACE // 8):
        tiles = [
            received[octet * 8 + i, :, :, coil * 128 : (coil + 1) * 128]
            .astype(F32)
            .reshape(32, 128)
            for i in range(8)
        ]
        for s, tile in enumerate(blocks_swapped(tiles)):
            row = coil * 128 + s * 16
            tile = tile.astype(BF)
            for h in range(2):
                left[h, row : row + 16, octet * 128 : (octet + 1) * 128] = tile[
                    h * 16 : (h + 1) * 16
                ]


def pack_kernel(measured, sens, out, mine, maps, sems):
    copies = [
        pltpu.make_async_copy(source.at[:, :, :, pl.ds(0, 8), :], target, sems.at[n])
        for n, (source, target) in enumerate(((measured, mine), (sens, maps)))
    ]
    for copy in copies:
        copy.start()
    for copy in copies:
        copy.wait()
    for i in range(PAIRS):
        c, s = i // SLICES, i % SLICES
        out[i] = jnp.concatenate(
            [mine[c, h, s].astype(F32)[:4] for h in range(2)]
            + [maps[c, h, s].astype(F32)[:2] for h in range(2)],
            axis=0,
        ).astype(BF)


def kspace_kernel(measured, halo, keep, follow, w1, w2, table, out, refined, *scratch):
    cos, sin = table.at[0], table.at[1]

    def one(i, x3, hidden):
        c, s = i // SLICES, i % SLICES
        mask = keep[s] > 0
        own = jnp.concatenate(
            [jnp.where(mask, measured[c, h, s].astype(F32), 0.0) for h in range(2)], axis=0
        )
        rim = jnp.where(follow[s] > 0, halo[i].astype(F32)[0:8], 0.0)
        two = iota((8, N), 0) < 2
        held = jnp.concatenate(
            [
                jnp.where(two, rim, own[0:8]),
                own[8:16],
                jnp.where(two, pltpu.roll(rim, 4, 0), own[16:24]),
                own[24:32],
            ],
            axis=0,
        )
        x3[0:32] = before(own).astype(BF)
        x3[32:64] = own.astype(BF)
        x3[64:96] = after(own).astype(BF)
        x3[96:128] = jnp.concatenate(
            [before(rim), rim, after(rim), jnp.zeros_like(rim)], axis=0
        ).astype(BF)
        hidden[...] = jnp.maximum(dot(w1[...], x3[...]).astype(BF), 0)
        spread = dot(w2[...], hidden[...])
        total = held + before(spread[0:32]) + spread[32:64] + after(spread[64:96])
        total = total.astype(BF)
        row = pl.multiple_of(i * 16, 16)
        for h in range(2):
            refined[h, pl.ds(row, 16), :] = total[h * 16 : (h + 1) * 16]

    def step(i, carry):
        for k in range(UNROLL):
            one(i * UNROLL + k, scratch[2 * k], scratch[2 * k + 1])
        return carry

    lax.fori_loop(0, PAIRS // UNROLL, step, 0)
    for part in range(2):
        rows = pl.ds(part * 256, 256)
        co, si = cos[rows, :], sin[rows, :]
        real = dot_nt(co, refined[0]) - dot_nt(si, refined[1])
        imag = dot_nt(si, refined[0]) + dot_nt(co, refined[1])
        out[part * 16 : (part + 1) * 16, 0] = real.astype(BF).reshape(16, 16, LANES)
        out[part * 16 : (part + 1) * 16, 1] = imag.astype(BF).reshape(16, 16, LANES)


def combine_kernel(received, sens, halo, table, out, left, image, partial):
    cos, sin = table.at[0], table.at[1]
    for c in range(COILS):
        regroup(received, left, c)
        rows = slice(c * 128, (c + 1) * 128)
        image[c, 0] = dot(left[0, rows], cos[...]) - dot(left[1, rows], sin[...])
        image[c, 1] = dot(left[0, rows], sin[...]) + dot(left[1, rows], cos[...])
        for s in range(SLICES):
            rows = slice(s * 16, (s + 1) * 16)
            real, imag = image[c, 0, rows], image[c, 1, rows]
            extra = halo[c * SLICES + s].astype(F32)
            sr, si = (
                jnp.concatenate(
                    [extra[8 + 2 * h : 10 + 2 * h], sens[c, h, s].astype(F32)[2:]], axis=0
                )
                for h in range(2)
            )
            pr = sr * real + si * imag
            pi = sr * imag - si * real
            if c:
                pr = pr + wide(partial, 0, rows)
                pi = pi + wide(partial, 1, rows)
            put(partial, pr, 0, rows)
            put(partial, pi, 1, rows)
    turn = RING - lax.axis_index("space") % RING
    for x in range(ROWS):
        place = (x + 2) % ROWS
        both = jnp.concatenate(
            [wide(partial, h, pl.ds(place, 8, stride=16)) for h in range(2)], axis=0
        )
        out[(x // 4 + turn) % RING, x % 4 * 16 : (x % 4 + 1) * 16] = both.astype(BF)


def outer():
    space = lax.axis_index("space")
    quarter = (space + lax.axis_index("ring")) % RING
    first = jnp.where((space == 0) & (quarter == 0), 0.0, 1.0)
    last = jnp.where((space == SPACE - 1) & (quarter == RING - 1), 0.0, 1.0)
    return first, last


def image_weights(first, second, band1, band2, w1, w2):
    edge = outer()
    matrix = rows_of(first, 3, 3, 3)
    for x in range(6):
        block = dot_tn(matrix, band1[x])
        if x == 0:
            block = block * edge[0]
        if x == 5:
            block = block * edge[1]
        w1[x * CH : (x + 1) * CH, :] = block.astype(BF)
    matrix = doubled(rows_of(second, 3, 3, 3))
    for pair in range(3):
        w2[:, pair * 128 : (pair + 1) * 128] = dot(band2[pair], matrix).astype(BF)


def image_kernel(previous, own, w1, w2, out, rows8, x3, acc, fin):
    edge = outer()
    put(rows8, previous[0:32].astype(F32) * edge[0], slice(0, 32))
    put(rows8, previous[32:64].astype(F32), slice(32, 64))
    put(rows8, own[0:32].astype(F32), slice(64, 96))
    put(rows8, own[32:64].astype(F32) * edge[1], slice(96, 128))
    x3[0:48] = jnp.zeros((48, N), BF)
    x3[432:480] = jnp.zeros((48, N), BF)
    for s in range(SLICES):
        v = wide(rows8, pl.ds(s, 16, stride=8))
        base = (s + 1) * 48
        x3[base : base + 16] = before(v).astype(BF)
        x3[base + 16 : base + 32] = v.astype(BF)
        x3[base + 32 : base + 48] = after(v).astype(BF)
    acc[...] = jnp.zeros_like(acc)
    for t in range(SLICES):
        hidden = jnp.maximum(dot(w1[...], x3[t * 48 : t * 48 + 144]).astype(BF), 0)
        spread = dot(w2[...], hidden)
        for a in range(3):
            s = t + 1 - a
            if 0 <= s < SLICES:
                acc[s * 24 : (s + 1) * 24] = acc[s * 24 : (s + 1) * 24] + spread[a * 24 : (a + 1) * 24]
    for s in range(SLICES):
        v = acc[s * 24 : (s + 1) * 24]
        put(fin, before(v[0:8]) + v[8:16] + after(v[16:24]), slice(s * 8, (s + 1) * 8))
    for e in range(4):
        update = jnp.concatenate([wide(fin, pl.ds(o * 4 + e, 8, stride=8)) for o in range(2)], axis=0)
        value = (wide(rows8, slice(32 + e * 16, 48 + e * 16)) + update).astype(BF)
        for y in range(RING):
            out[y, e * 16 : (e + 1) * 16] = value


def expand_kernel(gathered, sens, table, out, image_out, image, data):
    cos, sin = table.at[0], table.at[1]
    turn = RING - lax.axis_index("space") % RING
    for x in range(ROWS):
        both = gathered[(x // 4 + turn) % RING, x % 4 * 16 : (x % 4 + 1) * 16].astype(F32)
        for h in range(2):
            put(image, both[h * 8 : (h + 1) * 8], h, pl.ds(x, 8, stride=16))
    for s in range(SLICES):
        rows = slice(s * 16, (s + 1) * 16)
        real, imag = wide(image, 0, rows), wide(image, 1, rows)
        image_out[0, s] = real.astype(BF)
        image_out[1, s] = imag.astype(BF)
        for c in range(COILS):
            sr, si = sens[c, 0, s].astype(F32), sens[c, 1, s].astype(F32)
            rows = slice(c * 128 + s * 16, c * 128 + (s + 1) * 16)
            data[0, rows] = (sr * real - si * imag).astype(BF)
            data[1, rows] = (sr * imag + si * real).astype(BF)
    for part in range(2):
        rows = pl.ds(part * 256, 256)
        co, si = cos[rows, :], sin[rows, :]
        real = dot_nt(co, data[0]) + dot_nt(si, data[1])
        imag = dot_nt(co, data[1]) - dot_nt(si, data[0])
        out[part * 16 : (part + 1) * 16, 0] = real.astype(BF).reshape(16, 16, LANES)
        out[part * 16 : (part + 1) * 16, 1] = imag.astype(BF).reshape(16, 16, LANES)


def finish_kernel(received, measured, keep, table, out, left):
    cos, sin = table.at[0], table.at[1]
    for c in range(COILS):
        regroup(received, left, c)
        rows = slice(c * 128, (c + 1) * 128)
        real = dot(left[0, rows], cos[...]) + dot(left[1, rows], sin[...])
        imag = dot(left[1, rows], cos[...]) - dot(left[0, rows], sin[...])
        for s in range(SLICES):
            mask = keep[s] > 0
            rows = slice(s * 16, (s + 1) * 16)
            for h, value in enumerate((real, imag)):
                out[c, h, s] = jnp.where(
                    mask, measured[c, h, s].astype(F32), value[rows]
                ).astype(BF)


def call(kernel, shapes, scratch, *operands, mib=12):
    single = not isinstance(shapes, list)
    return pl.pallas_call(
        kernel,
        out_shape=shapes,
        in_specs=[VMEM] * len(operands),
        out_specs=VMEM if single else [VMEM] * len(shapes),
        scratch_shapes=scratch,
        compiler_params=pltpu.CompilerParams(vmem_limit_bytes=mib * MIB),
    )(*operands)


def spread(array, axis):
    return lax.all_to_all(array, axis, split_axis=0, concat_axis=0, tiled=True)


def arr(*shape, dtype=BF):
    return jax.ShapeDtypeStruct(shape, dtype)


def local(
    measured, sensitivity, sample_lines, kspace_first, kspace_second, image_first, image_second
):
    plain, late = (jnp.asarray(t) for t in dft_tables())
    iband1, iband2 = (jnp.asarray(t) for t in image_bands())

    rim = pl.pallas_call(
        pack_kernel,
        out_shape=arr(PAIRS, 12, N),
        in_specs=[HBM] * 2,
        out_specs=VMEM,
        scratch_shapes=[pltpu.VMEM((COILS, 2, SLICES, 8, N), BF)] * 2
        + [pltpu.SemaphoreType.DMA((2,))],
    )(measured, sensitivity)
    halo = lax.ppermute(rim, "space", [((i + 1) % SPACE, i) for i in range(SPACE)])

    kw1, kw2, keep, follow = call(
        kspace_weights,
        [
            arr(HROWS * CH, 128),
            arr(96, HROWS * CH),
            arr(SLICES, ROWS, 1, dtype=F32),
            arr(SLICES, 8, 1, dtype=F32),
        ],
        [],
        sample_lines, kspace_first.transpose(2, 3, 1, 0), kspace_second.transpose(2, 3, 0, 1), late,
    )
    half_done = call(
        kspace_kernel,
        arr(SPACE, 2, ROWS, LANES),
        [
            pltpu.VMEM((2, LANES, N), BF),
        ]
        + [pltpu.VMEM((128, N), BF), pltpu.VMEM((HROWS * CH, N), BF)] * UNROLL,
        measured, halo, keep, follow, kw1, kw2, late,
        mib=28,
    )
    half_done = spread(half_done, "space")
    partial = call(
        combine_kernel,
        arr(RING, 64, N),
        [
            pltpu.VMEM((2, LANES, N), BF),
            pltpu.VMEM((COILS, 2, 128, N), F32),
            pltpu.VMEM((2, 4, 128, 128), F32),
        ],
        half_done, sensitivity, halo, late,
    )
    part = spread(partial, "ring").astype(F32).sum(axis=0).astype(BF)

    def place(half, i):
        block, quarter = i // RING % SPACE, i % RING
        return (half * RING + (quarter - block) % RING) * SPACE + block

    axes = ("half", "ring", "space")
    count = RING * SPACE
    exchange = [(place(half, i), place(1 - half, i)) for half in range(HALVES) for i in range(count)]
    forward = [
        (place(half ^ (i % (8 * RING) == 8 * RING - 1), i), place(half, i + 1))
        for half in range(HALVES)
        for i in range(count)
    ]
    other = lax.ppermute(part, axes, exchange)
    image_in = (part.astype(F32) + other.astype(F32)).astype(BF)
    previous = lax.ppermute(image_in, axes, forward)
    iw1, iw2 = call(
        image_weights,
        [arr(6 * CH, 144), arr(72, 6 * CH)],
        [],
        image_first.transpose(2, 3, 4, 1, 0), image_second.transpose(2, 3, 4, 0, 1), iband1, iband2,
    )
    copies = call(
        image_kernel,
        arr(RING, 64, N),
        [
            pltpu.VMEM((4, 128, 128), F32),
            pltpu.VMEM((480, N), BF),
            pltpu.VMEM((SLICES * 24, N), F32),
            pltpu.VMEM((4, SLICES * 8, 128), F32),
        ],
        previous, image_in, iw1, iw2,
    )
    gathered = spread(copies, "ring")
    midway, image_out = call(
        expand_kernel,
        [arr(SPACE, 2, ROWS, LANES), arr(2, SLICES, ROWS, N)],
        [pltpu.VMEM((2, 4, 128, 128), F32), pltpu.VMEM((2, LANES, N), BF)],
        gathered, sensitivity, plain,
    )
    midway = spread(midway, "space")
    kspace_out = call(
        finish_kernel,
        arr(COILS, 2, SLICES, ROWS, N),
        [pltpu.VMEM((2, LANES, N), BF)],
        midway, measured, keep, plain,
    )
    return kspace_out, image_out


def solution(mesh):
    mesh = Mesh(mesh.devices.reshape(HALVES, RING, SPACE), ("half", "ring", "space"))
    placed = P(("half", "ring"), None, None, "space", None)
    return jax.shard_map(
        local,
        mesh=mesh,
        in_specs=(placed, placed, P(), P(), P(), P(), P()),
        out_specs=(placed, P(None, None, "space", None)),
        check_vma=False,
    )
```

```python
import math

import jax
import jax.numpy as jnp
import numpy as np
from jax import lax
from jax.experimental import pallas as pl
from jax.experimental.pallas import tpu as pltpu
from jax.sharding import Mesh
from jax.sharding import PartitionSpec as P

N = 512
COILS = 2
SLICES = 8
ROWS = 16
CH = 64
SPACE = 32
RING = 4
HALVES = 2
PAIRS = COILS * SLICES
LANES = PAIRS * ROWS
MIB = 1024 * 1024
HROWS = ROWS + 2
EARLY = 14
UNROLL = 8
BF = jnp.bfloat16
F32 = jnp.float32
VMEM = pl.BlockSpec(memory_space=pltpu.VMEM)
HBM = pl.BlockSpec(memory_space=pltpu.HBM)
NT = (((1,), (1,)), ((), ()))
TN = (((0,), (0,)), ((), ()))


def dft_tables():
    position = np.arange(N)
    angles = (position[:, None] * position[None, :] % N).astype(np.float32) * np.float32(
        2.0 * math.pi / N
    )
    factor = np.float32(1.0 / math.sqrt(N))
    cos, sin = (np.cos(angles) * factor).astype(BF), (np.sin(angles) * factor).astype(BF)
    late = (position + np.where(position % ROWS < 2, ROWS, 0)) % N
    plain = np.stack([cos, sin])
    return plain, plain[:, late]


def iota(shape, dim):
    return lax.broadcasted_iota(jnp.int32, shape, dim)


def split(v, size, count):
    quotient = sum((v >= size * n).astype(jnp.int32) for n in range(1, count))
    return quotient, v - quotient * size


def rows_of(ref, *dims):
    return jnp.concatenate([ref[where].astype(F32) for where in np.ndindex(*dims)], axis=0).astype(BF)


def doubled(block):
    zero = jnp.zeros_like(block)
    return jnp.concatenate(
        [jnp.concatenate([block, zero], axis=1), jnp.concatenate([zero, block], axis=1)], axis=0
    )


def start_kernel(
    far_measured, far_sens, far_lines, far_first, far_second,
    rim, measured, w1, w2, w2b, keep, follow, sens, lines, first, second, sems,
):
    rows = pl.ds(0, 8)
    copies = [
        pltpu.make_async_copy(source, target, sems.at[n])
        for n, (source, target) in enumerate(
            (
                (far_measured, measured),
                (far_sens.at[:, :, :, rows, :], sens),
                (far_lines, lines),
                (far_first, first),
                (far_second, second),
            )
        )
    ]
    for copy in copies:
        copy.start()
    for copy in copies:
        copy.wait()
    for i in range(PAIRS):
        c, s = i // SLICES, i % SLICES
        rim[i] = jnp.concatenate(
            [measured[c, h, s].astype(F32)[:4] for h in range(2)]
            + [sens[c, h, s].astype(F32)[:2] for h in range(2)],
            axis=0,
        ).astype(BF)
    space = lax.axis_index("space")
    row = space * ROWS + iota((24, 128), 0)
    row = jnp.where(iota((24, 128), 0) >= ROWS + 4, row - 4, row)
    row = jnp.where(row >= N, row - N, row)
    for s in range(SLICES):
        hit = jnp.where(lines[s : s + 1, :] == row, 1.0, 0.0)
        hit = jnp.max(hit, axis=1, keepdims=True)
        keep[s] = hit[:ROWS]
        follow[s] = hit[ROWS:]
    whole = jnp.where(space == SPACE - 1, 0.0, 1.0)
    rest = iota((18, 128), 0)
    h_row = rest & 1
    p_row, q_row = split(rest >> 1, 3, 3)
    matrix = rows_of(first, 3, 3)
    lane = iota((18, 128), 1)
    late = lane >= 96
    rest = jnp.where(late, lane - 96, lane)
    q_lane = jnp.where(late, rest >> 3, rest >> 5)
    h_lane = jnp.where(late, (rest >> 2) & 1, (rest >> 4) & 1)
    row = jnp.where(late, ROWS + (rest & 3), rest & 15)
    hidden_row = jnp.where((h_row == h_lane) & (q_row == q_lane), row - p_row, -1)
    late = iota((CH, 128), 1) >= 96
    for r in range(HROWS):
        band = jnp.where(hidden_row == r, 1.0, 0.0).astype(BF)
        block = dot_tn(matrix, band)
        across = ~late if r + 1 >= ROWS else late
        block = jnp.where(across, block * whole, block)
        w1[r * CH : (r + 1) * CH, :] = block.astype(BF)
    matrix = doubled(rows_of(second, 3, 3))
    place = iota((96, 36), 0) & 15
    place = jnp.where(place < 2, place + ROWS, place)
    band = second_band(place, 5)
    for pair in range(EARLY // 2):
        block = dot(jnp.where(band == 2 * pair, 1.0, 0.0).astype(BF), matrix)
        w2[:, pair * 128 : (pair + 1) * 128] = block.astype(BF)
    place = iota((48, 36), 0) & 7
    place = jnp.where(place < 2, place + ROWS, jnp.where(place >= 6, place + 8, -64))
    band = second_band(place, 4)
    late = (iota((48, 128), 0) & 7) < 2
    upper = iota((48, 128), 1) >= CH
    for pair in range(EARLY // 2, HROWS // 2):
        block = dot(jnp.where(band == 2 * pair, 1.0, 0.0).astype(BF), matrix)
        beyond = 2 * pair + 1 + upper.astype(jnp.int32) >= ROWS
        block = jnp.where(late != beyond, block * whole, block)
        start = pair * 128 - EARLY * CH
        w2b[:, start : start + 128] = block.astype(BF)


def second_band(place, shift):
    line, lane = iota(place.shape, 0), iota(place.shape, 1)
    parity, rest = split(lane, 18, 2)
    o_lane = rest & 1
    p_lane, q_lane = split(rest >> 1, 3, 3)
    match = (line >> shift == q_lane) & ((line >> (shift - 1)) & 1 == o_lane)
    return jnp.where(match, place + p_lane - 2 - parity, -1)


def image_bands():
    first = np.zeros((6, 54, 144), np.float32)
    for x in range(6):
        for h in range(2):
            for a in range(3):
                for p in range(3):
                    for q in range(3):
                        first[x, a * 18 + p * 6 + q * 2 + h, a * 48 + q * 16 + (x + p) * 2 + h] = 1
    second = np.zeros((3, 72, 108), np.float32)
    for pair in range(3):
        for parity in range(2):
            for o in range(2):
                for a in range(3):
                    for q in range(3):
                        for e in range(4):
                            p = 2 * pair + parity - e
                            if 0 <= p < 3:
                                second[
                                    pair,
                                    a * 24 + q * 8 + o * 4 + e,
                                    parity * 54 + a * 18 + p * 6 + q * 2 + o,
                                ] = 1
    return first.astype(BF), second.astype(BF)


def dot(a, b):
    return jnp.dot(a, b, preferred_element_type=F32)


def dot_tn(a, b):
    return lax.dot_general(a, b, TN, preferred_element_type=F32)


def dot_nt(a, b):
    return lax.dot_general(a, b, NT, preferred_element_type=F32)


def before(v):
    lane = lax.broadcasted_iota(jnp.int32, v.shape, 1)
    return jnp.where(lane == 0, 0.0, pltpu.roll(v, 1, 1))


def after(v):
    lane = lax.broadcasted_iota(jnp.int32, v.shape, 1)
    return jnp.where(lane == N - 1, 0.0, pltpu.roll(v, N - 1, 1))


def blocks_swapped(tiles):
    tiles = list(tiles)
    group = lax.broadcasted_iota(jnp.int32, tiles[0].shape, 1) // 16
    for bit in (4, 2, 1):
        upper = (group & bit) != 0
        for i in range(8):
            if i & bit:
                continue
            a, b = tiles[i], tiles[i + bit]
            tiles[i] = jnp.where(upper, pltpu.roll(b, 16 * bit, 1), a)
            tiles[i + bit] = jnp.where(upper, b, pltpu.roll(a, 128 - 16 * bit, 1))
    return tiles


def wide(ref, *where):
    *lead, rows = where
    return jnp.concatenate([ref[(*lead, b, rows, slice(None))] for b in range(4)], axis=1)


def put(ref, value, *where):
    *lead, rows = where
    for b in range(4):
        ref[(*lead, b, rows, slice(None))] = value[:, b * 128 : (b + 1) * 128]


def regroup(received, left, coil):
    for octet in range(SPACE // 8):
        tiles = [
            received[octet * 8 + i, :, :, coil * 128 : (coil + 1) * 128]
            .astype(F32)
            .reshape(32, 128)
            for i in range(8)
        ]
        for s, tile in enumerate(blocks_swapped(tiles)):
            row = coil * 128 + s * 16
            tile = tile.astype(BF)
            for h in range(2):
                left[h, row : row + 16, octet * 128 : (octet + 1) * 128] = tile[
                    h * 16 : (h + 1) * 16
                ]


def unrolled(one):
    def step(i, carry):
        for k in range(UNROLL):
            one(i * UNROLL + k, k)
        return carry

    lax.fori_loop(0, PAIRS // UNROLL, step, 0)


def early_kernel(measured, keep, w1, w2, table, patches, total):
    def one(i, k):
        c, s = i // SLICES, i % SLICES
        mask = keep[s] > 0
        own = jnp.concatenate(
            [jnp.where(mask, measured[c, h, s].astype(F32), 0.0) for h in range(2)], axis=0
        )
        shifted = jnp.concatenate([before(own), own, after(own)], axis=0).astype(BF)
        patches[i] = shifted
        hidden = jnp.maximum(dot(w1[: EARLY * CH, :96], shifted).astype(BF), 0)
        spread = dot(w2[...], hidden)
        total[i] = own + before(spread[0:32]) + spread[32:64] + after(spread[64:96])

    unrolled(one)


def late_kernel(patches, total, halo, follow, w1, w2, table, out, refined, *scratch):
    cos, sin = table.at[0], table.at[1]

    def one(i, k):
        x3 = scratch[k]
        s = i % SLICES
        rim = jnp.where(follow[s] > 0, halo[i].astype(F32)[0:8], 0.0)
        x3[0:96] = patches[i]
        x3[96:128] = jnp.concatenate(
            [before(rim), rim, after(rim), jnp.zeros_like(rim)], axis=0
        ).astype(BF)
        hidden = jnp.maximum(dot(w1[EARLY * CH :], x3[...]).astype(BF), 0)
        spread = dot(w2[...], hidden)
        more = before(spread[0:16]) + spread[16:32] + after(spread[32:48])
        line = iota((8, N), 0)
        row = pl.multiple_of(i * 16, 16)
        for h in range(2):
            extra = more[h * 8 : (h + 1) * 8]
            rows = rim if h == 0 else pltpu.roll(rim, 4, 0)
            done = total[i, h * 16 : (h + 1) * 16]
            done = jnp.concatenate(
                [
                    jnp.where(line < 2, rows + extra, done[0:8]),
                    jnp.where(line >= 6, done[8:16] + extra, done[8:16]),
                ],
                axis=0,
            )
            refined[h, pl.ds(row, 16), :] = done.astype(BF)

    unrolled(one)
    for part in range(2):
        rows = pl.ds(part * 256, 256)
        co, si = cos[rows, :], sin[rows, :]
        real = dot_nt(co, refined[0]) - dot_nt(si, refined[1])
        imag = dot_nt(si, refined[0]) + dot_nt(co, refined[1])
        out[part * 16 : (part + 1) * 16, 0] = real.astype(BF).reshape(16, 16, LANES)
        out[part * 16 : (part + 1) * 16, 1] = imag.astype(BF).reshape(16, 16, LANES)


def combine_kernel(received, sens, halo, table, out, left, image, partial):
    cos, sin = table.at[0], table.at[1]
    for c in range(COILS):
        regroup(received, left, c)
        rows = slice(c * 128, (c + 1) * 128)
        image[c, 0] = dot(left[0, rows], cos[...]) - dot(left[1, rows], sin[...])
        image[c, 1] = dot(left[0, rows], sin[...]) + dot(left[1, rows], cos[...])
        for s in range(SLICES):
            rows = slice(s * 16, (s + 1) * 16)
            real, imag = image[c, 0, rows], image[c, 1, rows]
            extra = halo[c * SLICES + s].astype(F32)
            sr, si = (
                jnp.concatenate(
                    [extra[8 + 2 * h : 10 + 2 * h], sens[c, h, s].astype(F32)[2:]], axis=0
                )
                for h in range(2)
            )
            pr = sr * real + si * imag
            pi = sr * imag - si * real
            if c:
                pr = pr + wide(partial, 0, rows)
                pi = pi + wide(partial, 1, rows)
            put(partial, pr, 0, rows)
            put(partial, pi, 1, rows)
    turn = RING - lax.axis_index("space") % RING
    for x in range(ROWS):
        place = (x + 2) % ROWS
        both = jnp.concatenate(
            [wide(partial, h, pl.ds(place, 8, stride=16)) for h in range(2)], axis=0
        )
        out[(x // 4 + turn) % RING, x % 4 * 16 : (x % 4 + 1) * 16] = both.astype(BF)


def outer():
    space = lax.axis_index("space")
    quarter = (space + lax.axis_index("ring")) % RING
    first = jnp.where((space == 0) & (quarter == 0), 0.0, 1.0)
    last = jnp.where((space == SPACE - 1) & (quarter == RING - 1), 0.0, 1.0)
    return first, last


def image_weights(first, second, band1, band2, w1, w2):
    edge = outer()
    matrix = rows_of(first, 3, 3, 3)
    for x in range(6):
        block = dot_tn(matrix, band1[x])
        if x == 0:
            block = block * edge[0]
        if x == 5:
            block = block * edge[1]
        w1[x * CH : (x + 1) * CH, :] = block.astype(BF)
    matrix = doubled(rows_of(second, 3, 3, 3))
    for pair in range(3):
        w2[:, pair * 128 : (pair + 1) * 128] = dot(band2[pair], matrix).astype(BF)


def image_kernel(previous, own, w1, w2, out, rows8, x3, acc, fin):
    edge = outer()
    put(rows8, previous[0:32].astype(F32) * edge[0], slice(0, 32))
    put(rows8, previous[32:64].astype(F32), slice(32, 64))
    put(rows8, own[0:32].astype(F32), slice(64, 96))
    put(rows8, own[32:64].astype(F32) * edge[1], slice(96, 128))
    x3[0:48] = jnp.zeros((48, N), BF)
    x3[432:480] = jnp.zeros((48, N), BF)
    for s in range(SLICES):
        v = wide(rows8, pl.ds(s, 16, stride=8))
        base = (s + 1) * 48
        x3[base : base + 16] = before(v).astype(BF)
        x3[base + 16 : base + 32] = v.astype(BF)
        x3[base + 32 : base + 48] = after(v).astype(BF)
    acc[...] = jnp.zeros_like(acc)
    for t in range(SLICES):
        hidden = jnp.maximum(dot(w1[...], x3[t * 48 : t * 48 + 144]).astype(BF), 0)
        spread = dot(w2[...], hidden)
        for a in range(3):
            s = t + 1 - a
            if 0 <= s < SLICES:
                acc[s * 24 : (s + 1) * 24] = acc[s * 24 : (s + 1) * 24] + spread[a * 24 : (a + 1) * 24]
    for s in range(SLICES):
        v = acc[s * 24 : (s + 1) * 24]
        put(fin, before(v[0:8]) + v[8:16] + after(v[16:24]), slice(s * 8, (s + 1) * 8))
    for e in range(4):
        update = jnp.concatenate([wide(fin, pl.ds(o * 4 + e, 8, stride=8)) for o in range(2)], axis=0)
        value = (wide(rows8, slice(32 + e * 16, 48 + e * 16)) + update).astype(BF)
        for y in range(RING):
            out[y, e * 16 : (e + 1) * 16] = value


def expand_kernel(gathered, sens, table, out, image_out, image, data):
    cos, sin = table.at[0], table.at[1]
    turn = RING - lax.axis_index("space") % RING
    for x in range(ROWS):
        both = gathered[(x // 4 + turn) % RING, x % 4 * 16 : (x % 4 + 1) * 16].astype(F32)
        for h in range(2):
            put(image, both[h * 8 : (h + 1) * 8], h, pl.ds(x, 8, stride=16))
    for s in range(SLICES):
        rows = slice(s * 16, (s + 1) * 16)
        real, imag = wide(image, 0, rows), wide(image, 1, rows)
        image_out[0, s] = real.astype(BF)
        image_out[1, s] = imag.astype(BF)
        for c in range(COILS):
            sr, si = sens[c, 0, s].astype(F32), sens[c, 1, s].astype(F32)
            rows = slice(c * 128 + s * 16, c * 128 + (s + 1) * 16)
            data[0, rows] = (sr * real - si * imag).astype(BF)
            data[1, rows] = (sr * imag + si * real).astype(BF)
    for part in range(2):
        rows = pl.ds(part * 256, 256)
        co, si = cos[rows, :], sin[rows, :]
        real = dot_nt(co, data[0]) + dot_nt(si, data[1])
        imag = dot_nt(co, data[1]) - dot_nt(si, data[0])
        out[part * 16 : (part + 1) * 16, 0] = real.astype(BF).reshape(16, 16, LANES)
        out[part * 16 : (part + 1) * 16, 1] = imag.astype(BF).reshape(16, 16, LANES)


def finish_kernel(received, measured, keep, table, out, left):
    cos, sin = table.at[0], table.at[1]
    for c in range(COILS):
        regroup(received, left, c)
        rows = slice(c * 128, (c + 1) * 128)
        real = dot(left[0, rows], cos[...]) + dot(left[1, rows], sin[...])
        imag = dot(left[1, rows], cos[...]) - dot(left[0, rows], sin[...])
        for s in range(SLICES):
            mask = keep[s] > 0
            rows = slice(s * 16, (s + 1) * 16)
            for h, value in enumerate((real, imag)):
                out[c, h, s] = jnp.where(
                    mask, measured[c, h, s].astype(F32), value[rows]
                ).astype(BF)


def call(kernel, shapes, scratch, *operands, mib=12):
    single = not isinstance(shapes, list)
    return pl.pallas_call(
        kernel,
        out_shape=shapes,
        in_specs=[VMEM] * len(operands),
        out_specs=VMEM if single else [VMEM] * len(shapes),
        scratch_shapes=scratch,
        compiler_params=pltpu.CompilerParams(vmem_limit_bytes=mib * MIB),
    )(*operands)


def spread(array, axis):
    return lax.all_to_all(array, axis, split_axis=0, concat_axis=0, tiled=True)


def arr(*shape, dtype=BF):
    return jax.ShapeDtypeStruct(shape, dtype)


def local(
    measured, sensitivity, sample_lines, kspace_first, kspace_second, image_first, image_second
):
    plain, late = (jnp.asarray(t) for t in dft_tables())
    iband1, iband2 = (jnp.asarray(t) for t in image_bands())

    eight = pltpu.VMEM((COILS, 2, SLICES, 8, N), BF)
    small = pltpu.VMEM((3, 3, 2, CH), BF)
    rim, near, kw1, kw2, kw2b, keep, follow = pl.pallas_call(
        start_kernel,
        out_shape=[
            arr(PAIRS, 12, N),
            arr(COILS, 2, SLICES, ROWS, N),
            arr(HROWS * CH, 128),
            arr(96, EARLY * CH),
            arr(48, (HROWS - EARLY) * CH),
            arr(SLICES, ROWS, 1, dtype=F32),
            arr(SLICES, 8, 1, dtype=F32),
        ],
        in_specs=[HBM] * 5,
        out_specs=[VMEM] * 7,
        scratch_shapes=[
            eight, pltpu.VMEM((SLICES, 128), jnp.int32), small, small,
            pltpu.SemaphoreType.DMA((5,)),
        ],
        compiler_params=pltpu.CompilerParams(vmem_limit_bytes=12 * MIB),
    )(
        *(
            pltpu.with_memory_space_constraint(v, pltpu.HBM)
            for v in (
                measured,
                sensitivity,
                sample_lines,
                kspace_first.transpose(2, 3, 1, 0),
                kspace_second.transpose(2, 3, 0, 1),
            )
        )
    )
    halo = lax.ppermute(rim, "space", [((i + 1) % SPACE, i) for i in range(SPACE)])
    patches, total = call(
        early_kernel,
        [arr(PAIRS, 96, N), arr(PAIRS, 32, N, dtype=F32)],
        [],
        near, keep, kw1, kw2, late,
        mib=28,
    )
    half_done = call(
        late_kernel,
        arr(SPACE, 2, ROWS, LANES),
        [pltpu.VMEM((2, LANES, N), BF)] + [pltpu.VMEM((128, N), BF)] * UNROLL,
        patches, total, halo, follow, kw1, kw2b, late,
        mib=20,
    )
    half_done = spread(half_done, "space")
    partial = call(
        combine_kernel,
        arr(RING, 64, N),
        [
            pltpu.VMEM((2, LANES, N), BF),
            pltpu.VMEM((COILS, 2, 128, N), F32),
            pltpu.VMEM((2, 4, 128, 128), F32),
        ],
        half_done, sensitivity, halo, late,
    )
    part = spread(partial, "ring").astype(F32).sum(axis=0).astype(BF)

    def place(half, i):
        block, quarter = i // RING % SPACE, i % RING
        return (half * RING + (quarter - block) % RING) * SPACE + block

    axes = ("half", "ring", "space")
    count = RING * SPACE
    exchange = [(place(half, i), place(1 - half, i)) for half in range(HALVES) for i in range(count)]
    forward = [
        (place(half ^ (i % (8 * RING) == 8 * RING - 1), i), place(half, i + 1))
        for half in range(HALVES)
        for i in range(count)
    ]
    other = lax.ppermute(part, axes, exchange)
    image_in = (part.astype(F32) + other.astype(F32)).astype(BF)
    previous = lax.ppermute(image_in, axes, forward)
    iw1, iw2 = call(
        image_weights,
        [arr(6 * CH, 144), arr(72, 6 * CH)],
        [],
        image_first.transpose(2, 3, 4, 1, 0), image_second.transpose(2, 3, 4, 0, 1), iband1, iband2,
    )
    copies = call(
        image_kernel,
        arr(RING, 64, N),
        [
            pltpu.VMEM((4, 128, 128), F32),
            pltpu.VMEM((480, N), BF),
            pltpu.VMEM((SLICES * 24, N), F32),
            pltpu.VMEM((4, SLICES * 8, 128), F32),
        ],
        previous, image_in, iw1, iw2,
    )
    gathered = spread(copies, "ring")
    midway, image_out = call(
        expand_kernel,
        [arr(SPACE, 2, ROWS, LANES), arr(2, SLICES, ROWS, N)],
        [pltpu.VMEM((2, 4, 128, 128), F32), pltpu.VMEM((2, LANES, N), BF)],
        gathered, sensitivity, plain,
    )
    midway = spread(midway, "space")
    kspace_out = call(
        finish_kernel,
        arr(COILS, 2, SLICES, ROWS, N),
        [pltpu.VMEM((2, LANES, N), BF)],
        midway, measured, keep, plain,
    )
    return kspace_out, image_out


def solution(mesh):
    mesh = Mesh(mesh.devices.reshape(HALVES, RING, SPACE), ("half", "ring", "space"))
    placed = P(("half", "ring"), None, None, "space", None)
    return jax.shard_map(
        local,
        mesh=mesh,
        in_specs=(placed, placed, P(), P(), P(), P(), P()),
        out_specs=(placed, P(None, None, "space", None)),
        check_vma=False,
    )
```

```python
import math

import jax
import jax.numpy as jnp
import numpy as np
from jax import lax
from jax.experimental import pallas as pl
from jax.experimental.pallas import tpu as pltpu
from jax.sharding import Mesh
from jax.sharding import PartitionSpec as P

N = 512
COILS = 2
SLICES = 8
ROWS = 16
CH = 64
SPACE = 32
RING = 4
HALVES = 2
PAIRS = COILS * SLICES
LANES = PAIRS * ROWS
MIB = 1024 * 1024
HROWS = ROWS + 2
EARLY = 14
EARLY_GROUP = 1
LATE_GROUP = 4
LOOPS = 2
BF = jnp.bfloat16
F32 = jnp.float32
VMEM = pl.BlockSpec(memory_space=pltpu.VMEM)
HBM = pl.BlockSpec(memory_space=pltpu.HBM)
NT = (((1,), (1,)), ((), ()))
TN = (((0,), (0,)), ((), ()))


def dft_tables():
    position = np.arange(N)
    angles = (position[:, None] * position[None, :] % N).astype(np.float32) * np.float32(
        2.0 * math.pi / N
    )
    factor = np.float32(1.0 / math.sqrt(N))
    cos, sin = (np.cos(angles) * factor).astype(BF), (np.sin(angles) * factor).astype(BF)
    late = (position + np.where(position % ROWS < 2, ROWS, 0)) % N
    plain = np.stack([cos, sin])
    return plain, plain[:, late]


def iota(shape, dim):
    return lax.broadcasted_iota(jnp.int32, shape, dim)


def split(v, size, count):
    quotient = sum((v >= size * n).astype(jnp.int32) for n in range(1, count))
    return quotient, v - quotient * size


def rows_of(ref, *dims):
    return jnp.concatenate([ref[where].astype(F32) for where in np.ndindex(*dims)], axis=0).astype(BF)


def doubled(block):
    zero = jnp.zeros_like(block)
    return jnp.concatenate(
        [jnp.concatenate([block, zero], axis=1), jnp.concatenate([zero, block], axis=1)], axis=0
    )


def start_kernel(
    far_measured, far_sens, far_lines, far_first, far_second,
    rim, measured, w1, w1b, w2, w2b, keep, follow, sens, lines, first, second, sems,
):
    rows = pl.ds(0, 8)
    copies = [
        pltpu.make_async_copy(source, target, sems.at[n])
        for n, (source, target) in enumerate(
            (
                (far_measured, measured),
                (far_sens.at[:, :, :, rows, :], sens),
                (far_lines, lines),
                (far_first, first),
                (far_second, second),
            )
        )
    ]
    for copy in copies:
        copy.start()
    for copy in copies:
        copy.wait()
    for i in range(PAIRS):
        c, s = i // SLICES, i % SLICES
        rim[i] = jnp.concatenate(
            [measured[c, h, s].astype(F32)[:4] for h in range(2)]
            + [sens[c, h, s].astype(F32)[:2] for h in range(2)],
            axis=0,
        ).astype(BF)
    space = lax.axis_index("space")
    row = space * ROWS + iota((24, 128), 0)
    row = jnp.where(iota((24, 128), 0) >= ROWS + 4, row - 4, row)
    row = jnp.where(row >= N, row - N, row)
    for s in range(SLICES):
        hit = jnp.where(lines[s : s + 1, :] == row, 1.0, 0.0)
        hit = jnp.max(hit, axis=1, keepdims=True)
        keep[s] = hit[:ROWS]
        follow[s] = hit[ROWS:]
    whole = jnp.where(space == SPACE - 1, 0.0, 1.0)
    rest = iota((18, 128), 0)
    h_row = rest & 1
    p_row, q_row = split(rest >> 1, 3, 3)
    matrix = rows_of(first, 3, 3)
    lane = iota((18, 128), 1)
    band = first_band(h_row, p_row, q_row, lane >> 5, (lane >> 4) & 1, lane & 15)
    for r in range(EARLY):
        block = dot_tn(matrix, jnp.where(band == r, 1.0, 0.0).astype(BF))
        w1[r * CH : (r + 1) * CH, :] = block[:, :96].astype(BF)
    t = lane & 15
    h_lane = jnp.where(t < 8, t >> 1, (t - 8) >> 2)
    row = jnp.where(t < 8, ROWS - 2 + (t & 1), ROWS + (t & 3))
    band = first_band(h_row, p_row, q_row, lane >> 4, h_lane, row)
    following = (iota((CH, 128), 1) & 15) >= 8
    for r in range(EARLY, HROWS):
        block = dot_tn(matrix, jnp.where(band == r, 1.0, 0.0).astype(BF))
        across = ~following if r + 1 >= ROWS else following
        block = jnp.where(across, block * whole, block)
        start = (r - EARLY) * CH
        w1b[start : start + CH, :] = block[:, :48].astype(BF)
    matrix = doubled(rows_of(second, 3, 3))
    place = iota((96, 36), 0) & 15
    place = jnp.where(place < 2, place + ROWS, place)
    band = second_band(place, 5)
    for pair in range(EARLY // 2):
        block = dot(jnp.where(band == 2 * pair, 1.0, 0.0).astype(BF), matrix)
        w2[:, pair * 128 : (pair + 1) * 128] = block.astype(BF)
    place = iota((48, 36), 0) & 7
    place = jnp.where(place < 2, place + ROWS, jnp.where(place >= 6, place + 8, -64))
    band = second_band(place, 4)
    late = (iota((48, 128), 0) & 7) < 2
    upper = iota((48, 128), 1) >= CH
    for pair in range(EARLY // 2, HROWS // 2):
        block = dot(jnp.where(band == 2 * pair, 1.0, 0.0).astype(BF), matrix)
        beyond = 2 * pair + 1 + upper.astype(jnp.int32) >= ROWS
        block = jnp.where(late != beyond, block * whole, block)
        start = pair * 128 - EARLY * CH
        w2b[:, start : start + 128] = block.astype(BF)


def first_band(h_row, p_row, q_row, q_lane, h_lane, row):
    return jnp.where((h_row == h_lane) & (q_row == q_lane), row - p_row, -1)


def second_band(place, shift):
    line, lane = iota(place.shape, 0), iota(place.shape, 1)
    parity, rest = split(lane, 18, 2)
    o_lane = rest & 1
    p_lane, q_lane = split(rest >> 1, 3, 3)
    match = (line >> shift == q_lane) & ((line >> (shift - 1)) & 1 == o_lane)
    return jnp.where(match, place + p_lane - 2 - parity, -1)


def image_bands():
    first = np.zeros((6, 54, 144), np.float32)
    for x in range(6):
        for h in range(2):
            for a in range(3):
                for p in range(3):
                    for q in range(3):
                        first[x, a * 18 + p * 6 + q * 2 + h, a * 48 + q * 16 + (x + p) * 2 + h] = 1
    second = np.zeros((3, 72, 108), np.float32)
    for pair in range(3):
        for parity in range(2):
            for o in range(2):
                for a in range(3):
                    for q in range(3):
                        for e in range(4):
                            p = 2 * pair + parity - e
                            if 0 <= p < 3:
                                second[
                                    pair,
                                    a * 24 + q * 8 + o * 4 + e,
                                    parity * 54 + a * 18 + p * 6 + q * 2 + o,
                                ] = 1
    return first.astype(BF), second.astype(BF)


def dot(a, b):
    return jnp.dot(a, b, preferred_element_type=F32)


def dot_tn(a, b):
    return lax.dot_general(a, b, TN, preferred_element_type=F32)


def dot_nt(a, b):
    return lax.dot_general(a, b, NT, preferred_element_type=F32)


def before(v):
    lane = lax.broadcasted_iota(jnp.int32, v.shape, 1)
    return jnp.where(lane == 0, 0.0, pltpu.roll(v, 1, 1))


def after(v):
    lane = lax.broadcasted_iota(jnp.int32, v.shape, 1)
    return jnp.where(lane == N - 1, 0.0, pltpu.roll(v, N - 1, 1))


def blocks_swapped(tiles):
    tiles = list(tiles)
    group = lax.broadcasted_iota(jnp.int32, tiles[0].shape, 1) // 16
    for bit in (4, 2, 1):
        upper = (group & bit) != 0
        for i in range(8):
            if i & bit:
                continue
            a, b = tiles[i], tiles[i + bit]
            tiles[i] = jnp.where(upper, pltpu.roll(b, 16 * bit, 1), a)
            tiles[i + bit] = jnp.where(upper, b, pltpu.roll(a, 128 - 16 * bit, 1))
    return tiles


def wide(ref, *where):
    *lead, rows = where
    return jnp.concatenate([ref[(*lead, b, rows, slice(None))] for b in range(4)], axis=1)


def put(ref, value, *where):
    *lead, rows = where
    for b in range(4):
        ref[(*lead, b, rows, slice(None))] = value[:, b * 128 : (b + 1) * 128]


def regroup(received, left, coil):
    for octet in range(SPACE // 8):
        tiles = [
            received[octet * 8 + i, :, :, coil * 128 : (coil + 1) * 128]
            .astype(F32)
            .reshape(32, 128)
            for i in range(8)
        ]
        for s, tile in enumerate(blocks_swapped(tiles)):
            row = coil * 128 + s * 16
            tile = tile.astype(BF)
            for h in range(2):
                left[h, row : row + 16, octet * 128 : (octet + 1) * 128] = tile[
                    h * 16 : (h + 1) * 16
                ]


def grouped(group, one):
    def step(i, carry):
        for k in range(PAIRS // LOOPS // group):
            one([i * (PAIRS // LOOPS) + k * group + n for n in range(group)])
        return carry

    lax.fori_loop(0, LOOPS, step, 0)


def side_by_side(blocks):
    blocks = [jnp.concatenate([before(v), v, after(v)], axis=0).astype(BF) for v in blocks]
    return jnp.concatenate(blocks, axis=1)


def apart(spread, n):
    third = spread.shape[0] // 3
    left, middle, right = (
        spread[q * third : (q + 1) * third, n * N : (n + 1) * N] for q in range(3)
    )
    return before(left) + middle + after(right)


def early_kernel(measured, keep, w1, w2, table, tail, total):
    def own_rows(i):
        c, s = i // SLICES, i % SLICES
        mask = keep[s] > 0
        return [jnp.where(mask, measured[c, h, s].astype(F32), 0.0) for h in range(2)]

    def one(pairs):
        owns = [own_rows(i) for i in pairs]
        blocks = [jnp.concatenate(own, axis=0) for own in owns]
        hidden = jnp.maximum(dot(w1[...], side_by_side(blocks)).astype(BF), 0)
        spread = dot(w2[...], hidden)
        for n, i in enumerate(pairs):
            total[i] = blocks[n] + apart(spread, n)
            tail[i] = jnp.concatenate(
                [own[ROWS - 2 :] for own in owns[n]] + [jnp.zeros((4, N), F32)], axis=0
            )

    grouped(EARLY_GROUP, one)


def late_kernel(tail, total, halo, follow, w1, w2, table, out, refined):
    cos, sin = table.at[0], table.at[1]

    def one(pairs):
        rims = [
            jnp.where(follow[i % SLICES] > 0, halo[i].astype(F32)[0:8], 0.0) for i in pairs
        ]
        patches = side_by_side(
            [jnp.concatenate([tail[i], rim], axis=0) for i, rim in zip(pairs, rims)]
        )
        hidden = jnp.maximum(dot(w1[...], patches).astype(BF), 0)
        spread = dot(w2[...], hidden)
        line = iota((8, N), 0)
        for n, i in enumerate(pairs):
            more = apart(spread, n)
            row = i * 16 if isinstance(i, int) else pl.multiple_of(i * 16, 16)
            for h in range(2):
                extra = more[h * 8 : (h + 1) * 8]
                rows = rims[n] if h == 0 else pltpu.roll(rims[n], 4, 0)
                done = total[i, h * 16 : (h + 1) * 16]
                done = jnp.concatenate(
                    [
                        jnp.where(line < 2, rows + extra, done[0:8]),
                        jnp.where(line >= 6, done[8:16] + extra, done[8:16]),
                    ],
                    axis=0,
                )
                refined[h, pl.ds(row, 16), :] = done.astype(BF)

    grouped(LATE_GROUP, one)
    for part in range(2):
        rows = pl.ds(part * 256, 256)
        co, si = cos[rows, :], sin[rows, :]
        real = dot_nt(co, refined[0]) - dot_nt(si, refined[1])
        imag = dot_nt(si, refined[0]) + dot_nt(co, refined[1])
        out[part * 16 : (part + 1) * 16, 0] = real.astype(BF).reshape(16, 16, LANES)
        out[part * 16 : (part + 1) * 16, 1] = imag.astype(BF).reshape(16, 16, LANES)


def combine_kernel(received, sens, halo, table, out, left, image, partial):
    cos, sin = table.at[0], table.at[1]
    for c in range(COILS):
        regroup(received, left, c)
        rows = slice(c * 128, (c + 1) * 128)
        image[c, 0] = dot(left[0, rows], cos[...]) - dot(left[1, rows], sin[...])
        image[c, 1] = dot(left[0, rows], sin[...]) + dot(left[1, rows], cos[...])
        for s in range(SLICES):
            rows = slice(s * 16, (s + 1) * 16)
            real, imag = image[c, 0, rows], image[c, 1, rows]
            extra = halo[c * SLICES + s].astype(F32)
            sr, si = (
                jnp.concatenate(
                    [extra[8 + 2 * h : 10 + 2 * h], sens[c, h, s].astype(F32)[2:]], axis=0
                )
                for h in range(2)
            )
            pr = sr * real + si * imag
            pi = sr * imag - si * real
            if c:
                pr = pr + wide(partial, 0, rows)
                pi = pi + wide(partial, 1, rows)
            put(partial, pr, 0, rows)
            put(partial, pi, 1, rows)
    turn = RING - lax.axis_index("space") % RING
    for x in range(ROWS):
        place = (x + 2) % ROWS
        both = jnp.concatenate(
            [wide(partial, h, pl.ds(place, 8, stride=16)) for h in range(2)], axis=0
        )
        out[(x // 4 + turn) % RING, x % 4 * 16 : (x % 4 + 1) * 16] = both.astype(BF)


def outer():
    space = lax.axis_index("space")
    quarter = (space + lax.axis_index("ring")) % RING
    first = jnp.where((space == 0) & (quarter == 0), 0.0, 1.0)
    last = jnp.where((space == SPACE - 1) & (quarter == RING - 1), 0.0, 1.0)
    return first, last


def image_weights(first, second, band1, band2, w1, w2):
    edge = outer()
    matrix = rows_of(first, 3, 3, 3)
    for x in range(6):
        block = dot_tn(matrix, band1[x])
        if x == 0:
            block = block * edge[0]
        if x == 5:
            block = block * edge[1]
        w1[x * CH : (x + 1) * CH, :] = block.astype(BF)
    matrix = doubled(rows_of(second, 3, 3, 3))
    for pair in range(3):
        w2[:, pair * 128 : (pair + 1) * 128] = dot(band2[pair], matrix).astype(BF)


def image_kernel(previous, own, w1, w2, out, rows8, x3, acc, fin):
    edge = outer()
    put(rows8, previous[0:32].astype(F32) * edge[0], slice(0, 32))
    put(rows8, previous[32:64].astype(F32), slice(32, 64))
    put(rows8, own[0:32].astype(F32), slice(64, 96))
    put(rows8, own[32:64].astype(F32) * edge[1], slice(96, 128))
    x3[0:48] = jnp.zeros((48, N), BF)
    x3[432:480] = jnp.zeros((48, N), BF)
    for s in range(SLICES):
        v = wide(rows8, pl.ds(s, 16, stride=8))
        base = (s + 1) * 48
        x3[base : base + 16] = before(v).astype(BF)
        x3[base + 16 : base + 32] = v.astype(BF)
        x3[base + 32 : base + 48] = after(v).astype(BF)
    acc[...] = jnp.zeros_like(acc)
    for t in range(SLICES):
        hidden = jnp.maximum(dot(w1[...], x3[t * 48 : t * 48 + 144]).astype(BF), 0)
        spread = dot(w2[...], hidden)
        for a in range(3):
            s = t + 1 - a
            if 0 <= s < SLICES:
                acc[s * 24 : (s + 1) * 24] = acc[s * 24 : (s + 1) * 24] + spread[a * 24 : (a + 1) * 24]
    for s in range(SLICES):
        v = acc[s * 24 : (s + 1) * 24]
        put(fin, before(v[0:8]) + v[8:16] + after(v[16:24]), slice(s * 8, (s + 1) * 8))
    for e in range(4):
        update = jnp.concatenate([wide(fin, pl.ds(o * 4 + e, 8, stride=8)) for o in range(2)], axis=0)
        value = (wide(rows8, slice(32 + e * 16, 48 + e * 16)) + update).astype(BF)
        for y in range(RING):
            out[y, e * 16 : (e + 1) * 16] = value


def expand_kernel(gathered, sens, table, out, image_out, image, data):
    cos, sin = table.at[0], table.at[1]
    turn = RING - lax.axis_index("space") % RING
    for x in range(ROWS):
        both = gathered[(x // 4 + turn) % RING, x % 4 * 16 : (x % 4 + 1) * 16].astype(F32)
        for h in range(2):
            put(image, both[h * 8 : (h + 1) * 8], h, pl.ds(x, 8, stride=16))
    for s in range(SLICES):
        rows = slice(s * 16, (s + 1) * 16)
        real, imag = wide(image, 0, rows), wide(image, 1, rows)
        image_out[0, s] = real.astype(BF)
        image_out[1, s] = imag.astype(BF)
        for c in range(COILS):
            sr, si = sens[c, 0, s].astype(F32), sens[c, 1, s].astype(F32)
            rows = slice(c * 128 + s * 16, c * 128 + (s + 1) * 16)
            data[0, rows] = (sr * real - si * imag).astype(BF)
            data[1, rows] = (sr * imag + si * real).astype(BF)
    for part in range(2):
        rows = pl.ds(part * 256, 256)
        co, si = cos[rows, :], sin[rows, :]
        real = dot_nt(co, data[0]) + dot_nt(si, data[1])
        imag = dot_nt(co, data[1]) - dot_nt(si, data[0])
        out[part * 16 : (part + 1) * 16, 0] = real.astype(BF).reshape(16, 16, LANES)
        out[part * 16 : (part + 1) * 16, 1] = imag.astype(BF).reshape(16, 16, LANES)


def finish_kernel(received, measured, keep, table, out, left):
    cos, sin = table.at[0], table.at[1]
    for c in range(COILS):
        regroup(received, left, c)
        rows = slice(c * 128, (c + 1) * 128)
        real = dot(left[0, rows], cos[...]) + dot(left[1, rows], sin[...])
        imag = dot(left[1, rows], cos[...]) - dot(left[0, rows], sin[...])
        for s in range(SLICES):
            mask = keep[s] > 0
            rows = slice(s * 16, (s + 1) * 16)
            for h, value in enumerate((real, imag)):
                out[c, h, s] = jnp.where(
                    mask, measured[c, h, s].astype(F32), value[rows]
                ).astype(BF)


def call(kernel, shapes, scratch, *operands, mib=12):
    single = not isinstance(shapes, list)
    return pl.pallas_call(
        kernel,
        out_shape=shapes,
        in_specs=[VMEM] * len(operands),
        out_specs=VMEM if single else [VMEM] * len(shapes),
        scratch_shapes=scratch,
        compiler_params=pltpu.CompilerParams(vmem_limit_bytes=mib * MIB),
    )(*operands)


def spread(array, axis):
    return lax.all_to_all(array, axis, split_axis=0, concat_axis=0, tiled=True)


def arr(*shape, dtype=BF):
    return jax.ShapeDtypeStruct(shape, dtype)


def local(
    measured, sensitivity, sample_lines, kspace_first, kspace_second, image_first, image_second
):
    plain, late = (jnp.asarray(t) for t in dft_tables())
    iband1, iband2 = (jnp.asarray(t) for t in image_bands())

    eight = pltpu.VMEM((COILS, 2, SLICES, 8, N), BF)
    small = pltpu.VMEM((3, 3, 2, CH), BF)
    rim, near, kw1, kw1b, kw2, kw2b, keep, follow = pl.pallas_call(
        start_kernel,
        out_shape=[
            arr(PAIRS, 12, N),
            arr(COILS, 2, SLICES, ROWS, N),
            arr(EARLY * CH, 96),
            arr((HROWS - EARLY) * CH, 48),
            arr(96, EARLY * CH),
            arr(48, (HROWS - EARLY) * CH),
            arr(SLICES, ROWS, 1, dtype=F32),
            arr(SLICES, 8, 1, dtype=F32),
        ],
        in_specs=[HBM] * 5,
        out_specs=[VMEM] * 8,
        scratch_shapes=[
            eight, pltpu.VMEM((SLICES, 128), jnp.int32), small, small,
            pltpu.SemaphoreType.DMA((5,)),
        ],
        compiler_params=pltpu.CompilerParams(vmem_limit_bytes=12 * MIB),
    )(
        *(
            pltpu.with_memory_space_constraint(v, pltpu.HBM)
            for v in (
                measured,
                sensitivity,
                sample_lines,
                kspace_first.transpose(2, 3, 1, 0),
                kspace_second.transpose(2, 3, 0, 1),
            )
        )
    )
    halo = lax.ppermute(rim, "space", [((i + 1) % SPACE, i) for i in range(SPACE)])
    tail, total = call(
        early_kernel,
        [arr(PAIRS, 8, N, dtype=F32), arr(PAIRS, 32, N, dtype=F32)],
        [],
        near, keep, kw1, kw2, late,
        mib=28,
    )
    half_done = call(
        late_kernel,
        arr(SPACE, 2, ROWS, LANES),
        [pltpu.VMEM((2, LANES, N), BF)],
        tail, total, halo, follow, kw1b, kw2b, late,
        mib=20,
    )
    half_done = spread(half_done, "space")
    partial = call(
        combine_kernel,
        arr(RING, 64, N),
        [
            pltpu.VMEM((2, LANES, N), BF),
            pltpu.VMEM((COILS, 2, 128, N), F32),
            pltpu.VMEM((2, 4, 128, 128), F32),
        ],
        half_done, sensitivity, halo, late,
    )
    part = spread(partial, "ring").astype(F32).sum(axis=0).astype(BF)

    def place(half, i):
        block, quarter = i // RING % SPACE, i % RING
        return (half * RING + (quarter - block) % RING) * SPACE + block

    axes = ("half", "ring", "space")
    count = RING * SPACE
    exchange = [(place(half, i), place(1 - half, i)) for half in range(HALVES) for i in range(count)]
    forward = [
        (place(half ^ (i % (8 * RING) == 8 * RING - 1), i), place(half, i + 1))
        for half in range(HALVES)
        for i in range(count)
    ]
    other = lax.ppermute(part, axes, exchange)
    image_in = (part.astype(F32) + other.astype(F32)).astype(BF)
    previous = lax.ppermute(image_in, axes, forward)
    iw1, iw2 = call(
        image_weights,
        [arr(6 * CH, 144), arr(72, 6 * CH)],
        [],
        image_first.transpose(2, 3, 4, 1, 0), image_second.transpose(2, 3, 4, 0, 1), iband1, iband2,
    )
    copies = call(
        image_kernel,
        arr(RING, 64, N),
        [
            pltpu.VMEM((4, 128, 128), F32),
            pltpu.VMEM((480, N), BF),
            pltpu.VMEM((SLICES * 24, N), F32),
            pltpu.VMEM((4, SLICES * 8, 128), F32),
        ],
        previous, image_in, iw1, iw2,
    )
    gathered = spread(copies, "ring")
    midway, image_out = call(
        expand_kernel,
        [arr(SPACE, 2, ROWS, LANES), arr(2, SLICES, ROWS, N)],
        [pltpu.VMEM((2, 4, 128, 128), F32), pltpu.VMEM((2, LANES, N), BF)],
        gathered, sensitivity, plain,
    )
    midway = spread(midway, "space")
    kspace_out = call(
        finish_kernel,
        arr(COILS, 2, SLICES, ROWS, N),
        [pltpu.VMEM((2, LANES, N), BF)],
        midway, measured, keep, plain,
    )
    return kspace_out, image_out


def solution(mesh):
    mesh = Mesh(mesh.devices.reshape(HALVES, RING, SPACE), ("half", "ring", "space"))
    placed = P(("half", "ring"), None, None, "space", None)
    return jax.shard_map(
        local,
        mesh=mesh,
        in_specs=(placed, placed, P(), P(), P(), P(), P()),
        out_specs=(placed, P(None, None, "space", None)),
        check_vma=False,
    )
```

```python
import math

import jax
import jax.numpy as jnp
import numpy as np
from jax import lax
from jax.experimental import pallas as pl
from jax.experimental.pallas import tpu as pltpu
from jax.sharding import Mesh
from jax.sharding import PartitionSpec as P

N = 512
COILS = 2
SLICES = 8
ROWS = 16
CH = 64
SPACE = 32
RING = 4
HALVES = 2
PAIRS = COILS * SLICES
LANES = PAIRS * ROWS
MIB = 1024 * 1024
HROWS = ROWS + 2
EARLY = 14
EARLY_GROUP = 1
LATE_GROUP = 4
IMAGE_GROUP = 2
LOOPS = 2
BF = jnp.bfloat16
F32 = jnp.float32
VMEM = pl.BlockSpec(memory_space=pltpu.VMEM)
HBM = pl.BlockSpec(memory_space=pltpu.HBM)
NT = (((1,), (1,)), ((), ()))
TN = (((0,), (0,)), ((), ()))


def dft_tables():
    position = np.arange(N)
    angles = (position[:, None] * position[None, :] % N).astype(np.float32) * np.float32(
        2.0 * math.pi / N
    )
    factor = np.float32(1.0 / math.sqrt(N))
    cos, sin = (np.cos(angles) * factor).astype(BF), (np.sin(angles) * factor).astype(BF)
    late = (position + np.where(position % ROWS < 2, ROWS, 0)) % N
    plain = np.stack([cos, sin])
    return plain, plain[:, late]


def iota(shape, dim):
    return lax.broadcasted_iota(jnp.int32, shape, dim)


def split(v, size, count):
    quotient = sum((v >= size * n).astype(jnp.int32) for n in range(1, count))
    return quotient, v - quotient * size


def rows_of(ref, *dims):
    return jnp.concatenate([ref[where].astype(F32) for where in np.ndindex(*dims)], axis=0).astype(BF)


def doubled(block):
    zero = jnp.zeros_like(block)
    return jnp.concatenate(
        [jnp.concatenate([block, zero], axis=1), jnp.concatenate([zero, block], axis=1)], axis=0
    )


def start_kernel(
    far_measured, far_sens, far_lines, far_first, far_second,
    rim, measured, w1, w1b, w2, w2b, keep, follow, sens, lines, first, second, sems,
):
    rows = pl.ds(0, 8)
    copies = [
        pltpu.make_async_copy(source, target, sems.at[n])
        for n, (source, target) in enumerate(
            (
                (far_lines, lines),
                (far_first, first),
                (far_second, second),
                (far_measured, measured),
                (far_sens.at[:, :, :, rows, :], sens),
            )
        )
    ]
    for copy in copies:
        copy.start()
    for copy in copies[:3]:
        copy.wait()
    space = lax.axis_index("space")
    row = space * ROWS + iota((24, 128), 0)
    row = jnp.where(iota((24, 128), 0) >= ROWS + 4, row - 4, row)
    row = jnp.where(row >= N, row - N, row)
    for s in range(SLICES):
        hit = jnp.where(lines[s : s + 1, :] == row, 1.0, 0.0)
        hit = jnp.max(hit, axis=1, keepdims=True)
        keep[s] = hit[:ROWS]
        follow[s] = hit[ROWS:]
    whole = jnp.where(space == SPACE - 1, 0.0, 1.0)
    rest = iota((18, 128), 0)
    h_row = rest & 1
    p_row, q_row = split(rest >> 1, 3, 3)
    matrix = rows_of(first, 3, 3)
    lane = iota((18, 128), 1)
    band = first_band(h_row, p_row, q_row, lane >> 5, (lane >> 4) & 1, lane & 15)
    for r in range(EARLY):
        block = dot_tn(matrix, jnp.where(band == r, 1.0, 0.0).astype(BF))
        w1[r * CH : (r + 1) * CH, :] = block[:, :96].astype(BF)
    t = lane & 15
    h_lane = jnp.where(t < 8, t >> 1, (t - 8) >> 2)
    row = jnp.where(t < 8, ROWS - 2 + (t & 1), ROWS + (t & 3))
    band = first_band(h_row, p_row, q_row, lane >> 4, h_lane, row)
    following = (iota((CH, 128), 1) & 15) >= 8
    for r in range(EARLY, HROWS):
        block = dot_tn(matrix, jnp.where(band == r, 1.0, 0.0).astype(BF))
        across = ~following if r + 1 >= ROWS else following
        block = jnp.where(across, block * whole, block)
        start = (r - EARLY) * CH
        w1b[start : start + CH, :] = block[:, :48].astype(BF)
    matrix = doubled(rows_of(second, 3, 3))
    place = iota((96, 36), 0) & 15
    place = jnp.where(place < 2, place + ROWS, place)
    band = second_band(place, 5)
    for pair in range(EARLY // 2):
        block = dot(jnp.where(band == 2 * pair, 1.0, 0.0).astype(BF), matrix)
        w2[:, pair * 128 : (pair + 1) * 128] = block.astype(BF)
    place = iota((48, 36), 0) & 7
    place = jnp.where(place < 2, place + ROWS, jnp.where(place >= 6, place + 8, -64))
    band = second_band(place, 4)
    late = (iota((48, 128), 0) & 7) < 2
    upper = iota((48, 128), 1) >= CH
    for pair in range(EARLY // 2, HROWS // 2):
        block = dot(jnp.where(band == 2 * pair, 1.0, 0.0).astype(BF), matrix)
        beyond = 2 * pair + 1 + upper.astype(jnp.int32) >= ROWS
        block = jnp.where(late != beyond, block * whole, block)
        start = pair * 128 - EARLY * CH
        w2b[:, start : start + 128] = block.astype(BF)
    for copy in copies[3:]:
        copy.wait()
    for i in range(PAIRS):
        c, s = i // SLICES, i % SLICES
        rim[i] = jnp.concatenate(
            [measured[c, h, s].astype(F32)[:4] for h in range(2)]
            + [sens[c, h, s].astype(F32)[:2] for h in range(2)],
            axis=0,
        ).astype(BF)


def first_band(h_row, p_row, q_row, q_lane, h_lane, row):
    return jnp.where((h_row == h_lane) & (q_row == q_lane), row - p_row, -1)


def second_band(place, shift):
    line, lane = iota(place.shape, 0), iota(place.shape, 1)
    parity, rest = split(lane, 18, 2)
    o_lane = rest & 1
    p_lane, q_lane = split(rest >> 1, 3, 3)
    match = (line >> shift == q_lane) & ((line >> (shift - 1)) & 1 == o_lane)
    return jnp.where(match, place + p_lane - 2 - parity, -1)


def image_bands():
    first = np.zeros((6, 54, 144), np.float32)
    for x in range(6):
        for h in range(2):
            for a in range(3):
                for p in range(3):
                    for q in range(3):
                        first[x, a * 18 + p * 6 + q * 2 + h, a * 48 + q * 16 + (x + p) * 2 + h] = 1
    second = np.zeros((3, 72, 108), np.float32)
    for pair in range(3):
        for parity in range(2):
            for o in range(2):
                for a in range(3):
                    for q in range(3):
                        for e in range(4):
                            p = 2 * pair + parity - e
                            if 0 <= p < 3:
                                second[
                                    pair,
                                    a * 24 + q * 8 + o * 4 + e,
                                    parity * 54 + a * 18 + p * 6 + q * 2 + o,
                                ] = 1
    return first.astype(BF), second.astype(BF)


def dot(a, b):
    return jnp.dot(a, b, preferred_element_type=F32)


def dot_tn(a, b):
    return lax.dot_general(a, b, TN, preferred_element_type=F32)


def dot_nt(a, b):
    return lax.dot_general(a, b, NT, preferred_element_type=F32)


def before(v):
    lane = lax.broadcasted_iota(jnp.int32, v.shape, 1)
    return jnp.where(lane == 0, 0.0, pltpu.roll(v, 1, 1))


def after(v):
    lane = lax.broadcasted_iota(jnp.int32, v.shape, 1)
    return jnp.where(lane == N - 1, 0.0, pltpu.roll(v, N - 1, 1))


def blocks_swapped(tiles):
    tiles = list(tiles)
    group = lax.broadcasted_iota(jnp.int32, tiles[0].shape, 1) // 16
    for bit in (4, 2, 1):
        upper = (group & bit) != 0
        for i in range(8):
            if i & bit:
                continue
            a, b = tiles[i], tiles[i + bit]
            tiles[i] = jnp.where(upper, pltpu.roll(b, 16 * bit, 1), a)
            tiles[i + bit] = jnp.where(upper, b, pltpu.roll(a, 128 - 16 * bit, 1))
    return tiles


def wide(ref, *where):
    *lead, rows = where
    return jnp.concatenate([ref[(*lead, b, rows, slice(None))] for b in range(4)], axis=1)


def put(ref, value, *where):
    *lead, rows = where
    for b in range(4):
        ref[(*lead, b, rows, slice(None))] = value[:, b * 128 : (b + 1) * 128]


def regroup(received, left, coil):
    for octet in range(SPACE // 8):
        tiles = [
            received[octet * 8 + i, :, :, coil * 128 : (coil + 1) * 128].reshape(32, 128)
            for i in range(8)
        ]
        for s, tile in enumerate(blocks_swapped(tiles)):
            row = coil * 128 + s * 16
            for h in range(2):
                left[h, row : row + 16, octet * 128 : (octet + 1) * 128] = tile[
                    h * 16 : (h + 1) * 16
                ]


def grouped(group, one):
    def step(i, carry):
        for k in range(PAIRS // LOOPS // group):
            one([i * (PAIRS // LOOPS) + k * group + n for n in range(group)])
        return carry

    lax.fori_loop(0, LOOPS, step, 0)


def side_by_side(blocks):
    blocks = [jnp.concatenate([before(v), v, after(v)], axis=0).astype(BF) for v in blocks]
    return jnp.concatenate(blocks, axis=1)


def apart(spread, n):
    third = spread.shape[0] // 3
    left, middle, right = (
        spread[q * third : (q + 1) * third, n * N : (n + 1) * N] for q in range(3)
    )
    return before(left) + middle + after(right)


def early_kernel(measured, keep, w1, w2, table, tail, total):
    def own_rows(i):
        c, s = i // SLICES, i % SLICES
        mask = keep[s] > 0
        return [jnp.where(mask, measured[c, h, s].astype(F32), 0.0) for h in range(2)]

    def one(pairs):
        owns = [own_rows(i) for i in pairs]
        blocks = [jnp.concatenate(own, axis=0) for own in owns]
        hidden = jnp.maximum(dot(w1[...], side_by_side(blocks)).astype(BF), 0)
        spread = dot(w2[...], hidden)
        for n, i in enumerate(pairs):
            total[i] = blocks[n] + apart(spread, n)
            tail[i] = jnp.concatenate(
                [own[ROWS - 2 :] for own in owns[n]] + [jnp.zeros((4, N), F32)], axis=0
            )

    grouped(EARLY_GROUP, one)


def late_kernel(tail, total, halo, follow, w1, w2, table, out, refined):
    cos, sin = table.at[0], table.at[1]

    def one(pairs):
        rims = [
            jnp.where(follow[i % SLICES] > 0, halo[i].astype(F32)[0:8], 0.0) for i in pairs
        ]
        patches = side_by_side(
            [jnp.concatenate([tail[i], rim], axis=0) for i, rim in zip(pairs, rims)]
        )
        hidden = jnp.maximum(dot(w1[...], patches).astype(BF), 0)
        spread = dot(w2[...], hidden)
        line = iota((8, N), 0)
        for n, i in enumerate(pairs):
            more = apart(spread, n)
            row = i * 16 if isinstance(i, int) else pl.multiple_of(i * 16, 16)
            for h in range(2):
                extra = more[h * 8 : (h + 1) * 8]
                rows = rims[n] if h == 0 else pltpu.roll(rims[n], 4, 0)
                done = total[i, h * 16 : (h + 1) * 16]
                done = jnp.concatenate(
                    [
                        jnp.where(line < 2, rows + extra, done[0:8]),
                        jnp.where(line >= 6, done[8:16] + extra, done[8:16]),
                    ],
                    axis=0,
                )
                refined[h, pl.ds(row, 16), :] = done.astype(BF)

    grouped(LATE_GROUP, one)
    for part in range(2):
        rows = pl.ds(part * 256, 256)
        co, si = cos[rows, :], sin[rows, :]
        real = dot_nt(co, refined[0]) - dot_nt(si, refined[1])
        imag = dot_nt(si, refined[0]) + dot_nt(co, refined[1])
        out[part * 16 : (part + 1) * 16, 0] = real.astype(BF).reshape(16, 16, LANES)
        out[part * 16 : (part + 1) * 16, 1] = imag.astype(BF).reshape(16, 16, LANES)


def combine_kernel(received, sens, halo, table, out, left, image, partial):
    cos, sin = table.at[0], table.at[1]
    for c in range(COILS):
        regroup(received, left, c)
        rows = slice(c * 128, (c + 1) * 128)
        image[c, 0] = dot(left[0, rows], cos[...]) - dot(left[1, rows], sin[...])
        image[c, 1] = dot(left[0, rows], sin[...]) + dot(left[1, rows], cos[...])
        for s in range(SLICES):
            rows = slice(s * 16, (s + 1) * 16)
            real, imag = image[c, 0, rows], image[c, 1, rows]
            extra = halo[c * SLICES + s].astype(F32)
            sr, si = (
                jnp.concatenate(
                    [extra[8 + 2 * h : 10 + 2 * h], sens[c, h, s].astype(F32)[2:]], axis=0
                )
                for h in range(2)
            )
            pr = sr * real + si * imag
            pi = sr * imag - si * real
            if c:
                pr = pr + wide(partial, 0, rows)
                pi = pi + wide(partial, 1, rows)
            put(partial, pr, 0, rows)
            put(partial, pi, 1, rows)
    turn = RING - lax.axis_index("space") % RING
    for x in range(ROWS):
        place = (x + 2) % ROWS
        both = jnp.concatenate(
            [wide(partial, h, pl.ds(place, 8, stride=16)) for h in range(2)], axis=0
        )
        out[(x // 4 + turn) % RING, x % 4 * 16 : (x % 4 + 1) * 16] = both.astype(BF)


def outer():
    space = lax.axis_index("space")
    quarter = (space + lax.axis_index("ring")) % RING
    first = jnp.where((space == 0) & (quarter == 0), 0.0, 1.0)
    last = jnp.where((space == SPACE - 1) & (quarter == RING - 1), 0.0, 1.0)
    return first, last


def image_weights(first, second, band1, band2, w1, w2):
    edge = outer()
    matrix = rows_of(first, 3, 3, 3)
    for x in range(6):
        block = dot_tn(matrix, band1[x])
        if x == 0:
            block = block * edge[0]
        if x == 5:
            block = block * edge[1]
        w1[x * CH : (x + 1) * CH, :] = block.astype(BF)
    matrix = doubled(rows_of(second, 3, 3, 3))
    for pair in range(3):
        w2[:, pair * 128 : (pair + 1) * 128] = dot(band2[pair], matrix).astype(BF)


def image_kernel(previous, own, w1, w2, out, rows8, x3, acc, fin):
    edge = outer()
    put(rows8, previous[0:32].astype(F32) * edge[0], slice(0, 32))
    put(rows8, previous[32:64].astype(F32), slice(32, 64))
    put(rows8, own[0:32].astype(F32), slice(64, 96))
    put(rows8, own[32:64].astype(F32) * edge[1], slice(96, 128))
    x3[0:48] = jnp.zeros((48, N), BF)
    x3[432:480] = jnp.zeros((48, N), BF)
    for s in range(SLICES):
        v = wide(rows8, pl.ds(s, 16, stride=8))
        base = (s + 1) * 48
        x3[base : base + 16] = before(v).astype(BF)
        x3[base + 16 : base + 32] = v.astype(BF)
        x3[base + 32 : base + 48] = after(v).astype(BF)
    acc[...] = jnp.zeros_like(acc)
    for start in range(0, SLICES, IMAGE_GROUP):
        group = range(start, start + IMAGE_GROUP)
        patches = jnp.concatenate([x3[t * 48 : t * 48 + 144] for t in group], axis=1)
        hidden = jnp.maximum(dot(w1[...], patches).astype(BF), 0)
        spread = dot(w2[...], hidden)
        for t in group:
            columns = slice((t - start) * N, (t - start + 1) * N)
            for a in range(3):
                s = t + 1 - a
                if 0 <= s < SLICES:
                    rows = slice(s * 24, (s + 1) * 24)
                    acc[rows] = acc[rows] + spread[a * 24 : (a + 1) * 24, columns]
    for s in range(SLICES):
        v = acc[s * 24 : (s + 1) * 24]
        put(fin, before(v[0:8]) + v[8:16] + after(v[16:24]), slice(s * 8, (s + 1) * 8))
    for e in range(4):
        update = jnp.concatenate([wide(fin, pl.ds(o * 4 + e, 8, stride=8)) for o in range(2)], axis=0)
        value = (wide(rows8, slice(32 + e * 16, 48 + e * 16)) + update).astype(BF)
        for y in range(RING):
            out[y, e * 16 : (e + 1) * 16] = value


def expand_kernel(gathered, sens, table, out, image_out, image, data):
    cos, sin = table.at[0], table.at[1]
    turn = RING - lax.axis_index("space") % RING
    for x in range(ROWS):
        both = gathered[(x // 4 + turn) % RING, x % 4 * 16 : (x % 4 + 1) * 16].astype(F32)
        for h in range(2):
            put(image, both[h * 8 : (h + 1) * 8], h, pl.ds(x, 8, stride=16))
    for s in range(SLICES):
        rows = slice(s * 16, (s + 1) * 16)
        real, imag = wide(image, 0, rows), wide(image, 1, rows)
        image_out[0, s] = real.astype(BF)
        image_out[1, s] = imag.astype(BF)
        for c in range(COILS):
            sr, si = sens[c, 0, s].astype(F32), sens[c, 1, s].astype(F32)
            rows = slice(c * 128 + s * 16, c * 128 + (s + 1) * 16)
            data[0, rows] = (sr * real - si * imag).astype(BF)
            data[1, rows] = (sr * imag + si * real).astype(BF)
    for part in range(2):
        rows = pl.ds(part * 256, 256)
        co, si = cos[rows, :], sin[rows, :]
        real = dot_nt(co, data[0]) + dot_nt(si, data[1])
        imag = dot_nt(co, data[1]) - dot_nt(si, data[0])
        out[part * 16 : (part + 1) * 16, 0] = real.astype(BF).reshape(16, 16, LANES)
        out[part * 16 : (part + 1) * 16, 1] = imag.astype(BF).reshape(16, 16, LANES)


def finish_kernel(received, measured, keep, table, image, out, image_out, left, done, sems):
    cos, sin = table.at[0], table.at[1]
    copies = [pltpu.make_async_copy(image, image_out, sems.at[COILS])]
    copies[0].start()
    for c in range(COILS):
        regroup(received, left, c)
        rows = slice(c * 128, (c + 1) * 128)
        real = dot(left[0, rows], cos[...]) + dot(left[1, rows], sin[...])
        imag = dot(left[1, rows], cos[...]) - dot(left[0, rows], sin[...])
        for s in range(SLICES):
            mask = keep[s] > 0
            rows = slice(s * 16, (s + 1) * 16)
            for h, value in enumerate((real, imag)):
                done[c, h, s] = jnp.where(
                    mask, measured[c, h, s].astype(F32), value[rows]
                ).astype(BF)
        copies.append(pltpu.make_async_copy(done.at[c], out.at[c], sems.at[c]))
        copies[-1].start()
    for copy in copies:
        copy.wait()


def call(kernel, shapes, scratch, *operands, mib=12):
    single = not isinstance(shapes, list)
    return pl.pallas_call(
        kernel,
        out_shape=shapes,
        in_specs=[VMEM] * len(operands),
        out_specs=VMEM if single else [VMEM] * len(shapes),
        scratch_shapes=scratch,
        compiler_params=pltpu.CompilerParams(vmem_limit_bytes=mib * MIB),
    )(*operands)


def spread(array, axis):
    return lax.all_to_all(array, axis, split_axis=0, concat_axis=0, tiled=True)


def arr(*shape, dtype=BF):
    return jax.ShapeDtypeStruct(shape, dtype)


def local(
    measured, sensitivity, sample_lines, kspace_first, kspace_second, image_first, image_second
):
    plain, late = (jnp.asarray(t) for t in dft_tables())
    iband1, iband2 = (jnp.asarray(t) for t in image_bands())

    eight = pltpu.VMEM((COILS, 2, SLICES, 8, N), BF)
    small = pltpu.VMEM((3, 3, 2, CH), BF)
    rim, near, kw1, kw1b, kw2, kw2b, keep, follow = pl.pallas_call(
        start_kernel,
        out_shape=[
            arr(PAIRS, 12, N),
            arr(COILS, 2, SLICES, ROWS, N),
            arr(EARLY * CH, 96),
            arr((HROWS - EARLY) * CH, 48),
            arr(96, EARLY * CH),
            arr(48, (HROWS - EARLY) * CH),
            arr(SLICES, ROWS, 1, dtype=F32),
            arr(SLICES, 8, 1, dtype=F32),
        ],
        in_specs=[HBM] * 5,
        out_specs=[VMEM] * 8,
        scratch_shapes=[
            eight, pltpu.VMEM((SLICES, 128), jnp.int32), small, small,
            pltpu.SemaphoreType.DMA((5,)),
        ],
        compiler_params=pltpu.CompilerParams(vmem_limit_bytes=12 * MIB),
    )(
        *(
            pltpu.with_memory_space_constraint(v, pltpu.HBM)
            for v in (
                measured,
                sensitivity,
                sample_lines,
                kspace_first.transpose(2, 3, 1, 0),
                kspace_second.transpose(2, 3, 0, 1),
            )
        )
    )
    halo = lax.ppermute(rim, "space", [((i + 1) % SPACE, i) for i in range(SPACE)])
    tail, total = call(
        early_kernel,
        [arr(PAIRS, 8, N, dtype=F32), arr(PAIRS, 32, N, dtype=F32)],
        [],
        near, keep, kw1, kw2, late,
        mib=28,
    )
    half_done = call(
        late_kernel,
        arr(SPACE, 2, ROWS, LANES),
        [pltpu.VMEM((2, LANES, N), BF)],
        tail, total, halo, follow, kw1b, kw2b, late,
        mib=20,
    )
    half_done = spread(half_done, "space")
    partial = call(
        combine_kernel,
        arr(RING, 64, N),
        [
            pltpu.VMEM((2, LANES, N), BF),
            pltpu.VMEM((COILS, 2, 128, N), F32),
            pltpu.VMEM((2, 4, 128, 128), F32),
        ],
        half_done, sensitivity, halo, late,
    )
    part = spread(partial, "ring").astype(F32).sum(axis=0).astype(BF)

    def place(half, i):
        block, quarter = i // RING % SPACE, i % RING
        return (half * RING + (quarter - block) % RING) * SPACE + block

    axes = ("half", "ring", "space")
    count = RING * SPACE
    exchange = [(place(half, i), place(1 - half, i)) for half in range(HALVES) for i in range(count)]
    forward = [
        (place(half ^ (i % (8 * RING) == 8 * RING - 1), i), place(half, i + 1))
        for half in range(HALVES)
        for i in range(count)
    ]
    other = lax.ppermute(part, axes, exchange)
    image_in = (part.astype(F32) + other.astype(F32)).astype(BF)
    previous = lax.ppermute(image_in, axes, forward)
    iw1, iw2 = call(
        image_weights,
        [arr(6 * CH, 144), arr(72, 6 * CH)],
        [],
        image_first.transpose(2, 3, 4, 1, 0), image_second.transpose(2, 3, 4, 0, 1), iband1, iband2,
    )
    copies = call(
        image_kernel,
        arr(RING, 64, N),
        [
            pltpu.VMEM((4, 128, 128), F32),
            pltpu.VMEM((480, N), BF),
            pltpu.VMEM((SLICES * 24, N), F32),
            pltpu.VMEM((4, SLICES * 8, 128), F32),
        ],
        previous, image_in, iw1, iw2,
    )
    gathered = spread(copies, "ring")
    midway, image_out = call(
        expand_kernel,
        [arr(SPACE, 2, ROWS, LANES), arr(2, SLICES, ROWS, N)],
        [pltpu.VMEM((2, 4, 128, 128), F32), pltpu.VMEM((2, LANES, N), BF)],
        gathered, sensitivity, plain,
    )
    midway = spread(midway, "space")
    whole = arr(COILS, 2, SLICES, ROWS, N)
    kspace_out, image_out = pl.pallas_call(
        finish_kernel,
        out_shape=[whole, arr(2, SLICES, ROWS, N)],
        in_specs=[VMEM] * 5,
        out_specs=[HBM] * 2,
        scratch_shapes=[
            pltpu.VMEM((2, LANES, N), BF),
            pltpu.VMEM(whole.shape, BF),
            pltpu.SemaphoreType.DMA((COILS + 1,)),
        ],
        compiler_params=pltpu.CompilerParams(vmem_limit_bytes=12 * MIB),
    )(midway, measured, keep, plain, image_out)
    return kspace_out, image_out


def solution(mesh):
    mesh = Mesh(mesh.devices.reshape(HALVES, RING, SPACE), ("half", "ring", "space"))
    placed = P(("half", "ring"), None, None, "space", None)
    return jax.shard_map(
        local,
        mesh=mesh,
        in_specs=(placed, placed, P(), P(), P(), P(), P()),
        out_specs=(placed, P(None, None, "space", None)),
        check_vma=False,
    )
```

```python
import math

import jax
import jax.numpy as jnp
import numpy as np
from jax import lax
from jax.experimental import pallas as pl
from jax.experimental.pallas import tpu as pltpu
from jax.sharding import Mesh
from jax.sharding import PartitionSpec as P

N = 512
COILS = 2
SLICES = 8
ROWS = 16
CH = 64
SPACE = 32
RING = 4
HALVES = 2
PAIRS = COILS * SLICES
LANES = PAIRS * ROWS
MIB = 1024 * 1024
HROWS = ROWS + 2
EARLY = 14
EARLY_GROUP = 1
LATE_GROUP = 4
IMAGE_GROUP = 2
LOOPS = 2
BF = jnp.bfloat16
F32 = jnp.float32
VMEM = pl.BlockSpec(memory_space=pltpu.VMEM)
HBM = pl.BlockSpec(memory_space=pltpu.HBM)
NT = (((1,), (1,)), ((), ()))
TN = (((0,), (0,)), ((), ()))


def dft_tables():
    position = np.arange(N)
    angles = (position[:, None] * position[None, :] % N).astype(np.float32) * np.float32(
        2.0 * math.pi / N
    )
    factor = np.float32(1.0 / math.sqrt(N))
    cos, sin = (np.cos(angles) * factor).astype(BF), (np.sin(angles) * factor).astype(BF)
    late = (position + np.where(position % ROWS < 2, ROWS, 0)) % N
    plain = np.stack([cos, sin])
    return plain, plain[:, late]


def iota(shape, dim):
    return lax.broadcasted_iota(jnp.int32, shape, dim)


def split(v, size, count):
    quotient = sum((v >= size * n).astype(jnp.int32) for n in range(1, count))
    return quotient, v - quotient * size


def rows_of(ref, *dims):
    return jnp.concatenate([ref[where].astype(F32) for where in np.ndindex(*dims)], axis=0).astype(BF)


def doubled(block):
    zero = jnp.zeros_like(block)
    return jnp.concatenate(
        [jnp.concatenate([block, zero], axis=1), jnp.concatenate([zero, block], axis=1)], axis=0
    )


def start_kernel(
    far_measured, far_sens, far_lines, far_first, far_second,
    rim, measured, w1, w1b, w2, w2b, keep, follow, sens, lines, first, second, sems,
):
    rows = pl.ds(0, 8)
    copies = [
        pltpu.make_async_copy(source, target, sems.at[n])
        for n, (source, target) in enumerate(
            (
                (far_lines, lines),
                (far_first, first),
                (far_second, second),
                (far_measured, measured),
                (far_sens.at[:, :, :, rows, :], sens),
            )
        )
    ]
    for copy in copies:
        copy.start()
    for copy in copies[:3]:
        copy.wait()
    space = lax.axis_index("space")
    row = space * ROWS + iota((24, 128), 0)
    row = jnp.where(iota((24, 128), 0) >= ROWS + 4, row - 4, row)
    row = jnp.where(row >= N, row - N, row)
    for s in range(SLICES):
        hit = jnp.where(lines[s : s + 1, :] == row, 1.0, 0.0)
        hit = jnp.max(hit, axis=1, keepdims=True)
        keep[s] = hit[:ROWS]
        follow[s] = hit[ROWS:]
    whole = jnp.where(space == SPACE - 1, 0.0, 1.0)
    rest = iota((18, 128), 0)
    h_row = rest & 1
    p_row, q_row = split(rest >> 1, 3, 3)
    matrix = rows_of(first, 3, 3)
    lane = iota((18, 128), 1)
    band = first_band(h_row, p_row, q_row, lane >> 5, (lane >> 4) & 1, lane & 15)
    for r in range(EARLY):
        block = dot_tn(matrix, jnp.where(band == r, 1.0, 0.0).astype(BF))
        w1[r * CH : (r + 1) * CH, :] = block[:, :96].astype(BF)
    t = lane & 15
    h_lane = jnp.where(t < 8, t >> 1, (t - 8) >> 2)
    row = jnp.where(t < 8, ROWS - 2 + (t & 1), ROWS + (t & 3))
    band = first_band(h_row, p_row, q_row, lane >> 4, h_lane, row)
    following = (iota((CH, 128), 1) & 15) >= 8
    for r in range(EARLY, HROWS):
        block = dot_tn(matrix, jnp.where(band == r, 1.0, 0.0).astype(BF))
        across = ~following if r + 1 >= ROWS else following
        block = jnp.where(across, block * whole, block)
        start = (r - EARLY) * CH
        w1b[start : start + CH, :] = block[:, :48].astype(BF)
    matrix = doubled(rows_of(second, 3, 3))
    place = iota((96, 36), 0) & 15
    place = jnp.where(place < 2, place + ROWS, place)
    band = second_band(place, 5)
    for pair in range(EARLY // 2):
        block = dot(jnp.where(band == 2 * pair, 1.0, 0.0).astype(BF), matrix)
        w2[:, pair * 128 : (pair + 1) * 128] = block.astype(BF)
    place = iota((48, 36), 0) & 7
    place = jnp.where(place < 2, place + ROWS, jnp.where(place >= 6, place + 8, -64))
    band = second_band(place, 4)
    late = (iota((48, 128), 0) & 7) < 2
    upper = iota((48, 128), 1) >= CH
    for pair in range(EARLY // 2, HROWS // 2):
        block = dot(jnp.where(band == 2 * pair, 1.0, 0.0).astype(BF), matrix)
        beyond = 2 * pair + 1 + upper.astype(jnp.int32) >= ROWS
        block = jnp.where(late != beyond, block * whole, block)
        start = pair * 128 - EARLY * CH
        w2b[:, start : start + 128] = block.astype(BF)
    for copy in copies[3:]:
        copy.wait()
    for i in range(PAIRS):
        c, s = i // SLICES, i % SLICES
        rim[i] = jnp.concatenate(
            [measured[c, h, s].astype(F32)[:4] for h in range(2)]
            + [sens[c, h, s].astype(F32)[:2] for h in range(2)],
            axis=0,
        ).astype(BF)


def first_band(h_row, p_row, q_row, q_lane, h_lane, row):
    return jnp.where((h_row == h_lane) & (q_row == q_lane), row - p_row, -1)


def second_band(place, shift):
    line, lane = iota(place.shape, 0), iota(place.shape, 1)
    parity, rest = split(lane, 18, 2)
    o_lane = rest & 1
    p_lane, q_lane = split(rest >> 1, 3, 3)
    match = (line >> shift == q_lane) & ((line >> (shift - 1)) & 1 == o_lane)
    return jnp.where(match, place + p_lane - 2 - parity, -1)


def image_bands():
    first = np.zeros((6, 54, 144), np.float32)
    for x in range(6):
        for h in range(2):
            for a in range(3):
                for p in range(3):
                    for q in range(3):
                        first[x, a * 18 + p * 6 + q * 2 + h, a * 48 + q * 16 + (x + p) * 2 + h] = 1
    second = np.zeros((3, 72, 108), np.float32)
    for pair in range(3):
        for parity in range(2):
            for o in range(2):
                for a in range(3):
                    for q in range(3):
                        for e in range(4):
                            p = 2 * pair + parity - e
                            if 0 <= p < 3:
                                second[
                                    pair,
                                    a * 24 + q * 8 + o * 4 + e,
                                    parity * 54 + a * 18 + p * 6 + q * 2 + o,
                                ] = 1
    return first.astype(BF), second.astype(BF)


def dot(a, b):
    return jnp.dot(a, b, preferred_element_type=F32)


def dot_tn(a, b):
    return lax.dot_general(a, b, TN, preferred_element_type=F32)


def dot_nt(a, b):
    return lax.dot_general(a, b, NT, preferred_element_type=F32)


def before(v):
    lane = lax.broadcasted_iota(jnp.int32, v.shape, 1)
    return jnp.where(lane == 0, 0.0, pltpu.roll(v, 1, 1))


def after(v):
    lane = lax.broadcasted_iota(jnp.int32, v.shape, 1)
    return jnp.where(lane == N - 1, 0.0, pltpu.roll(v, N - 1, 1))


def blocks_swapped(tiles):
    tiles = list(tiles)
    group = lax.broadcasted_iota(jnp.int32, tiles[0].shape, 1) // 16
    for bit in (4, 2, 1):
        upper = (group & bit) != 0
        for i in range(8):
            if i & bit:
                continue
            a, b = tiles[i], tiles[i + bit]
            tiles[i] = jnp.where(upper, pltpu.roll(b, 16 * bit, 1), a)
            tiles[i + bit] = jnp.where(upper, b, pltpu.roll(a, 128 - 16 * bit, 1))
    return tiles


def wide(ref, *where):
    *lead, rows = where
    return jnp.concatenate([ref[(*lead, b, rows, slice(None))] for b in range(4)], axis=1)


def put(ref, value, *where):
    *lead, rows = where
    for b in range(4):
        ref[(*lead, b, rows, slice(None))] = value[:, b * 128 : (b + 1) * 128]


def regroup(received, left, coil):
    for octet in range(SPACE // 8):
        tiles = [
            received[octet * 8 + i, :, :, coil * 128 : (coil + 1) * 128].reshape(32, 128)
            for i in range(8)
        ]
        for s, tile in enumerate(blocks_swapped(tiles)):
            row = coil * 128 + s * 16
            for h in range(2):
                left[h, row : row + 16, octet * 128 : (octet + 1) * 128] = tile[
                    h * 16 : (h + 1) * 16
                ]


def grouped(group, one):
    def step(i, carry):
        for k in range(PAIRS // LOOPS // group):
            one([i * (PAIRS // LOOPS) + k * group + n for n in range(group)])
        return carry

    lax.fori_loop(0, LOOPS, step, 0)


def side_by_side(blocks):
    blocks = [jnp.concatenate([before(v), v, after(v)], axis=0).astype(BF) for v in blocks]
    return jnp.concatenate(blocks, axis=1)


def apart(spread, n):
    third = spread.shape[0] // 3
    left, middle, right = (
        spread[q * third : (q + 1) * third, n * N : (n + 1) * N] for q in range(3)
    )
    return before(left) + middle + after(right)


def early_kernel(measured, keep, w1, w2, table, tail, total):
    def own_rows(i):
        c, s = i // SLICES, i % SLICES
        mask = keep[s] > 0
        return [jnp.where(mask, measured[c, h, s].astype(F32), 0.0) for h in range(2)]

    def one(pairs):
        owns = [own_rows(i) for i in pairs]
        blocks = [jnp.concatenate(own, axis=0) for own in owns]
        hidden = jnp.maximum(dot(w1[...], side_by_side(blocks)).astype(BF), 0)
        spread = dot(w2[...], hidden)
        for n, i in enumerate(pairs):
            total[i] = blocks[n] + apart(spread, n)
            tail[i] = jnp.concatenate(
                [own[ROWS - 2 :] for own in owns[n]] + [jnp.zeros((4, N), F32)], axis=0
            )

    grouped(EARLY_GROUP, one)


def late_kernel(tail, total, halo, follow, w1, w2, table, out, refined):
    cos, sin = table.at[0], table.at[1]

    def one(pairs):
        rims = [
            jnp.where(follow[i % SLICES] > 0, halo[i].astype(F32)[0:8], 0.0) for i in pairs
        ]
        patches = side_by_side(
            [jnp.concatenate([tail[i], rim], axis=0) for i, rim in zip(pairs, rims)]
        )
        hidden = jnp.maximum(dot(w1[...], patches).astype(BF), 0)
        spread = dot(w2[...], hidden)
        line = iota((8, N), 0)
        for n, i in enumerate(pairs):
            more = apart(spread, n)
            row = i * 16 if isinstance(i, int) else pl.multiple_of(i * 16, 16)
            for h in range(2):
                extra = more[h * 8 : (h + 1) * 8]
                rows = rims[n] if h == 0 else pltpu.roll(rims[n], 4, 0)
                done = total[i, h * 16 : (h + 1) * 16]
                done = jnp.concatenate(
                    [
                        jnp.where(line < 2, rows + extra, done[0:8]),
                        jnp.where(line >= 6, done[8:16] + extra, done[8:16]),
                    ],
                    axis=0,
                )
                refined[h, pl.ds(row, 16), :] = done.astype(BF)

    grouped(LATE_GROUP, one)
    for part in range(2):
        rows = pl.ds(part * 256, 256)
        co, si = cos[rows, :], sin[rows, :]
        real = dot_nt(co, refined[0]) - dot_nt(si, refined[1])
        imag = dot_nt(si, refined[0]) + dot_nt(co, refined[1])
        out[part * 16 : (part + 1) * 16, 0] = real.astype(BF).reshape(16, 16, LANES)
        out[part * 16 : (part + 1) * 16, 1] = imag.astype(BF).reshape(16, 16, LANES)


def combine_kernel(received, sens, halo, table, out, left, image, partial):
    cos, sin = table.at[0], table.at[1]
    for c in range(COILS):
        regroup(received, left, c)
        rows = slice(c * 128, (c + 1) * 128)
        image[c, 0] = dot(left[0, rows], cos[...]) - dot(left[1, rows], sin[...])
        image[c, 1] = dot(left[0, rows], sin[...]) + dot(left[1, rows], cos[...])
        for s in range(SLICES):
            rows = slice(s * 16, (s + 1) * 16)
            real, imag = image[c, 0, rows], image[c, 1, rows]
            extra = halo[c * SLICES + s].astype(F32)
            sr, si = (
                jnp.concatenate(
                    [extra[8 + 2 * h : 10 + 2 * h], sens[c, h, s].astype(F32)[2:]], axis=0
                )
                for h in range(2)
            )
            pr = sr * real + si * imag
            pi = sr * imag - si * real
            if c:
                pr = pr + wide(partial, 0, rows)
                pi = pi + wide(partial, 1, rows)
            put(partial, pr, 0, rows)
            put(partial, pi, 1, rows)
    turn = RING - lax.axis_index("space") % RING
    for x in range(ROWS):
        place = (x + 2) % ROWS
        both = jnp.concatenate(
            [wide(partial, h, pl.ds(place, 8, stride=16)) for h in range(2)], axis=0
        )
        out[(x // 4 + turn) % RING, x % 4 * 16 : (x % 4 + 1) * 16] = both.astype(BF)


def outer():
    space = lax.axis_index("space")
    quarter = (space + lax.axis_index("ring")) % RING
    first = jnp.where((space == 0) & (quarter == 0), 0.0, 1.0)
    last = jnp.where((space == SPACE - 1) & (quarter == RING - 1), 0.0, 1.0)
    return first, last


def image_weights(first, second, band1, band2, w1, w2):
    edge = outer()
    matrix = rows_of(first, 3, 3, 3)
    for x in range(6):
        block = dot_tn(matrix, band1[x])
        if x == 0:
            block = block * edge[0]
        if x == 5:
            block = block * edge[1]
        w1[x * CH : (x + 1) * CH, :] = block.astype(BF)
    matrix = doubled(rows_of(second, 3, 3, 3))
    for pair in range(3):
        w2[:, pair * 128 : (pair + 1) * 128] = dot(band2[pair], matrix).astype(BF)


def image_patches(rows8, x3):
    x3[0:48] = jnp.zeros((48, N), BF)
    x3[432:480] = jnp.zeros((48, N), BF)
    for s in range(SLICES):
        v = wide(rows8, pl.ds(s, 16, stride=8))
        base = (s + 1) * 48
        x3[base : base + 16] = before(v).astype(BF)
        x3[base + 16 : base + 32] = v.astype(BF)
        x3[base + 32 : base + 48] = after(v).astype(BF)


def image_sums(x3, w1, w2, acc):
    for start in range(0, SLICES, IMAGE_GROUP):
        group = range(start, start + IMAGE_GROUP)
        patches = jnp.concatenate([x3[t * 48 : t * 48 + 144] for t in group], axis=1)
        hidden = jnp.maximum(dot(w1, patches).astype(BF), 0)
        spread = dot(w2, hidden)
        for t in group:
            columns = slice((t - start) * N, (t - start + 1) * N)
            for a in range(3):
                s = t + 1 - a
                if 0 <= s < SLICES:
                    rows = slice(s * 24, (s + 1) * 24)
                    acc[rows] = acc[rows] + spread[a * 24 : (a + 1) * 24, columns]


def image_early(own, w1, w2, acc, rows8, x3):
    put(rows8, jnp.zeros((64, N), F32), slice(0, 64))
    put(rows8, own[0:32].astype(F32), slice(64, 96))
    put(rows8, own[32:64].astype(F32) * outer()[1], slice(96, 128))
    image_patches(rows8, x3)
    acc[...] = jnp.zeros_like(acc)
    image_sums(x3, w1[4 * CH :], w2[:, 4 * CH :], acc)


def image_late(previous, own, w1, w2, early, out, rows8, x3, acc, fin):
    edge = outer()
    put(rows8, previous[0:32].astype(F32) * edge[0], slice(0, 32))
    put(rows8, previous[32:64].astype(F32), slice(32, 64))
    put(rows8, own[0:32].astype(F32), slice(64, 96))
    put(rows8, own[32:64].astype(F32) * edge[1], slice(96, 128))
    image_patches(rows8, x3)
    acc[...] = early[...]
    image_sums(x3, w1[: 4 * CH], w2[:, : 4 * CH], acc)
    for s in range(SLICES):
        v = acc[s * 24 : (s + 1) * 24]
        put(fin, before(v[0:8]) + v[8:16] + after(v[16:24]), slice(s * 8, (s + 1) * 8))
    for e in range(4):
        update = jnp.concatenate([wide(fin, pl.ds(o * 4 + e, 8, stride=8)) for o in range(2)], axis=0)
        value = (wide(rows8, slice(32 + e * 16, 48 + e * 16)) + update).astype(BF)
        for y in range(RING):
            out[y, e * 16 : (e + 1) * 16] = value


def expand_kernel(gathered, sens, table, out, image_out, image, data):
    cos, sin = table.at[0], table.at[1]
    turn = RING - lax.axis_index("space") % RING
    for x in range(ROWS):
        both = gathered[(x // 4 + turn) % RING, x % 4 * 16 : (x % 4 + 1) * 16].astype(F32)
        for h in range(2):
            put(image, both[h * 8 : (h + 1) * 8], h, pl.ds(x, 8, stride=16))
    for s in range(SLICES):
        rows = slice(s * 16, (s + 1) * 16)
        real, imag = wide(image, 0, rows), wide(image, 1, rows)
        image_out[0, s] = real.astype(BF)
        image_out[1, s] = imag.astype(BF)
        for c in range(COILS):
            sr, si = sens[c, 0, s].astype(F32), sens[c, 1, s].astype(F32)
            rows = slice(c * 128 + s * 16, c * 128 + (s + 1) * 16)
            data[0, rows] = (sr * real - si * imag).astype(BF)
            data[1, rows] = (sr * imag + si * real).astype(BF)
    for part in range(2):
        rows = pl.ds(part * 256, 256)
        co, si = cos[rows, :], sin[rows, :]
        real = dot_nt(co, data[0]) + dot_nt(si, data[1])
        imag = dot_nt(co, data[1]) - dot_nt(si, data[0])
        out[part * 16 : (part + 1) * 16, 0] = real.astype(BF).reshape(16, 16, LANES)
        out[part * 16 : (part + 1) * 16, 1] = imag.astype(BF).reshape(16, 16, LANES)


def finish_kernel(received, measured, keep, table, image, out, image_out, left, done, sems):
    cos, sin = table.at[0], table.at[1]
    copies = [pltpu.make_async_copy(image, image_out, sems.at[COILS])]
    copies[0].start()
    for c in range(COILS):
        regroup(received, left, c)
        rows = slice(c * 128, (c + 1) * 128)
        real = dot(left[0, rows], cos[...]) + dot(left[1, rows], sin[...])
        imag = dot(left[1, rows], cos[...]) - dot(left[0, rows], sin[...])
        for s in range(SLICES):
            mask = keep[s] > 0
            rows = slice(s * 16, (s + 1) * 16)
            for h, value in enumerate((real, imag)):
                done[c, h, s] = jnp.where(
                    mask, measured[c, h, s].astype(F32), value[rows]
                ).astype(BF)
        copies.append(pltpu.make_async_copy(done.at[c], out.at[c], sems.at[c]))
        copies[-1].start()
    for copy in copies:
        copy.wait()


def call(kernel, shapes, scratch, *operands, mib=12):
    single = not isinstance(shapes, list)
    return pl.pallas_call(
        kernel,
        out_shape=shapes,
        in_specs=[VMEM] * len(operands),
        out_specs=VMEM if single else [VMEM] * len(shapes),
        scratch_shapes=scratch,
        compiler_params=pltpu.CompilerParams(vmem_limit_bytes=mib * MIB),
    )(*operands)


def spread(array, axis):
    return lax.all_to_all(array, axis, split_axis=0, concat_axis=0, tiled=True)


def arr(*shape, dtype=BF):
    return jax.ShapeDtypeStruct(shape, dtype)


def local(
    measured, sensitivity, sample_lines, kspace_first, kspace_second, image_first, image_second
):
    plain, late = (jnp.asarray(t) for t in dft_tables())
    iband1, iband2 = (jnp.asarray(t) for t in image_bands())

    eight = pltpu.VMEM((COILS, 2, SLICES, 8, N), BF)
    small = pltpu.VMEM((3, 3, 2, CH), BF)
    rim, near, kw1, kw1b, kw2, kw2b, keep, follow = pl.pallas_call(
        start_kernel,
        out_shape=[
            arr(PAIRS, 12, N),
            arr(COILS, 2, SLICES, ROWS, N),
            arr(EARLY * CH, 96),
            arr((HROWS - EARLY) * CH, 48),
            arr(96, EARLY * CH),
            arr(48, (HROWS - EARLY) * CH),
            arr(SLICES, ROWS, 1, dtype=F32),
            arr(SLICES, 8, 1, dtype=F32),
        ],
        in_specs=[HBM] * 5,
        out_specs=[VMEM] * 8,
        scratch_shapes=[
            eight, pltpu.VMEM((SLICES, 128), jnp.int32), small, small,
            pltpu.SemaphoreType.DMA((5,)),
        ],
        compiler_params=pltpu.CompilerParams(vmem_limit_bytes=12 * MIB),
    )(
        *(
            pltpu.with_memory_space_constraint(v, pltpu.HBM)
            for v in (
                measured,
                sensitivity,
                sample_lines,
                kspace_first.transpose(2, 3, 1, 0),
                kspace_second.transpose(2, 3, 0, 1),
            )
        )
    )
    halo = lax.ppermute(rim, "space", [((i + 1) % SPACE, i) for i in range(SPACE)])
    tail, total = call(
        early_kernel,
        [arr(PAIRS, 8, N, dtype=F32), arr(PAIRS, 32, N, dtype=F32)],
        [],
        near, keep, kw1, kw2, late,
        mib=28,
    )
    half_done = call(
        late_kernel,
        arr(SPACE, 2, ROWS, LANES),
        [pltpu.VMEM((2, LANES, N), BF)],
        tail, total, halo, follow, kw1b, kw2b, late,
        mib=20,
    )
    half_done = spread(half_done, "space")
    partial = call(
        combine_kernel,
        arr(RING, 64, N),
        [
            pltpu.VMEM((2, LANES, N), BF),
            pltpu.VMEM((COILS, 2, 128, N), F32),
            pltpu.VMEM((2, 4, 128, 128), F32),
        ],
        half_done, sensitivity, halo, late,
    )
    part = spread(partial, "ring").astype(F32).sum(axis=0).astype(BF)

    def place(half, i):
        block, quarter = i // RING % SPACE, i % RING
        return (half * RING + (quarter - block) % RING) * SPACE + block

    axes = ("half", "ring", "space")
    count = RING * SPACE
    exchange = [(place(half, i), place(1 - half, i)) for half in range(HALVES) for i in range(count)]
    forward = [
        (place(half ^ (i % (8 * RING) == 8 * RING - 1), i), place(half, i + 1))
        for half in range(HALVES)
        for i in range(count)
    ]
    other = lax.ppermute(part, axes, exchange)
    image_in = (part.astype(F32) + other.astype(F32)).astype(BF)
    previous = lax.ppermute(image_in, axes, forward)
    iw1, iw2 = call(
        image_weights,
        [arr(6 * CH, 144), arr(72, 6 * CH)],
        [],
        image_first.transpose(2, 3, 4, 1, 0), image_second.transpose(2, 3, 4, 0, 1), iband1, iband2,
    )
    rooms = [pltpu.VMEM((4, 128, 128), F32), pltpu.VMEM((480, N), BF)]
    early = call(image_early, arr(SLICES * 24, N, dtype=F32), rooms, image_in, iw1, iw2)
    copies = call(
        image_late,
        arr(RING, 64, N),
        rooms
        + [pltpu.VMEM((SLICES * 24, N), F32), pltpu.VMEM((4, SLICES * 8, 128), F32)],
        previous, image_in, iw1, iw2, early,
    )
    gathered = spread(copies, "ring")
    midway, image_out = call(
        expand_kernel,
        [arr(SPACE, 2, ROWS, LANES), arr(2, SLICES, ROWS, N)],
        [pltpu.VMEM((2, 4, 128, 128), F32), pltpu.VMEM((2, LANES, N), BF)],
        gathered, sensitivity, plain,
    )
    midway = spread(midway, "space")
    whole = arr(COILS, 2, SLICES, ROWS, N)
    kspace_out, image_out = pl.pallas_call(
        finish_kernel,
        out_shape=[whole, arr(2, SLICES, ROWS, N)],
        in_specs=[VMEM] * 5,
        out_specs=[HBM] * 2,
        scratch_shapes=[
            pltpu.VMEM((2, LANES, N), BF),
            pltpu.VMEM(whole.shape, BF),
            pltpu.SemaphoreType.DMA((COILS + 1,)),
        ],
        compiler_params=pltpu.CompilerParams(vmem_limit_bytes=12 * MIB),
    )(midway, measured, keep, plain, image_out)
    return kspace_out, image_out


def solution(mesh):
    mesh = Mesh(mesh.devices.reshape(HALVES, RING, SPACE), ("half", "ring", "space"))
    placed = P(("half", "ring"), None, None, "space", None)
    return jax.shard_map(
        local,
        mesh=mesh,
        in_specs=(placed, placed, P(), P(), P(), P(), P()),
        out_specs=(placed, P(None, None, "space", None)),
        check_vma=False,
    )
```

```python
import math

import jax
import jax.numpy as jnp
import numpy as np
from jax import lax
from jax.experimental import pallas as pl
from jax.experimental.pallas import tpu as pltpu
from jax.sharding import Mesh
from jax.sharding import PartitionSpec as P

N = 512
COILS = 2
SLICES = 8
ROWS = 16
CH = 64
SPACE = 32
RING = 4
HALVES = 2
PAIRS = COILS * SLICES
LANES = PAIRS * ROWS
MIB = 1024 * 1024
HROWS = ROWS + 2
EARLY = 14
EARLY_GROUP = 1
LATE_GROUP = 4
IMAGE_GROUP = 2
LOOPS = 2
BF = jnp.bfloat16
F32 = jnp.float32
VMEM = pl.BlockSpec(memory_space=pltpu.VMEM)
HBM = pl.BlockSpec(memory_space=pltpu.HBM)
NT = (((1,), (1,)), ((), ()))
TN = (((0,), (0,)), ((), ()))


def dft_tables():
    position = np.arange(N)
    angles = (position[:, None] * position[None, :] % N).astype(np.float32) * np.float32(
        2.0 * math.pi / N
    )
    factor = np.float32(1.0 / math.sqrt(N))
    cos, sin = (np.cos(angles) * factor).astype(BF), (np.sin(angles) * factor).astype(BF)
    late = (position + np.where(position % ROWS < 2, ROWS, 0)) % N
    plain = np.stack([cos, sin])
    return plain, plain[:, late]


def iota(shape, dim):
    return lax.broadcasted_iota(jnp.int32, shape, dim)


def split(v, size, count):
    quotient = sum((v >= size * n).astype(jnp.int32) for n in range(1, count))
    return quotient, v - quotient * size


def rows_of(ref, *dims):
    return jnp.concatenate([ref[where].astype(F32) for where in np.ndindex(*dims)], axis=0).astype(BF)


def doubled(block):
    zero = jnp.zeros_like(block)
    return jnp.concatenate(
        [jnp.concatenate([block, zero], axis=1), jnp.concatenate([zero, block], axis=1)], axis=0
    )


def start_kernel(
    far_measured, far_sens, far_lines, far_first, far_second,
    rim, measured, w1, w1b, w2, w2b, keep, follow, sens, lines, first, second, sems,
):
    rows = pl.ds(0, 8)
    copies = [
        pltpu.make_async_copy(source, target, sems.at[n])
        for n, (source, target) in enumerate(
            (
                (far_lines, lines),
                (far_first, first),
                (far_second, second),
                (far_measured, measured),
                (far_sens.at[:, :, :, rows, :], sens),
            )
        )
    ]
    for copy in copies:
        copy.start()
    for copy in copies[:3]:
        copy.wait()
    space = lax.axis_index("space")
    row = space * ROWS + iota((24, 128), 0)
    row = jnp.where(iota((24, 128), 0) >= ROWS + 4, row - 4, row)
    row = jnp.where(row >= N, row - N, row)
    for s in range(SLICES):
        hit = jnp.where(lines[s : s + 1, :] == row, 1.0, 0.0)
        hit = jnp.max(hit, axis=1, keepdims=True)
        keep[s] = hit[:ROWS]
        follow[s] = hit[ROWS:]
    whole = jnp.where(space == SPACE - 1, 0.0, 1.0)
    rest = iota((18, 128), 0)
    h_row = rest & 1
    p_row, q_row = split(rest >> 1, 3, 3)
    matrix = rows_of(first, 3, 3)
    lane = iota((18, 128), 1)
    band = first_band(h_row, p_row, q_row, lane >> 5, (lane >> 4) & 1, lane & 15)
    for r in range(EARLY):
        block = dot_tn(matrix, jnp.where(band == r, 1.0, 0.0).astype(BF))
        w1[r * CH : (r + 1) * CH, :] = block[:, :96].astype(BF)
    t = lane & 15
    h_lane = jnp.where(t < 8, t >> 1, (t - 8) >> 2)
    row = jnp.where(t < 8, ROWS - 2 + (t & 1), ROWS + (t & 3))
    band = first_band(h_row, p_row, q_row, lane >> 4, h_lane, row)
    following = (iota((CH, 128), 1) & 15) >= 8
    for r in range(EARLY, HROWS):
        block = dot_tn(matrix, jnp.where(band == r, 1.0, 0.0).astype(BF))
        across = ~following if r + 1 >= ROWS else following
        block = jnp.where(across, block * whole, block)
        start = (r - EARLY) * CH
        w1b[start : start + CH, :] = block[:, :48].astype(BF)
    matrix = doubled(rows_of(second, 3, 3))
    place = iota((96, 36), 0) & 15
    place = jnp.where(place < 2, place + ROWS, place)
    band = second_band(place, 5)
    for pair in range(EARLY // 2):
        block = dot(jnp.where(band == 2 * pair, 1.0, 0.0).astype(BF), matrix)
        w2[:, pair * 128 : (pair + 1) * 128] = block.astype(BF)
    place = iota((48, 36), 0) & 7
    place = jnp.where(place < 2, place + ROWS, jnp.where(place >= 6, place + 8, -64))
    band = second_band(place, 4)
    late = (iota((48, 128), 0) & 7) < 2
    upper = iota((48, 128), 1) >= CH
    for pair in range(EARLY // 2, HROWS // 2):
        block = dot(jnp.where(band == 2 * pair, 1.0, 0.0).astype(BF), matrix)
        beyond = 2 * pair + 1 + upper.astype(jnp.int32) >= ROWS
        block = jnp.where(late != beyond, block * whole, block)
        start = pair * 128 - EARLY * CH
        w2b[:, start : start + 128] = block.astype(BF)
    for copy in copies[3:]:
        copy.wait()
    for i in range(PAIRS):
        c, s = i // SLICES, i % SLICES
        rim[i] = jnp.concatenate(
            [measured[c, h, s].astype(F32)[:4] for h in range(2)]
            + [sens[c, h, s].astype(F32)[:2] for h in range(2)],
            axis=0,
        ).astype(BF)


def first_band(h_row, p_row, q_row, q_lane, h_lane, row):
    return jnp.where((h_row == h_lane) & (q_row == q_lane), row - p_row, -1)


def second_band(place, shift):
    line, lane = iota(place.shape, 0), iota(place.shape, 1)
    parity, rest = split(lane, 18, 2)
    o_lane = rest & 1
    p_lane, q_lane = split(rest >> 1, 3, 3)
    match = (line >> shift == q_lane) & ((line >> (shift - 1)) & 1 == o_lane)
    return jnp.where(match, place + p_lane - 2 - parity, -1)


def image_bands():
    first = np.zeros((6, 54, 144), np.float32)
    for x in range(6):
        for h in range(2):
            for a in range(3):
                for p in range(3):
                    for q in range(3):
                        first[x, a * 18 + p * 6 + q * 2 + h, a * 48 + q * 16 + (x + p) * 2 + h] = 1
    second = np.zeros((3, 72, 108), np.float32)
    for pair in range(3):
        for parity in range(2):
            for o in range(2):
                for a in range(3):
                    for q in range(3):
                        for e in range(4):
                            p = 2 * pair + parity - e
                            if 0 <= p < 3:
                                second[
                                    pair,
                                    a * 24 + q * 8 + o * 4 + e,
                                    parity * 54 + a * 18 + p * 6 + q * 2 + o,
                                ] = 1
    return first.astype(BF), second.astype(BF)


def dot(a, b):
    return jnp.dot(a, b, preferred_element_type=F32)


def dot_tn(a, b):
    return lax.dot_general(a, b, TN, preferred_element_type=F32)


def dot_nt(a, b):
    return lax.dot_general(a, b, NT, preferred_element_type=F32)


def before(v):
    lane = lax.broadcasted_iota(jnp.int32, v.shape, 1)
    return jnp.where(lane == 0, 0.0, pltpu.roll(v, 1, 1))


def after(v):
    lane = lax.broadcasted_iota(jnp.int32, v.shape, 1)
    return jnp.where(lane == N - 1, 0.0, pltpu.roll(v, N - 1, 1))


def blocks_swapped(tiles):
    tiles = list(tiles)
    group = lax.broadcasted_iota(jnp.int32, tiles[0].shape, 1) // 16
    for bit in (4, 2, 1):
        upper = (group & bit) != 0
        for i in range(8):
            if i & bit:
                continue
            a, b = tiles[i], tiles[i + bit]
            tiles[i] = jnp.where(upper, pltpu.roll(b, 16 * bit, 1), a)
            tiles[i + bit] = jnp.where(upper, b, pltpu.roll(a, 128 - 16 * bit, 1))
    return tiles


def wide(ref, *where):
    *lead, rows = where
    return jnp.concatenate([ref[(*lead, b, rows, slice(None))] for b in range(4)], axis=1)


def put(ref, value, *where):
    *lead, rows = where
    for b in range(4):
        ref[(*lead, b, rows, slice(None))] = value[:, b * 128 : (b + 1) * 128]


def regroup(received, left, coil):
    for octet in range(SPACE // 8):
        tiles = [
            received[octet * 8 + i, :, :, coil * 128 : (coil + 1) * 128].reshape(32, 128)
            for i in range(8)
        ]
        for s, tile in enumerate(blocks_swapped(tiles)):
            row = coil * 128 + s * 16
            for h in range(2):
                left[h, row : row + 16, octet * 128 : (octet + 1) * 128] = tile[
                    h * 16 : (h + 1) * 16
                ]


def grouped(group, one):
    def step(i, carry):
        for k in range(PAIRS // LOOPS // group):
            one([i * (PAIRS // LOOPS) + k * group + n for n in range(group)])
        return carry

    lax.fori_loop(0, LOOPS, step, 0)


def side_by_side(blocks):
    blocks = [jnp.concatenate([before(v), v, after(v)], axis=0).astype(BF) for v in blocks]
    return jnp.concatenate(blocks, axis=1)


def apart(spread, n):
    third = spread.shape[0] // 3
    left, middle, right = (
        spread[q * third : (q + 1) * third, n * N : (n + 1) * N] for q in range(3)
    )
    return before(left) + middle + after(right)


def early_kernel(measured, keep, w1, w2, table, tail, total):
    def own_rows(i):
        c, s = i // SLICES, i % SLICES
        mask = keep[s] > 0
        return [jnp.where(mask, measured[c, h, s].astype(F32), 0.0) for h in range(2)]

    def one(pairs):
        owns = [own_rows(i) for i in pairs]
        blocks = [jnp.concatenate(own, axis=0) for own in owns]
        hidden = jnp.maximum(dot(w1[...], side_by_side(blocks)).astype(BF), 0)
        spread = dot(w2[...], hidden)
        for n, i in enumerate(pairs):
            total[i] = blocks[n] + apart(spread, n)
            tail[i] = jnp.concatenate(
                [own[ROWS - 2 :] for own in owns[n]] + [jnp.zeros((4, N), F32)], axis=0
            )

    grouped(EARLY_GROUP, one)


def late_kernel(tail, total, halo, follow, w1, w2, table, out, refined):
    cos, sin = table.at[0], table.at[1]

    def one(pairs):
        rims = [
            jnp.where(follow[i % SLICES] > 0, halo[i].astype(F32)[0:8], 0.0) for i in pairs
        ]
        patches = side_by_side(
            [jnp.concatenate([tail[i], rim], axis=0) for i, rim in zip(pairs, rims)]
        )
        hidden = jnp.maximum(dot(w1[...], patches).astype(BF), 0)
        spread = dot(w2[...], hidden)
        line = iota((8, N), 0)
        for n, i in enumerate(pairs):
            more = apart(spread, n)
            row = i * 16 if isinstance(i, int) else pl.multiple_of(i * 16, 16)
            for h in range(2):
                extra = more[h * 8 : (h + 1) * 8]
                rows = rims[n] if h == 0 else pltpu.roll(rims[n], 4, 0)
                done = total[i, h * 16 : (h + 1) * 16]
                done = jnp.concatenate(
                    [
                        jnp.where(line < 2, rows + extra, done[0:8]),
                        jnp.where(line >= 6, done[8:16] + extra, done[8:16]),
                    ],
                    axis=0,
                )
                refined[h, pl.ds(row, 16), :] = done.astype(BF)

    grouped(LATE_GROUP, one)
    for part in range(2):
        rows = pl.ds(part * 256, 256)
        co, si = cos[rows, :], sin[rows, :]
        real = dot_nt(co, refined[0]) - dot_nt(si, refined[1])
        imag = dot_nt(si, refined[0]) + dot_nt(co, refined[1])
        out[part * 16 : (part + 1) * 16, 0] = real.astype(BF).reshape(16, 16, LANES)
        out[part * 16 : (part + 1) * 16, 1] = imag.astype(BF).reshape(16, 16, LANES)


def combine_kernel(received, sens, halo, table, out, left, image, partial):
    cos, sin = table.at[0], table.at[1]
    for c in range(COILS):
        regroup(received, left, c)
        rows = slice(c * 128, (c + 1) * 128)
        image[c, 0] = dot(left[0, rows], cos[...]) - dot(left[1, rows], sin[...])
        image[c, 1] = dot(left[0, rows], sin[...]) + dot(left[1, rows], cos[...])
        for s in range(SLICES):
            rows = slice(s * 16, (s + 1) * 16)
            real, imag = image[c, 0, rows], image[c, 1, rows]
            extra = halo[c * SLICES + s].astype(F32)
            sr, si = (
                jnp.concatenate(
                    [extra[8 + 2 * h : 10 + 2 * h], sens[c, h, s].astype(F32)[2:]], axis=0
                )
                for h in range(2)
            )
            pr = sr * real + si * imag
            pi = sr * imag - si * real
            if c:
                pr = pr + wide(partial, 0, rows)
                pi = pi + wide(partial, 1, rows)
            put(partial, pr, 0, rows)
            put(partial, pi, 1, rows)
    turn = RING - lax.axis_index("space") % RING
    for x in range(ROWS):
        place = (x + 2) % ROWS
        both = jnp.concatenate(
            [wide(partial, h, pl.ds(place, 8, stride=16)) for h in range(2)], axis=0
        )
        out[(x // 4 + turn) % RING, x % 4 * 16 : (x % 4 + 1) * 16] = both.astype(BF)


def outer():
    space = lax.axis_index("space")
    quarter = (space + lax.axis_index("ring")) % RING
    first = jnp.where((space == 0) & (quarter == 0), 0.0, 1.0)
    last = jnp.where((space == SPACE - 1) & (quarter == RING - 1), 0.0, 1.0)
    return first, last


def image_weights(first, second, band1, band2, w1, w2):
    edge = outer()
    matrix = rows_of(first, 3, 3, 3)
    for x in range(6):
        block = dot_tn(matrix, band1[x])
        if x == 0:
            block = block * edge[0]
        if x == 5:
            block = block * edge[1]
        w1[x * CH : (x + 1) * CH, :] = block.astype(BF)
    matrix = doubled(rows_of(second, 3, 3, 3))
    for pair in range(3):
        w2[:, pair * 128 : (pair + 1) * 128] = dot(band2[pair], matrix).astype(BF)


def image_patches(x3, above, below):
    x3[0:48] = jnp.zeros((48, N), BF)
    x3[432:480] = jnp.zeros((48, N), BF)
    for s in range(SLICES):
        first, second = above(s), below(s)
        for q in range(3):
            base = (s + 1) * 48 + q * 16
            x3[base : base + 16] = jnp.concatenate([first[q], second[q]], axis=0).astype(BF)


def taps(v):
    return before(v), v, after(v)


def image_sums(x3, w1, w2, acc):
    for start in range(0, SLICES, IMAGE_GROUP):
        group = range(start, start + IMAGE_GROUP)
        patches = jnp.concatenate([x3[t * 48 : t * 48 + 144] for t in group], axis=1)
        hidden = jnp.maximum(dot(w1, patches).astype(BF), 0)
        spread = dot(w2, hidden)
        for t in group:
            columns = slice((t - start) * N, (t - start + 1) * N)
            for a in range(3):
                s = t + 1 - a
                if 0 <= s < SLICES:
                    rows = slice(s * 24, (s + 1) * 24)
                    acc[rows] = acc[rows] + spread[a * 24 : (a + 1) * 24, columns]


def image_early(own, w1, w2, acc, half, rows8, x3):
    put(rows8, own[0:32].astype(F32), slice(64, 96))
    put(rows8, own[32:64].astype(F32) * outer()[1], slice(96, 128))

    def below(s):
        shifted = taps(wide(rows8, pl.ds(64 + s, 8, stride=8)))
        half[s] = jnp.concatenate(shifted, axis=0)
        return shifted

    image_patches(x3, lambda s: [jnp.zeros((8, N), F32)] * 3, below)
    acc[...] = jnp.zeros_like(acc)
    image_sums(x3, w1[4 * CH :], w2[:, 4 * CH :], acc)


def image_late(previous, own, w1, w2, early, half, out, rows8, x3, acc, fin):
    edge = outer()
    put(rows8, previous[0:32].astype(F32) * edge[0], slice(0, 32))
    put(rows8, previous[32:64].astype(F32), slice(32, 64))
    put(rows8, own[0:32].astype(F32), slice(64, 96))
    put(rows8, own[32:64].astype(F32) * edge[1], slice(96, 128))
    image_patches(
        x3,
        lambda s: taps(wide(rows8, pl.ds(s, 8, stride=8))),
        lambda s: [half[s, q * 8 : (q + 1) * 8] for q in range(3)],
    )
    acc[...] = early[...]
    image_sums(x3, w1[: 4 * CH], w2[:, : 4 * CH], acc)
    for s in range(SLICES):
        v = acc[s * 24 : (s + 1) * 24]
        put(fin, before(v[0:8]) + v[8:16] + after(v[16:24]), slice(s * 8, (s + 1) * 8))
    for e in range(4):
        update = jnp.concatenate([wide(fin, pl.ds(o * 4 + e, 8, stride=8)) for o in range(2)], axis=0)
        value = (wide(rows8, slice(32 + e * 16, 48 + e * 16)) + update).astype(BF)
        for y in range(RING):
            out[y, e * 16 : (e + 1) * 16] = value


def expand_kernel(gathered, sens, table, out, image_out, image, data):
    cos, sin = table.at[0], table.at[1]
    turn = RING - lax.axis_index("space") % RING
    for x in range(ROWS):
        both = gathered[(x // 4 + turn) % RING, x % 4 * 16 : (x % 4 + 1) * 16].astype(F32)
        for h in range(2):
            put(image, both[h * 8 : (h + 1) * 8], h, pl.ds(x, 8, stride=16))
    for s in range(SLICES):
        rows = slice(s * 16, (s + 1) * 16)
        real, imag = wide(image, 0, rows), wide(image, 1, rows)
        image_out[0, s] = real.astype(BF)
        image_out[1, s] = imag.astype(BF)
        for c in range(COILS):
            sr, si = sens[c, 0, s].astype(F32), sens[c, 1, s].astype(F32)
            rows = slice(c * 128 + s * 16, c * 128 + (s + 1) * 16)
            data[0, rows] = (sr * real - si * imag).astype(BF)
            data[1, rows] = (sr * imag + si * real).astype(BF)
    for part in range(2):
        rows = pl.ds(part * 256, 256)
        co, si = cos[rows, :], sin[rows, :]
        real = dot_nt(co, data[0]) + dot_nt(si, data[1])
        imag = dot_nt(co, data[1]) - dot_nt(si, data[0])
        out[part * 16 : (part + 1) * 16, 0] = real.astype(BF).reshape(16, 16, LANES)
        out[part * 16 : (part + 1) * 16, 1] = imag.astype(BF).reshape(16, 16, LANES)


def finish_kernel(received, measured, keep, table, image, out, image_out, left, done, sems):
    cos, sin = table.at[0], table.at[1]
    copies = [pltpu.make_async_copy(image, image_out, sems.at[COILS])]
    copies[0].start()
    for c in range(COILS):
        regroup(received, left, c)
        rows = slice(c * 128, (c + 1) * 128)
        real = dot(left[0, rows], cos[...]) + dot(left[1, rows], sin[...])
        imag = dot(left[1, rows], cos[...]) - dot(left[0, rows], sin[...])
        for s in range(SLICES):
            mask = keep[s] > 0
            rows = slice(s * 16, (s + 1) * 16)
            for h, value in enumerate((real, imag)):
                done[c, h, s] = jnp.where(
                    mask, measured[c, h, s].astype(F32), value[rows]
                ).astype(BF)
        copies.append(pltpu.make_async_copy(done.at[c], out.at[c], sems.at[c]))
        copies[-1].start()
    for copy in copies:
        copy.wait()


def call(kernel, shapes, scratch, *operands, mib=12, flags=None):
    single = not isinstance(shapes, list)
    return pl.pallas_call(
        kernel,
        out_shape=shapes,
        in_specs=[VMEM] * len(operands),
        out_specs=VMEM if single else [VMEM] * len(shapes),
        scratch_shapes=scratch,
        compiler_params=pltpu.CompilerParams(vmem_limit_bytes=mib * MIB, flags=flags),
    )(*operands)


def spread(array, axis):
    return lax.all_to_all(array, axis, split_axis=0, concat_axis=0, tiled=True)


def arr(*shape, dtype=BF):
    return jax.ShapeDtypeStruct(shape, dtype)


def local(
    measured, sensitivity, sample_lines, kspace_first, kspace_second, image_first, image_second
):
    plain, late = (jnp.asarray(t) for t in dft_tables())
    iband1, iband2 = (jnp.asarray(t) for t in image_bands())

    eight = pltpu.VMEM((COILS, 2, SLICES, 8, N), BF)
    small = pltpu.VMEM((3, 3, 2, CH), BF)
    rim, near, kw1, kw1b, kw2, kw2b, keep, follow = pl.pallas_call(
        start_kernel,
        out_shape=[
            arr(PAIRS, 12, N),
            arr(COILS, 2, SLICES, ROWS, N),
            arr(EARLY * CH, 96),
            arr((HROWS - EARLY) * CH, 48),
            arr(96, EARLY * CH),
            arr(48, (HROWS - EARLY) * CH),
            arr(SLICES, ROWS, 1, dtype=F32),
            arr(SLICES, 8, 1, dtype=F32),
        ],
        in_specs=[HBM] * 5,
        out_specs=[VMEM] * 8,
        scratch_shapes=[
            eight, pltpu.VMEM((SLICES, 128), jnp.int32), small, small,
            pltpu.SemaphoreType.DMA((5,)),
        ],
        compiler_params=pltpu.CompilerParams(vmem_limit_bytes=12 * MIB),
    )(
        *(
            pltpu.with_memory_space_constraint(v, pltpu.HBM)
            for v in (
                measured,
                sensitivity,
                sample_lines,
                kspace_first.transpose(2, 3, 1, 0),
                kspace_second.transpose(2, 3, 0, 1),
            )
        )
    )
    halo = lax.ppermute(rim, "space", [((i + 1) % SPACE, i) for i in range(SPACE)])
    tail, total = call(
        early_kernel,
        [arr(PAIRS, 8, N, dtype=F32), arr(PAIRS, 32, N, dtype=F32)],
        [],
        near, keep, kw1, kw2, late,
        mib=28,
    )
    half_done = call(
        late_kernel,
        arr(SPACE, 2, ROWS, LANES),
        [pltpu.VMEM((2, LANES, N), BF)],
        tail, total, halo, follow, kw1b, kw2b, late,
        mib=20,
    )
    half_done = spread(half_done, "space")
    partial = call(
        combine_kernel,
        arr(RING, 64, N),
        [
            pltpu.VMEM((2, LANES, N), BF),
            pltpu.VMEM((COILS, 2, 128, N), F32),
            pltpu.VMEM((2, 4, 128, 128), F32),
        ],
        half_done, sensitivity, halo, late,
    )
    part = spread(partial, "ring").astype(F32).sum(axis=0).astype(BF)

    def place(half, i):
        block, quarter = i // RING % SPACE, i % RING
        return (half * RING + (quarter - block) % RING) * SPACE + block

    axes = ("half", "ring", "space")
    count = RING * SPACE
    exchange = [(place(half, i), place(1 - half, i)) for half in range(HALVES) for i in range(count)]
    forward = [
        (place(half ^ (i % (8 * RING) == 8 * RING - 1), i), place(half, i + 1))
        for half in range(HALVES)
        for i in range(count)
    ]
    other = lax.ppermute(part, axes, exchange)
    image_in = (part.astype(F32) + other.astype(F32)).astype(BF)
    previous = lax.ppermute(image_in, axes, forward)
    iw1, iw2 = call(
        image_weights,
        [arr(6 * CH, 144), arr(72, 6 * CH)],
        [],
        image_first.transpose(2, 3, 4, 1, 0), image_second.transpose(2, 3, 4, 0, 1), iband1, iband2,
    )
    rooms = [pltpu.VMEM((4, 128, 128), F32), pltpu.VMEM((480, N), BF)]
    early, half = call(
        image_early,
        [arr(SLICES * 24, N, dtype=F32), arr(SLICES, 24, N, dtype=F32)],
        rooms,
        image_in, iw1, iw2,
    )
    copies = call(
        image_late,
        arr(RING, 64, N),
        rooms
        + [pltpu.VMEM((SLICES * 24, N), F32), pltpu.VMEM((4, SLICES * 8, 128), F32)],
        previous, image_in, iw1, iw2, early, half,
    )
    gathered = spread(copies, "ring")
    midway, image_out = call(
        expand_kernel,
        [arr(SPACE, 2, ROWS, LANES), arr(2, SLICES, ROWS, N)],
        [pltpu.VMEM((2, 4, 128, 128), F32), pltpu.VMEM((2, LANES, N), BF)],
        gathered, sensitivity, plain,
    )
    midway = spread(midway, "space")
    whole = arr(COILS, 2, SLICES, ROWS, N)
    kspace_out, image_out = pl.pallas_call(
        finish_kernel,
        out_shape=[whole, arr(2, SLICES, ROWS, N)],
        in_specs=[VMEM] * 5,
        out_specs=[HBM] * 2,
        scratch_shapes=[
            pltpu.VMEM((2, LANES, N), BF),
            pltpu.VMEM(whole.shape, BF),
            pltpu.SemaphoreType.DMA((COILS + 1,)),
        ],
        compiler_params=pltpu.CompilerParams(vmem_limit_bytes=12 * MIB),
    )(midway, measured, keep, plain, image_out)
    return kspace_out, image_out


def solution(mesh):
    mesh = Mesh(mesh.devices.reshape(HALVES, RING, SPACE), ("half", "ring", "space"))
    placed = P(("half", "ring"), None, None, "space", None)
    return jax.shard_map(
        local,
        mesh=mesh,
        in_specs=(placed, placed, P(), P(), P(), P(), P()),
        out_specs=(placed, P(None, None, "space", None)),
        check_vma=False,
    )
```

```python
import math

import jax
import jax.numpy as jnp
import numpy as np
from jax import lax
from jax.experimental import pallas as pl
from jax.experimental.pallas import tpu as pltpu
from jax.sharding import Mesh
from jax.sharding import PartitionSpec as P

N = 512
COILS = 2
SLICES = 8
ROWS = 16
CH = 64
SPACE = 32
RING = 4
HALVES = 2
PAIRS = COILS * SLICES
LANES = PAIRS * ROWS
MIB = 1024 * 1024
HROWS = ROWS + 2
EARLY = 14
EARLY_GROUP = 1
LATE_GROUP = 4
IMAGE_GROUP = 2
LOOPS = 2
BF = jnp.bfloat16
F32 = jnp.float32
VMEM = pl.BlockSpec(memory_space=pltpu.VMEM)
HBM = pl.BlockSpec(memory_space=pltpu.HBM)
NT = (((1,), (1,)), ((), ()))
TN = (((0,), (0,)), ((), ()))


def dft_tables():
    position = np.arange(N)
    angles = (position[:, None] * position[None, :] % N).astype(np.float32) * np.float32(
        2.0 * math.pi / N
    )
    factor = np.float32(1.0 / math.sqrt(N))
    cos, sin = (np.cos(angles) * factor).astype(BF), (np.sin(angles) * factor).astype(BF)
    late = (position + np.where(position % ROWS < 2, ROWS, 0)) % N
    plain = np.stack([cos, sin])
    return plain, plain[:, late]


def iota(shape, dim):
    return lax.broadcasted_iota(jnp.int32, shape, dim)


def split(v, size, count):
    quotient = sum((v >= size * n).astype(jnp.int32) for n in range(1, count))
    return quotient, v - quotient * size


def rows_of(ref, *dims):
    return jnp.concatenate([ref[where].astype(F32) for where in np.ndindex(*dims)], axis=0).astype(BF)


def doubled(block):
    zero = jnp.zeros_like(block)
    return jnp.concatenate(
        [jnp.concatenate([block, zero], axis=1), jnp.concatenate([zero, block], axis=1)], axis=0
    )


def start_kernel(
    far_measured, far_sens, far_lines, far_first, far_second,
    rim, measured, w1, w1b, w2, w2b, keep, follow, sens, lines, first, second, sems,
):
    rows = pl.ds(0, 8)
    copies = [
        pltpu.make_async_copy(source, target, sems.at[n])
        for n, (source, target) in enumerate(
            (
                (far_lines, lines),
                (far_first, first),
                (far_second, second),
                (far_measured, measured),
                (far_sens.at[:, :, :, rows, :], sens),
            )
        )
    ]
    for copy in copies:
        copy.start()
    for copy in copies[:3]:
        copy.wait()
    space = lax.axis_index("space")
    row = space * ROWS + iota((24, 128), 0)
    row = jnp.where(iota((24, 128), 0) >= ROWS + 4, row - 4, row)
    row = jnp.where(row >= N, row - N, row)
    for s in range(SLICES):
        hit = jnp.where(lines[s : s + 1, :] == row, 1.0, 0.0)
        hit = jnp.max(hit, axis=1, keepdims=True)
        keep[s] = hit[:ROWS]
        follow[s] = hit[ROWS:]
    whole = jnp.where(space == SPACE - 1, 0.0, 1.0)
    rest = iota((18, 128), 0)
    h_row = rest & 1
    p_row, q_row = split(rest >> 1, 3, 3)
    matrix = rows_of(first, 3, 3)
    lane = iota((18, 128), 1)
    band = first_band(h_row, p_row, q_row, lane >> 5, (lane >> 4) & 1, lane & 15)
    for r in range(EARLY):
        block = dot_tn(matrix, jnp.where(band == r, 1.0, 0.0).astype(BF))
        w1[r * CH : (r + 1) * CH, :] = block[:, :96].astype(BF)
    t = lane & 15
    h_lane = jnp.where(t < 8, t >> 1, (t - 8) >> 2)
    row = jnp.where(t < 8, ROWS - 2 + (t & 1), ROWS + (t & 3))
    band = first_band(h_row, p_row, q_row, lane >> 4, h_lane, row)
    following = (iota((CH, 128), 1) & 15) >= 8
    for r in range(EARLY, HROWS):
        block = dot_tn(matrix, jnp.where(band == r, 1.0, 0.0).astype(BF))
        across = ~following if r + 1 >= ROWS else following
        block = jnp.where(across, block * whole, block)
        start = (r - EARLY) * CH
        w1b[start : start + CH, :] = block[:, :48].astype(BF)
    matrix = doubled(rows_of(second, 3, 3))
    place = iota((96, 36), 0) & 15
    place = jnp.where(place < 2, place + ROWS, place)
    band = second_band(place, 5)
    for pair in range(EARLY // 2):
        block = dot(jnp.where(band == 2 * pair, 1.0, 0.0).astype(BF), matrix)
        w2[:, pair * 128 : (pair + 1) * 128] = block.astype(BF)
    place = iota((48, 36), 0) & 7
    place = jnp.where(place < 2, place + ROWS, jnp.where(place >= 6, place + 8, -64))
    band = second_band(place, 4)
    late = (iota((48, 128), 0) & 7) < 2
    upper = iota((48, 128), 1) >= CH
    for pair in range(EARLY // 2, HROWS // 2):
        block = dot(jnp.where(band == 2 * pair, 1.0, 0.0).astype(BF), matrix)
        beyond = 2 * pair + 1 + upper.astype(jnp.int32) >= ROWS
        block = jnp.where(late != beyond, block * whole, block)
        start = pair * 128 - EARLY * CH
        w2b[:, start : start + 128] = block.astype(BF)
    for copy in copies[3:]:
        copy.wait()
    for i in range(PAIRS):
        c, s = i // SLICES, i % SLICES
        rim[i] = jnp.concatenate(
            [measured[c, h, s].astype(F32)[:4] for h in range(2)]
            + [sens[c, h, s].astype(F32)[:2] for h in range(2)],
            axis=0,
        ).astype(BF)


def first_band(h_row, p_row, q_row, q_lane, h_lane, row):
    return jnp.where((h_row == h_lane) & (q_row == q_lane), row - p_row, -1)


def second_band(place, shift):
    line, lane = iota(place.shape, 0), iota(place.shape, 1)
    parity, rest = split(lane, 18, 2)
    o_lane = rest & 1
    p_lane, q_lane = split(rest >> 1, 3, 3)
    match = (line >> shift == q_lane) & ((line >> (shift - 1)) & 1 == o_lane)
    return jnp.where(match, place + p_lane - 2 - parity, -1)


def image_bands():
    first = np.zeros((6, 54, 144), np.float32)
    for x in range(6):
        for h in range(2):
            for a in range(3):
                for p in range(3):
                    for q in range(3):
                        first[x, a * 18 + p * 6 + q * 2 + h, a * 48 + q * 16 + (x + p) * 2 + h] = 1
    second = np.zeros((3, 72, 108), np.float32)
    for pair in range(3):
        for parity in range(2):
            for o in range(2):
                for a in range(3):
                    for q in range(3):
                        for e in range(4):
                            p = 2 * pair + parity - e
                            if 0 <= p < 3:
                                second[
                                    pair,
                                    a * 24 + q * 8 + o * 4 + e,
                                    parity * 54 + a * 18 + p * 6 + q * 2 + o,
                                ] = 1
    return first.astype(BF), second.astype(BF)


def dot(a, b):
    return jnp.dot(a, b, preferred_element_type=F32)


def dot_tn(a, b):
    return lax.dot_general(a, b, TN, preferred_element_type=F32)


def dot_nt(a, b):
    return lax.dot_general(a, b, NT, preferred_element_type=F32)


def before(v):
    lane = lax.broadcasted_iota(jnp.int32, v.shape, 1)
    return jnp.where(lane == 0, 0.0, pltpu.roll(v, 1, 1))


def after(v):
    lane = lax.broadcasted_iota(jnp.int32, v.shape, 1)
    return jnp.where(lane == N - 1, 0.0, pltpu.roll(v, N - 1, 1))


def blocks_swapped(tiles):
    tiles = list(tiles)
    group = lax.broadcasted_iota(jnp.int32, tiles[0].shape, 1) // 16
    for bit in (4, 2, 1):
        upper = (group & bit) != 0
        for i in range(8):
            if i & bit:
                continue
            a, b = tiles[i], tiles[i + bit]
            tiles[i] = jnp.where(upper, pltpu.roll(b, 16 * bit, 1), a)
            tiles[i + bit] = jnp.where(upper, b, pltpu.roll(a, 128 - 16 * bit, 1))
    return tiles


def wide(ref, *where):
    *lead, rows = where
    return jnp.concatenate([ref[(*lead, b, rows, slice(None))] for b in range(4)], axis=1)


def put(ref, value, *where):
    *lead, rows = where
    for b in range(4):
        ref[(*lead, b, rows, slice(None))] = value[:, b * 128 : (b + 1) * 128]


def regroup(received, left, coil):
    for octet in range(SPACE // 8):
        tiles = [
            received[octet * 8 + i, :, :, coil * 128 : (coil + 1) * 128].reshape(32, 128)
            for i in range(8)
        ]
        for s, tile in enumerate(blocks_swapped(tiles)):
            row = coil * 128 + s * 16
            for h in range(2):
                left[h, row : row + 16, octet * 128 : (octet + 1) * 128] = tile[
                    h * 16 : (h + 1) * 16
                ]


def grouped(group, one):
    def step(i, carry):
        for k in range(PAIRS // LOOPS // group):
            one([i * (PAIRS // LOOPS) + k * group + n for n in range(group)])
        return carry

    lax.fori_loop(0, LOOPS, step, 0)


def side_by_side(blocks):
    blocks = [jnp.concatenate([before(v), v, after(v)], axis=0).astype(BF) for v in blocks]
    return jnp.concatenate(blocks, axis=1)


def apart(spread, n):
    third = spread.shape[0] // 3
    left, middle, right = (
        spread[q * third : (q + 1) * third, n * N : (n + 1) * N] for q in range(3)
    )
    return before(left) + middle + after(right)


def early_kernel(measured, keep, w1, w2, table, tail, total):
    def own_rows(i):
        c, s = i // SLICES, i % SLICES
        mask = keep[s] > 0
        return [jnp.where(mask, measured[c, h, s].astype(F32), 0.0) for h in range(2)]

    def one(pairs):
        owns = [own_rows(i) for i in pairs]
        blocks = [jnp.concatenate(own, axis=0) for own in owns]
        hidden = jnp.maximum(dot(w1[...], side_by_side(blocks)).astype(BF), 0)
        spread = dot(w2[...], hidden)
        for n, i in enumerate(pairs):
            total[i] = blocks[n] + apart(spread, n)
            tail[i] = jnp.concatenate(
                [own[ROWS - 2 :] for own in owns[n]] + [jnp.zeros((4, N), F32)], axis=0
            )

    grouped(EARLY_GROUP, one)


def late_kernel(tail, total, halo, follow, w1, w2, table, out, refined):
    cos, sin = table.at[0], table.at[1]

    def one(pairs):
        rims = [
            jnp.where(follow[i % SLICES] > 0, halo[i].astype(F32)[0:8], 0.0) for i in pairs
        ]
        patches = side_by_side(
            [jnp.concatenate([tail[i], rim], axis=0) for i, rim in zip(pairs, rims)]
        )
        hidden = jnp.maximum(dot(w1[...], patches).astype(BF), 0)
        spread = dot(w2[...], hidden)
        line = iota((8, N), 0)
        for n, i in enumerate(pairs):
            more = apart(spread, n)
            row = i * 16 if isinstance(i, int) else pl.multiple_of(i * 16, 16)
            for h in range(2):
                extra = more[h * 8 : (h + 1) * 8]
                rows = rims[n] if h == 0 else pltpu.roll(rims[n], 4, 0)
                done = total[i, h * 16 : (h + 1) * 16]
                done = jnp.concatenate(
                    [
                        jnp.where(line < 2, rows + extra, done[0:8]),
                        jnp.where(line >= 6, done[8:16] + extra, done[8:16]),
                    ],
                    axis=0,
                )
                refined[h, pl.ds(row, 16), :] = done.astype(BF)

    grouped(LATE_GROUP, one)
    for part in range(2):
        rows = pl.ds(part * 256, 256)
        co, si = cos[rows, :], sin[rows, :]
        real = dot_nt(co, refined[0]) - dot_nt(si, refined[1])
        imag = dot_nt(si, refined[0]) + dot_nt(co, refined[1])
        out[part * 16 : (part + 1) * 16, 0] = real.astype(BF).reshape(16, 16, LANES)
        out[part * 16 : (part + 1) * 16, 1] = imag.astype(BF).reshape(16, 16, LANES)


def combine_kernel(received, sens, halo, table, out, left, image, partial):
    cos, sin = table.at[0], table.at[1]
    for c in range(COILS):
        regroup(received, left, c)
        rows = slice(c * 128, (c + 1) * 128)
        image[c, 0] = dot(left[0, rows], cos[...]) - dot(left[1, rows], sin[...])
        image[c, 1] = dot(left[0, rows], sin[...]) + dot(left[1, rows], cos[...])
        for s in range(SLICES):
            rows = slice(s * 16, (s + 1) * 16)
            real, imag = image[c, 0, rows], image[c, 1, rows]
            extra = halo[c * SLICES + s].astype(F32)
            sr, si = (
                jnp.concatenate(
                    [extra[8 + 2 * h : 10 + 2 * h], sens[c, h, s].astype(F32)[2:]], axis=0
                )
                for h in range(2)
            )
            pr = sr * real + si * imag
            pi = sr * imag - si * real
            if c:
                pr = pr + wide(partial, 0, rows)
                pi = pi + wide(partial, 1, rows)
            put(partial, pr, 0, rows)
            put(partial, pi, 1, rows)
    turn = RING - lax.axis_index("space") % RING
    for x in range(ROWS):
        place = (x + 2) % ROWS
        both = jnp.concatenate(
            [wide(partial, h, pl.ds(place, 8, stride=16)) for h in range(2)], axis=0
        )
        out[(x // 4 + turn) % RING, x % 4 * 16 : (x % 4 + 1) * 16] = both.astype(BF)


def outer():
    space = lax.axis_index("space")
    quarter = (space + lax.axis_index("ring")) % RING
    first = jnp.where((space == 0) & (quarter == 0), 0.0, 1.0)
    last = jnp.where((space == SPACE - 1) & (quarter == RING - 1), 0.0, 1.0)
    return first, last


def image_weights(first, second, band1, band2, w1, w2):
    edge = outer()
    matrix = rows_of(first, 3, 3, 3)
    for x in range(6):
        block = dot_tn(matrix, band1[x])
        if x == 0:
            block = block * edge[0]
        if x == 5:
            block = block * edge[1]
        w1[x * CH : (x + 1) * CH, :] = block.astype(BF)
    matrix = doubled(rows_of(second, 3, 3, 3))
    for pair in range(3):
        w2[:, pair * 128 : (pair + 1) * 128] = dot(band2[pair], matrix).astype(BF)


def image_patches(x3, above, below):
    x3[0:48] = jnp.zeros((48, N), BF)
    x3[432:480] = jnp.zeros((48, N), BF)
    for s in range(SLICES):
        first, second = above(s), below(s)
        for q in range(3):
            base = (s + 1) * 48 + q * 16
            x3[base : base + 16] = jnp.concatenate([first[q], second[q]], axis=0).astype(BF)


def taps(v):
    return before(v), v, after(v)


def image_sums(x3, w1, w2, acc):
    for start in range(0, SLICES, IMAGE_GROUP):
        group = range(start, start + IMAGE_GROUP)
        patches = jnp.concatenate([x3[t * 48 : t * 48 + 144] for t in group], axis=1)
        hidden = jnp.maximum(dot(w1, patches).astype(BF), 0)
        spread = dot(w2, hidden)
        for t in group:
            columns = slice((t - start) * N, (t - start + 1) * N)
            for a in range(3):
                s = t + 1 - a
                if 0 <= s < SLICES:
                    rows = slice(s * 24, (s + 1) * 24)
                    acc[rows] = acc[rows] + spread[a * 24 : (a + 1) * 24, columns]


def image_early(own, w1, w2, acc, half, rows8, x3):
    put(rows8, own[0:32].astype(F32), slice(64, 96))
    put(rows8, own[32:64].astype(F32) * outer()[1], slice(96, 128))

    def below(s):
        shifted = taps(wide(rows8, pl.ds(64 + s, 8, stride=8)))
        half[s] = jnp.concatenate(shifted, axis=0)
        return shifted

    image_patches(x3, lambda s: [jnp.zeros((8, N), F32)] * 3, below)
    acc[...] = jnp.zeros_like(acc)
    image_sums(x3, w1[4 * CH :], w2[:, 4 * CH :], acc)


def image_late(previous, own, w1, w2, early, half, out, rows8, x3, acc, fin):
    edge = outer()
    put(rows8, previous[0:32].astype(F32) * edge[0], slice(0, 32))
    put(rows8, previous[32:64].astype(F32), slice(32, 64))
    put(rows8, own[0:32].astype(F32), slice(64, 96))
    put(rows8, own[32:64].astype(F32) * edge[1], slice(96, 128))
    image_patches(
        x3,
        lambda s: taps(wide(rows8, pl.ds(s, 8, stride=8))),
        lambda s: [half[s, q * 8 : (q + 1) * 8] for q in range(3)],
    )
    acc[...] = early[...]
    image_sums(x3, w1[: 4 * CH], w2[:, : 4 * CH], acc)
    for s in range(SLICES):
        v = acc[s * 24 : (s + 1) * 24]
        put(fin, before(v[0:8]) + v[8:16] + after(v[16:24]), slice(s * 8, (s + 1) * 8))
    for e in range(4):
        update = jnp.concatenate([wide(fin, pl.ds(o * 4 + e, 8, stride=8)) for o in range(2)], axis=0)
        value = (wide(rows8, slice(32 + e * 16, 48 + e * 16)) + update).astype(BF)
        for y in range(RING):
            out[y, e * 16 : (e + 1) * 16] = value


def expand_kernel(gathered, sens, table, out, image_out, image, data):
    cos, sin = table.at[0], table.at[1]
    turn = RING - lax.axis_index("space") % RING
    for x in range(ROWS):
        both = gathered[(x // 4 + turn) % RING, x % 4 * 16 : (x % 4 + 1) * 16].astype(F32)
        for h in range(2):
            put(image, both[h * 8 : (h + 1) * 8], h, pl.ds(x, 8, stride=16))
    for s in range(SLICES):
        rows = slice(s * 16, (s + 1) * 16)
        real, imag = wide(image, 0, rows), wide(image, 1, rows)
        image_out[0, s] = real.astype(BF)
        image_out[1, s] = imag.astype(BF)
        for c in range(COILS):
            sr, si = sens[c, 0, s].astype(F32), sens[c, 1, s].astype(F32)
            rows = slice(c * 128 + s * 16, c * 128 + (s + 1) * 16)
            data[0, rows] = (sr * real - si * imag).astype(BF)
            data[1, rows] = (sr * imag + si * real).astype(BF)
    for part in range(2):
        rows = pl.ds(part * 256, 256)
        co, si = cos[rows, :], sin[rows, :]
        real = dot_nt(co, data[0]) + dot_nt(si, data[1])
        imag = dot_nt(co, data[1]) - dot_nt(si, data[0])
        out[part * 16 : (part + 1) * 16, 0] = real.astype(BF).reshape(16, 16, LANES)
        out[part * 16 : (part + 1) * 16, 1] = imag.astype(BF).reshape(16, 16, LANES)


def finish_kernel(received, measured, keep, table, image, out, image_out, left, done, sems):
    cos, sin = table.at[0], table.at[1]
    copies = [pltpu.make_async_copy(image, image_out, sems.at[2 * COILS])]
    copies[0].start()
    for c in range(COILS):
        regroup(received, left, c)
        rows = slice(c * 128, (c + 1) * 128)
        real = dot(left[0, rows], cos[...]) + dot(left[1, rows], sin[...])
        imag = dot(left[1, rows], cos[...]) - dot(left[0, rows], sin[...])
        for s in range(SLICES):
            mask = keep[s] > 0
            rows = slice(s * 16, (s + 1) * 16)
            for h, value in enumerate((real, imag)):
                done[c, h, s] = jnp.where(
                    mask, measured[c, h, s].astype(F32), value[rows]
                ).astype(BF)
            if s % 4 == 3:
                four = pl.ds(s - 3, 4)
                copies.append(
                    pltpu.make_async_copy(
                        done.at[c, :, four], out.at[c, :, four], sems.at[2 * c + s // 4]
                    )
                )
                copies[-1].start()
    for copy in copies:
        copy.wait()


def call(kernel, shapes, scratch, *operands, mib=12, flags=None):
    single = not isinstance(shapes, list)
    return pl.pallas_call(
        kernel,
        out_shape=shapes,
        in_specs=[VMEM] * len(operands),
        out_specs=VMEM if single else [VMEM] * len(shapes),
        scratch_shapes=scratch,
        compiler_params=pltpu.CompilerParams(vmem_limit_bytes=mib * MIB, flags=flags),
    )(*operands)


def spread(array, axis):
    return lax.all_to_all(array, axis, split_axis=0, concat_axis=0, tiled=True)


def arr(*shape, dtype=BF):
    return jax.ShapeDtypeStruct(shape, dtype)


def local(
    measured, sensitivity, sample_lines, kspace_first, kspace_second, image_first, image_second
):
    plain, late = (jnp.asarray(t) for t in dft_tables())
    iband1, iband2 = (jnp.asarray(t) for t in image_bands())

    eight = pltpu.VMEM((COILS, 2, SLICES, 8, N), BF)
    small = pltpu.VMEM((3, 3, 2, CH), BF)
    rim, near, kw1, kw1b, kw2, kw2b, keep, follow = pl.pallas_call(
        start_kernel,
        out_shape=[
            arr(PAIRS, 12, N),
            arr(COILS, 2, SLICES, ROWS, N),
            arr(EARLY * CH, 96),
            arr((HROWS - EARLY) * CH, 48),
            arr(96, EARLY * CH),
            arr(48, (HROWS - EARLY) * CH),
            arr(SLICES, ROWS, 1, dtype=F32),
            arr(SLICES, 8, 1, dtype=F32),
        ],
        in_specs=[HBM] * 5,
        out_specs=[VMEM] * 8,
        scratch_shapes=[
            eight, pltpu.VMEM((SLICES, 128), jnp.int32), small, small,
            pltpu.SemaphoreType.DMA((5,)),
        ],
        compiler_params=pltpu.CompilerParams(vmem_limit_bytes=12 * MIB),
    )(
        *(
            pltpu.with_memory_space_constraint(v, pltpu.HBM)
            for v in (
                measured,
                sensitivity,
                sample_lines,
                kspace_first.transpose(2, 3, 1, 0),
                kspace_second.transpose(2, 3, 0, 1),
            )
        )
    )
    halo = lax.ppermute(rim, "space", [((i + 1) % SPACE, i) for i in range(SPACE)])
    tail, total = call(
        early_kernel,
        [arr(PAIRS, 8, N, dtype=F32), arr(PAIRS, 32, N, dtype=F32)],
        [],
        near, keep, kw1, kw2, late,
        mib=28,
    )
    half_done = call(
        late_kernel,
        arr(SPACE, 2, ROWS, LANES),
        [pltpu.VMEM((2, LANES, N), BF)],
        tail, total, halo, follow, kw1b, kw2b, late,
        mib=20,
    )
    half_done = spread(half_done, "space")
    partial = call(
        combine_kernel,
        arr(RING, 64, N),
        [
            pltpu.VMEM((2, LANES, N), BF),
            pltpu.VMEM((COILS, 2, 128, N), F32),
            pltpu.VMEM((2, 4, 128, 128), F32),
        ],
        half_done, sensitivity, halo, late,
    )
    part = spread(partial, "ring").astype(F32).sum(axis=0).astype(BF)

    def place(half, i):
        block, quarter = i // RING % SPACE, i % RING
        return (half * RING + (quarter - block) % RING) * SPACE + block

    axes = ("half", "ring", "space")
    count = RING * SPACE
    exchange = [(place(half, i), place(1 - half, i)) for half in range(HALVES) for i in range(count)]
    forward = [
        (place(half ^ (i % (8 * RING) == 8 * RING - 1), i), place(half, i + 1))
        for half in range(HALVES)
        for i in range(count)
    ]
    other = lax.ppermute(part, axes, exchange)
    image_in = (part.astype(F32) + other.astype(F32)).astype(BF)
    previous = lax.ppermute(image_in, axes, forward)
    iw1, iw2 = call(
        image_weights,
        [arr(6 * CH, 144), arr(72, 6 * CH)],
        [],
        image_first.transpose(2, 3, 4, 1, 0), image_second.transpose(2, 3, 4, 0, 1), iband1, iband2,
    )
    rooms = [pltpu.VMEM((4, 128, 128), F32), pltpu.VMEM((480, N), BF)]
    early, half = call(
        image_early,
        [arr(SLICES * 24, N, dtype=F32), arr(SLICES, 24, N, dtype=F32)],
        rooms,
        image_in, iw1, iw2,
    )
    copies = call(
        image_late,
        arr(RING, 64, N),
        rooms
        + [pltpu.VMEM((SLICES * 24, N), F32), pltpu.VMEM((4, SLICES * 8, 128), F32)],
        previous, image_in, iw1, iw2, early, half,
    )
    gathered = spread(copies, "ring")
    midway, image_out = call(
        expand_kernel,
        [arr(SPACE, 2, ROWS, LANES), arr(2, SLICES, ROWS, N)],
        [pltpu.VMEM((2, 4, 128, 128), F32), pltpu.VMEM((2, LANES, N), BF)],
        gathered, sensitivity, plain,
    )
    midway = spread(midway, "space")
    whole = arr(COILS, 2, SLICES, ROWS, N)
    kspace_out, image_out = pl.pallas_call(
        finish_kernel,
        out_shape=[whole, arr(2, SLICES, ROWS, N)],
        in_specs=[VMEM] * 5,
        out_specs=[HBM] * 2,
        scratch_shapes=[
            pltpu.VMEM((2, LANES, N), BF),
            pltpu.VMEM(whole.shape, BF),
            pltpu.SemaphoreType.DMA((2 * COILS + 1,)),
        ],
        compiler_params=pltpu.CompilerParams(vmem_limit_bytes=12 * MIB),
    )(midway, measured, keep, plain, image_out)
    return kspace_out, image_out


def solution(mesh):
    mesh = Mesh(mesh.devices.reshape(HALVES, RING, SPACE), ("half", "ring", "space"))
    placed = P(("half", "ring"), None, None, "space", None)
    return jax.shard_map(
        local,
        mesh=mesh,
        in_specs=(placed, placed, P(), P(), P(), P(), P()),
        out_specs=(placed, P(None, None, "space", None)),
        check_vma=False,
    )
```
